32 devices in a mesh: dp: 16 (over z, x, core), tensor: 2 (over y).
Axes of the slice: x: 2, y: 2, z: 4, core: 2. Of those that a mesh axis runs over, the one named last changes fastest.
Arguments:
- layer_input: bfloat16 [32768, 768], P(('dp', 'tensor')), may hold values from -6 to 6
- teacher: bfloat16 [32768, 768], P(('dp', 'tensor')), may hold values from -6 to 6
- lengths: int32 [16], P('dp'), may hold values from 512 to 2048, as said below
- qkv_weight: bfloat16 [3, 768, 768], P(None, ('tensor', 'dp')), may hold values from -0.21875 to 0.21875
- out_weight: bfloat16 [768, 768], P(('tensor', 'dp')), may hold values from -6 to 6
- ln1_gain: bfloat16 [768], P('dp'), may hold values from 0.099609375 to 1.8984375
- ln1_bias: bfloat16 [768], P('dp'), may hold values from -3 to 3
- in_weight: bfloat16 [3072, 768], P(('tensor', 'dp')), may hold values from -0.21875 to 0.21875
- down_weight: bfloat16 [3072, 768], P(('tensor', 'dp')), may hold values from -0.109375 to 0.109375
- ln2_gain: bfloat16 [768], P('dp'), may hold values from 0.099609375 to 1.8984375
- ln2_bias: bfloat16 [768], P('dp'), may hold values from -3 to 3
Outputs:
- output: bfloat16 [32768, 768], P(('dp', 'tensor'))
- loss: float32 [], replicated
- input_grad: float32 [32768, 768], P(('dp', 'tensor'))
- grad_qkv: float32 [3, 768, 768], P(None, ('tensor', 'dp'))
- grad_out: float32 [768, 768], P(('tensor', 'dp'))
- grad_ln1_gain: float32 [768], P('dp')
- grad_ln1_bias: float32 [768], P('dp')
- grad_in: float32 [3072, 768], P(('tensor', 'dp'))
- grad_down: float32 [3072, 768], P(('tensor', 'dp'))
- grad_ln2_gain: float32 [768], P('dp')
- grad_ln2_bias: float32 [768], P('dp')
The draws below stay inside these ranges and needn't reach their ends.
Inputs may be any that keep to these rules, and one draw needn't show every extreme that they name: lengths[s] valid tokens fill the start of slot s of 2048 positions; the rest of the slot is padding.
All inputs are finite; a program needn't handle non-finite values.
Results may differ from the reference program's by a relative error of at most 0.014.
Values may be sent and summed in bfloat16 or wider, within the bound.
A program may use at most 512 MiB of HBM per device.

```python
import jax
import jax.numpy as jnp
from jax import lax

D = 768
HEADS = 12
FF = 3072
HD = 64
SLOT = 2048
SLOTS = 16
TOKENS = 32768
GRAD_SCALE = 6291456


def draw_lengths(key, part):
    spread_key = jax.random.fold_in(key, 101)
    short_key = jax.random.fold_in(key, 202)
    long_key = jax.random.fold_in(key, 303)
    slot_index = jnp.arange(SLOTS)
    floor_len = SLOT // 4 + SLOT // 2 * slot_index // SLOTS
    spread = jax.random.randint(spread_key, (SLOTS,), 0, SLOT // 2 + 1)
    drawn = jnp.minimum(floor_len + spread, SLOT)
    half_slots = max(SLOTS // 2, 1)
    short_pick = jax.random.randint(short_key, (), 0, half_slots)
    long_pick = jax.random.randint(long_key, (), half_slots, SLOTS)
    drawn = jnp.where(slot_index == short_pick, SLOT // 4, drawn)
    drawn = jnp.where(slot_index == long_pick, SLOT, drawn)
    return drawn.astype(jnp.int32)


def level_of(stream_key, shape, split, smallest, largest):
    gain, own = 1.0, jax.random.fold_in(stream_key, 6)
    for axis_at, blocks in split:
        draws = jnp.exp(jax.random.uniform(jax.random.fold_in(own, axis_at), (blocks,), jnp.float32, smallest / len(split), largest / len(split)))
        gain = gain * jnp.repeat(draws, shape[axis_at] // blocks).reshape([-1 if axis == axis_at else 1 for axis in range(len(shape))])
    return gain


def normal_values(own_key, dims, scale, bound, split=(), kind=jnp.bfloat16):
    values = jax.random.normal(own_key, dims, jnp.float32) * scale
    if len(split) > 0:
        values = level_of(own_key, dims, split, -0.22, 0.18) * values
    return jnp.clip(values, min=-bound, max=bound).astype(kind)


def setup_inputs(seed: int = 0) -> dict:
    seeds = jax.random.split(jax.random.key(seed), 12)
    return {
        "layer_input": normal_values(seeds[0], (TOKENS, D), 1.0, 6.0, ((0, 32),)),
        "teacher": normal_values(seeds[1], (TOKENS, D), 1.0, 6.0, ((0, 32),)),
        "lengths": draw_lengths(jax.random.fold_in(seeds[11], 71), 0),
        "qkv_weight": normal_values(seeds[3], (3, D, D), D ** -0.5, 0.21875, ((1, 32),)),
        "out_weight": normal_values(seeds[4], (D, D), (max(4 * D // SLOT, 1)) ** -0.5, 6.0, ((0, 32),)),
        "ln1_gain": jnp.clip(1.0 + 0.18 * jax.random.normal(seeds[5], (D,), jnp.float32), 0.099609375, 1.8984375).astype(jnp.bfloat16),
        "ln1_bias": normal_values(seeds[6], (D,), 0.5, 3.0, ((0, 16),)),
        "in_weight": normal_values(seeds[7], (FF, D), D ** -0.5, 0.21875, ((0, 32),)),
        "down_weight": normal_values(seeds[8], (FF, D), FF ** -0.5, 0.109375, ((0, 32),)),
        "ln2_gain": jnp.clip(1.0 + 0.18 * jax.random.normal(seeds[9], (D,), jnp.float32), 0.099609375, 1.8984375).astype(jnp.bfloat16),
        "ln2_bias": normal_values(seeds[10], (D,), 0.5, 3.0, ((0, 16),)),
    }


EPSILON = 1e-05
NEG_LARGE = -1e+30
ROPE_BASE = 10000.0
INV_ROOT2 = 0.7071067811865476
HIGHEST_PRECISION = lax.Precision.HIGHEST

@jax.custom_vjp
def low(v):
    return lax.optimization_barrier(v.astype(jnp.bfloat16)).astype(jnp.float32)

@jax.custom_vjp
def low_back(v):
    return v

def low_keep(v):
    return (low(v), None)

def low_pass(kept, grad):
    return (grad,)

def back_keep(v):
    return (v, None)

def back_low(kept, grad):
    return (low(grad),)
low.defvjp(low_keep, low_pass)
low_back.defvjp(back_keep, back_low)

def angle_tables():
    places = jnp.arange(SLOT).astype(jnp.float32)
    ladder = jnp.arange(HD // 2).astype(jnp.float32)
    inverse_freq = ROPE_BASE ** (-2.0 * ladder / HD)
    angles = places[:, None] * inverse_freq[None, :]
    return (jnp.cos(angles), jnp.sin(angles))

def rotate(values, cosine, sine_table):
    halves = values.reshape(values.shape[:-1] + (HD // 2, 2))
    even_part = halves[..., 0]
    odd_part = halves[..., 1]
    cosine_wide = cosine[:, None, :]
    sine_wide = sine_table[:, None, :]
    turned = jnp.stack([even_part * cosine_wide - odd_part * sine_wide, odd_part * cosine_wide + even_part * sine_wide], -1)
    return turned.reshape(values.shape)

def layer_norm(values, gain_vec, offset):
    centre = values - lax.optimization_barrier(jnp.mean(values, axis=-1, keepdims=True))
    inverse = lax.rsqrt(lax.optimization_barrier(jnp.mean(centre * centre, axis=-1, keepdims=True)) + EPSILON)
    normed = centre * inverse
    return normed * gain_vec + offset

def gelu_exact(values):
    return 0.5 * values * (1.0 + jax.scipy.special.erf(values * INV_ROOT2))

def attend_slot(packed):
    queries, key_rows, values, length = packed
    scores = jnp.einsum('qhd,khd->hqk', queries, key_rows, precision=HIGHEST_PRECISION) * 0.125
    scores = low_back(scores)
    key_valid = jnp.arange(SLOT) < length
    scores = jnp.where(key_valid[None, None, :], scores, NEG_LARGE)
    peak_score = lax.optimization_barrier(jnp.max(scores, axis=-1, keepdims=True))
    exp_scores = jnp.exp(scores - peak_score)
    soft_weights = low(exp_scores / lax.optimization_barrier(jnp.sum(exp_scores, axis=-1, keepdims=True)))
    mixed = jnp.einsum('hqk,khd->qhd', soft_weights, values, precision=HIGHEST_PRECISION)
    return mixed.reshape(SLOT, D)

def reference(layer_input, teacher, lengths, qkv_weight, out_weight, ln1_gain, ln1_bias, in_weight, down_weight, ln2_gain, ln2_bias):
    floats = tuple((member.astype(jnp.float32) for member in (layer_input, qkv_weight, out_weight, ln1_gain, ln1_bias, in_weight, down_weight, ln2_gain, ln2_bias)))
    target = teacher.astype(jnp.float32)
    valid_count = jnp.sum(lengths).astype(jnp.float32)
    row_valid = (jnp.arange(SLOT)[None, :] < lengths[:, None]).reshape(TOKENS)
    cosine, sine_table = angle_tables()

    def forward(inputs_f, qkv_f, out_f, gain_one, bias_one, in_f, down_f, gain_two, bias_two):
        projected = low_back(jnp.einsum('tc,jhc->jth', inputs_f, qkv_f, precision=HIGHEST_PRECISION))
        shaped = projected.reshape(3, SLOTS, SLOT, HEADS, HD)
        queries = low(rotate(shaped[0], cosine, sine_table))
        key_rows = low(rotate(shaped[1], cosine, sine_table))
        values = low(shaped[2])
        context = lax.map(jax.checkpoint(attend_slot), (queries, key_rows, values, lengths)).reshape(TOKENS, D)
        context = low(low_back(context))
        attended = low_back(jnp.dot(context, out_f, precision=HIGHEST_PRECISION))
        hidden = layer_norm(inputs_f + attended, gain_one, bias_one)
        pre_act = low_back(jnp.dot(low(hidden), in_f.T, precision=HIGHEST_PRECISION))
        branch = low_back(jnp.dot(low(gelu_exact(pre_act)), down_f, precision=HIGHEST_PRECISION))
        return layer_norm(hidden + branch, gain_two, bias_two)

    def objective(inputs_f, qkv_f, out_f, gain_one, bias_one, in_f, down_f, gain_two, bias_two):
        final = forward(inputs_f, qkv_f, out_f, gain_one, bias_one, in_f, down_f, gain_two, bias_two)
        misfit = jnp.where(row_valid[:, None], final - target, 0.0)
        loss_value = jnp.sum(misfit * misfit) / (valid_count * D)
        return (loss_value * GRAD_SCALE, (final, loss_value))
    scaled, pullback, aux_pair = jax.vjp(objective, *floats, has_aux=True)
    final, loss_value = aux_pair
    grads = pullback(jnp.ones_like(scaled))
    return (final.astype(jnp.bfloat16), loss_value, grads[0], grads[1], grads[2], grads[3], grads[4], grads[5], grads[6], grads[7], grads[8])
```

```python
import functools

import jax
import jax.numpy as jnp
from jax import lax
from jax.experimental import pallas as pl
from jax.experimental.pallas import tpu as pltpu
from jax.sharding import PartitionSpec as P

D = 768
HD = 64
SLOT = 2048
PAIR = 2 * HD
EPSILON = 1e-05
NEG_LARGE = -1e30
ROPE_BASE = 10000.0
INV_ROOT2 = 0.7071067811865476
INV_ROOT_TWO_PI = 0.3989422804014327
LOG2E = 1.4426950408889634
LN2 = 0.6931471805599453
EVERYONE = ("tensor", "dp")

BF = jnp.bfloat16
F32 = jnp.float32
NT = (((1,), (1,)), ((), ()))
NN = (((1,), (0,)), ((), ()))
VMEM_LIMIT = 56 << 20


def dot(a, b, dims):
    return lax.dot_general(a, b, dims, preferred_element_type=F32)


def lanes(rows):
    return lax.broadcasted_iota(jnp.int32, (rows, PAIR), 1)


def in_head(rows, head):
    lane = lanes(rows)
    return lane < HD if head == 0 else lane >= HD


def pick(mask, values):
    return jnp.where(mask, values, jnp.zeros_like(values))


def swap_pairs(values):
    even = lanes(values.shape[0]) % 2 == 0
    return jnp.where(even, pltpu.roll(values, PAIR - 1, 1), pltpu.roll(values, 1, 1))


def turn(values, cosine, signed_sine):
    return values * cosine + swap_pairs(values) * signed_sine


def turn_back(values, cosine, signed_sine):
    return values * cosine - swap_pairs(values) * signed_sine


def angle_tables(places):
    lane = jnp.arange(PAIR)
    inverse_freq = ROPE_BASE ** (-2.0 * ((lane % HD) // 2).astype(F32) / HD)
    angles = places.astype(F32)[:, None] * inverse_freq[None, :]
    sine = jnp.sin(angles)
    return jnp.cos(angles), jnp.where(lane % 2 == 0, -sine, sine)


def project_kernel(with_q, x_ref, w_ref, cos_ref, sin_ref, *outs):
    x = x_ref[...]
    cosine, sine = cos_ref[...], sin_ref[...]
    first = 0 if with_q else 1
    for j in range(first, 3):
        out = outs[j - first]
        full = dot(x, w_ref[j], NT)
        for pair in range(D // PAIR):
            cols = slice(pair * PAIR, (pair + 1) * PAIR)
            part = full[:, cols]
            if j < 2:
                part = turn(part, cosine, sine)
            if j == 0:
                part = part * (0.125 * LOG2E)
            out[:, cols] = part.astype(BF)


def project(x, weights, cosine, sine, with_q):
    rows = x.shape[0]
    block = 256
    count = 3 if with_q else 2
    spec = pl.BlockSpec((block, D), lambda i: (i, 0))
    table = pl.BlockSpec((block, PAIR), lambda i: (i, 0))
    return pl.pallas_call(
        functools.partial(project_kernel, with_q),
        grid=(rows // block,),
        in_specs=[spec, pl.BlockSpec((3, D, D), lambda i: (0, 0, 0)), table, table],
        out_specs=[spec] * count,
        out_shape=[jax.ShapeDtypeStruct((rows, D), BF)] * count,
        compiler_params=pltpu.CompilerParams(vmem_limit_bytes=VMEM_LIMIT),
        cost_estimate=pl.CostEstimate(
            flops=2 * rows * D * D * count, bytes_accessed=8 * rows * D + 6 * D * D, transcendentals=0
        ),
        name="project",
    )(x, weights, cosine, sine)


def attend_kernel(q_ref, k_ref, v_ref, bias_ref, o_ref, lse_ref):
    keys = k_ref.shape[0]
    rows = q_ref.shape[0]
    q, k = q_ref[...], k_ref[...]
    bias = bias_ref[...]
    v_cols = jnp.transpose(v_ref[...].astype(F32)).astype(BF)
    outs = []
    for head in range(2):
        s = dot(k, pick(in_head(rows, head), q), NT) + bias
        peak = jnp.max(s, axis=0, keepdims=True)
        p = jnp.exp2(s - peak).astype(BF)
        v_aug = jnp.concatenate([v_cols[head * HD : (head + 1) * HD], jnp.ones((16, keys), BF)], axis=0)
        mixed = dot(v_aug, p, NN)
        total = mixed[HD : HD + 1]
        outs.append(mixed[:HD] / total)
        lse_ref[0, head : head + 1, :] = peak + jnp.log2(total)
    o_ref[...] = jnp.transpose(jnp.concatenate(outs, axis=0)).astype(BF)


def attend(q, k, v, bias):
    rows, keys = q.shape[0], k.shape[0]
    block = min(512, rows)
    pairs = q.shape[1] // PAIR
    q_spec = pl.BlockSpec((block, PAIR), lambda p, i: (i, p))
    k_spec = pl.BlockSpec((keys, PAIR), lambda p, i: (0, p))
    return pl.pallas_call(
        attend_kernel,
        grid=(pairs, rows // block),
        in_specs=[q_spec, k_spec, k_spec, pl.BlockSpec((keys, 1), lambda p, i: (0, 0))],
        out_specs=[q_spec, pl.BlockSpec((1, 8, block), lambda p, i: (p, 0, i))],
        out_shape=[
            jax.ShapeDtypeStruct(q.shape, BF),
            jax.ShapeDtypeStruct((pairs, 8, rows), F32),
        ],
        compiler_params=pltpu.CompilerParams(vmem_limit_bytes=VMEM_LIMIT),
        cost_estimate=pl.CostEstimate(
            flops=16 * rows * keys * D, bytes_accessed=4 * (rows + keys) * D, transcendentals=rows * keys * 12
        ),
        name="attend",
    )(q, k, v, bias)


def attend_back_kernel(
    q_ref, k_ref, v_ref, do_ref, o_ref, lse_ref, bias_ref, cosq_ref, sinq_ref, cosk_ref, sink_ref,
    dq_ref, dk_ref, dv_ref, dq_cols, delta,
):
    step = pl.program_id(1)
    rows, keys = q_ref.shape[0], k_ref.shape[0]
    part = min(256, rows)
    k, v, bias = k_ref[...], v_ref[...], bias_ref[...]
    k_cols = jnp.transpose(k.astype(F32)).astype(BF)

    @pl.when(step == 0)
    def _():
        dq_cols[...] = jnp.zeros_like(dq_cols)
        both = jnp.transpose(do_ref[...].astype(F32) * o_ref[...].astype(F32))
        delta[0:1, :] = jnp.sum(both[:HD], axis=0, keepdims=True)
        delta[1:2, :] = jnp.sum(both[HD:], axis=0, keepdims=True)

    dk = jnp.zeros((keys, PAIR), F32)
    dv = jnp.zeros((keys, PAIR), F32)
    for first in range(0, rows, part):
        here = slice(first, first + part)
        q, do = q_ref[here, :], do_ref[here, :]
        for head in range(2):
            mine = in_head(part, head)
            q_head, do_head = pick(mine, q), pick(mine, do)
            s = dot(k, q_head, NT)
            p = jnp.exp2(s - lse_ref[0, head : head + 1, here] + bias)
            dp = dot(v, do_head, NT)
            ds = (p * (dp - delta[head : head + 1, here])).astype(BF)
            dv += dot(p.astype(BF), do_head, NN)
            dk += dot(ds, q_head, NN)
            span = slice(head * HD, (head + 1) * HD)
            dq_cols[span, here] += dot(k_cols[span], ds, NN)
    dk_ref[...] = turn_back(dk * LN2, cosk_ref[...], sink_ref[...]).astype(BF)
    dv_ref[...] = dv.astype(BF)

    @pl.when(step == pl.num_programs(1) - 1)
    def _():
        dq = jnp.transpose(dq_cols[...]) * 0.125
        dq_ref[...] = turn_back(dq, cosq_ref[...], sinq_ref[...]).astype(BF)


def attend_back(q, k, v, do, o, lse, bias, cosine, sine):
    rows, keys = q.shape[0], k.shape[0]
    block = min(512, keys)
    pairs = q.shape[1] // PAIR
    q_spec = pl.BlockSpec((rows, PAIR), lambda p, i: (0, p))
    k_spec = pl.BlockSpec((block, PAIR), lambda p, i: (i, p))
    q_table = pl.BlockSpec((rows, PAIR), lambda p, i: (0, 0))
    k_table = pl.BlockSpec((block, PAIR), lambda p, i: (i, 0))
    return pl.pallas_call(
        attend_back_kernel,
        grid=(pairs, keys // block),
        in_specs=[
            q_spec, k_spec, k_spec, q_spec, q_spec,
            pl.BlockSpec((1, 8, rows), lambda p, i: (p, 0, 0)),
            pl.BlockSpec((block, 1), lambda p, i: (i, 0)),
            q_table, q_table, k_table, k_table,
        ],
        out_specs=[q_spec, k_spec, k_spec],
        out_shape=[
            jax.ShapeDtypeStruct(q.shape, BF),
            jax.ShapeDtypeStruct(k.shape, BF),
            jax.ShapeDtypeStruct(k.shape, BF),
        ],
        scratch_shapes=[pltpu.VMEM((PAIR, rows), F32), pltpu.VMEM((8, rows), F32)],
        compiler_params=pltpu.CompilerParams(vmem_limit_bytes=VMEM_LIMIT),
        cost_estimate=pl.CostEstimate(
            flops=40 * rows * keys * D, bytes_accessed=8 * (rows + keys) * D, transcendentals=rows * keys * 12
        ),
        name="attend_back",
    )(q, k, v, do, o, lse, bias, cosine, sine, cosine, sine)


def layer_norm(values, gain_vec, offset):
    centre = values - jnp.mean(values, axis=-1, keepdims=True)
    inverse = lax.rsqrt(jnp.mean(centre * centre, axis=-1, keepdims=True) + EPSILON)
    normed = centre * inverse
    return (normed * gain_vec + offset, normed, inverse)


def norm_back(grad_result, normed, inverse, gain_vec):
    scaled = grad_result * gain_vec
    grad_values = inverse * (
        scaled
        - jnp.mean(scaled, axis=-1, keepdims=True)
        - normed * jnp.mean(scaled * normed, axis=-1, keepdims=True)
    )
    return (grad_values, jnp.sum(grad_result * normed, axis=0), jnp.sum(grad_result, axis=0))


def gelu_exact(values):
    return 0.5 * values * (1.0 + jax.scipy.special.erf(values * INV_ROOT2))


def gelu_slope(values):
    return (
        0.5 * (1.0 + jax.scipy.special.erf(values * INV_ROOT2))
        + values * jnp.exp(-0.5 * values * values) * INV_ROOT_TWO_PI
    )


def on_device(
    layer_input, teacher, lengths, qkv_weight, out_weight, ln1_gain, ln1_bias,
    in_weight, down_weight, ln2_gain, ln2_bias,
):
    own_rows = layer_input.shape[0]
    data_size = lax.axis_size("dp")
    tensor_index = lax.axis_index("tensor")
    group_rows = own_rows * lax.axis_size("tensor")
    assert group_rows == SLOT and lax.axis_size("tensor") == 2 and lengths.shape[0] == 1

    def gather(values, axis):
        return lax.all_gather(values, EVERYONE, axis=axis, tiled=True)

    def gather_vec(values):
        return lax.all_gather(values, "dp", axis=0, tiled=True).astype(F32)

    def scatter(values, axis):
        return lax.psum_scatter(values, EVERYONE, scatter_dimension=axis, tiled=True)

    def swap(values):
        return lax.ppermute(values, "tensor", [(0, 1), (1, 0)])

    valid_count = lax.psum(jnp.sum(lengths).astype(F32), "dp")
    own_places = tensor_index * own_rows + jnp.arange(own_rows)
    other_places = (1 - tensor_index) * own_rows + jnp.arange(own_rows)
    places = jnp.concatenate([own_places, other_places])
    row_valid = own_places < lengths[0]
    bias = jnp.where(places < lengths[0], 0.0, NEG_LARGE).astype(F32)[:, None]
    cosine, sine = angle_tables(places)

    other_x = swap(layer_input)
    qkv_full = gather(qkv_weight, 1)
    out_full = gather(out_weight, 0)
    in_full = gather(in_weight, 0)
    down_full = gather(down_weight, 0)
    gain_one, bias_one = gather_vec(ln1_gain), gather_vec(ln1_bias)
    gain_two, bias_two = gather_vec(ln2_gain), gather_vec(ln2_bias)

    q, k_own, v_own = project(layer_input, qkv_full, cosine[:own_rows], sine[:own_rows], True)
    k_other, v_other = project(other_x, qkv_full, cosine[own_rows:], sine[own_rows:], False)
    k = jnp.concatenate([k_own, k_other])
    v = jnp.concatenate([v_own, v_other])
    context, lse = attend(q, k, v, bias)

    attended = jnp.dot(context, out_full, preferred_element_type=F32)
    hidden, normed_one, inverse_one = layer_norm(layer_input.astype(F32) + attended, gain_one, bias_one)
    hidden_in = hidden.astype(BF)
    pre_act = jnp.einsum("tc,fc->tf", hidden_in, in_full, preferred_element_type=F32)
    activated = gelu_exact(pre_act).astype(BF)
    branch = jnp.dot(activated, down_full, preferred_element_type=F32)
    final, normed_two, inverse_two = layer_norm(hidden + branch, gain_two, bias_two)
    misfit = jnp.where(row_valid[:, None], final - teacher.astype(F32), 0.0)
    loss_part = jnp.sum(misfit * misfit)
    grad_scale = group_rows * data_size * D // 4
    grad_final = misfit * (2.0 * grad_scale / (valid_count * D))
    grad_mid, ln2_gain_part, ln2_bias_part = norm_back(grad_final, normed_two, inverse_two, gain_two)
    g_branch = grad_mid.astype(BF)
    grad_down_w = jnp.einsum("tf,tc->fc", activated, g_branch, preferred_element_type=F32)
    grad_act = jnp.einsum("tc,fc->tf", g_branch, down_full, preferred_element_type=F32)
    grad_pre = (grad_act * gelu_slope(pre_act)).astype(BF)
    grad_in_w = jnp.einsum("tf,tc->fc", grad_pre, hidden_in, preferred_element_type=F32)
    grad_hidden = grad_mid + jnp.dot(grad_pre, in_full, preferred_element_type=F32)
    grad_res, ln1_gain_part, ln1_bias_part = norm_back(grad_hidden, normed_one, inverse_one, gain_one)
    g_att = grad_res.astype(BF)
    grad_out_w = jnp.einsum("th,tc->hc", context, g_att, preferred_element_type=F32)
    g_context = jnp.einsum("tc,hc->th", g_att, out_full, preferred_element_type=F32).astype(BF)

    grad_in, grad_down, grad_out = scatter(grad_in_w, 0), scatter(grad_down_w, 0), scatter(grad_out_w, 0)

    dq, dk, dv = attend_back(q, k, v, g_context, context, lse, bias, cosine, sine)
    pass_on = jnp.dot(dk[own_rows:], qkv_full[1], preferred_element_type=F32) + jnp.dot(
        dv[own_rows:], qkv_full[2], preferred_element_type=F32
    )
    from_other = swap(pass_on.astype(BF)).astype(F32)
    both_x = jnp.concatenate([layer_input, other_x])
    grad_q_w = jnp.einsum("th,tc->hc", dq, layer_input, preferred_element_type=F32)
    grad_k_w = jnp.einsum("th,tc->hc", dk, both_x, preferred_element_type=F32)
    grad_v_w = jnp.einsum("th,tc->hc", dv, both_x, preferred_element_type=F32)
    grad_qkv = scatter(jnp.stack([grad_q_w, grad_k_w, grad_v_w]), 1)
    input_grad = (
        grad_res
        + jnp.dot(dq, qkv_full[0], preferred_element_type=F32)
        + jnp.dot(dk[:own_rows], qkv_full[1], preferred_element_type=F32)
        + jnp.dot(dv[:own_rows], qkv_full[2], preferred_element_type=F32)
        + from_other
    )
    norm_parts = jnp.stack([ln1_gain_part, ln1_bias_part, ln2_gain_part, ln2_bias_part])
    loss_total, norm_sums = lax.psum((loss_part, norm_parts), ("dp", "tensor"))
    loss_value = loss_total / (valid_count * D)
    own_share = D // data_size
    own_norms = lax.dynamic_slice_in_dim(norm_sums, lax.axis_index("dp") * own_share, own_share, 1)
    return (
        final.astype(BF), loss_value, input_grad, grad_qkv, grad_out,
        own_norms[0], own_norms[1], grad_in, grad_down, own_norms[2], own_norms[3],
    )


def solution(mesh):
    rows = P(("dp", "tensor"), None)
    shard = P(EVERYONE, None)
    in_specs = (
        rows, rows, P("dp"), P(None, EVERYONE, None), shard, P("dp"), P("dp"), shard, shard, P("dp"), P("dp"),
    )
    out_specs = (
        rows, P(), rows, P(None, EVERYONE, None), shard, P("dp"), P("dp"), shard, shard, P("dp"), P("dp"),
    )
    return jax.shard_map(on_device, mesh=mesh, in_specs=in_specs, out_specs=out_specs, check_vma=False)
```

```python
import functools

import jax
import jax.numpy as jnp
from jax import lax
from jax.experimental import pallas as pl
from jax.experimental.pallas import tpu as pltpu
from jax.sharding import PartitionSpec as P

D = 768
HD = 64
SLOT = 2048
PAIR = 2 * HD
EPSILON = 1e-05
NEG_LARGE = -1e30
ROPE_BASE = 10000.0
INV_ROOT2 = 0.7071067811865476
INV_ROOT_TWO_PI = 0.3989422804014327
LOG2E = 1.4426950408889634
LN2 = 0.6931471805599453
EVERYONE = ("tensor", "dp")

BF = jnp.bfloat16
F32 = jnp.float32
NT = (((1,), (1,)), ((), ()))
NN = (((1,), (0,)), ((), ()))
VMEM_LIMIT = 56 << 20


def dot(a, b, dims):
    return lax.dot_general(a, b, dims, preferred_element_type=F32)


def lanes(rows):
    return lax.broadcasted_iota(jnp.int32, (rows, PAIR), 1)


def in_head(rows, head):
    lane = lanes(rows)
    return lane < HD if head == 0 else lane >= HD


def pick(mask, values):
    return jnp.where(mask, values, jnp.zeros_like(values))


def swap_pairs(values):
    even = lanes(values.shape[0]) % 2 == 0
    return jnp.where(even, pltpu.roll(values, PAIR - 1, 1), pltpu.roll(values, 1, 1))


def turn(values, cosine, signed_sine):
    return values * cosine + swap_pairs(values) * signed_sine


def turn_back(values, cosine, signed_sine):
    return values * cosine - swap_pairs(values) * signed_sine


def angle_tables(places):
    lane = jnp.arange(PAIR)
    inverse_freq = ROPE_BASE ** (-2.0 * ((lane % HD) // 2).astype(F32) / HD)
    angles = places.astype(F32)[:, None] * inverse_freq[None, :]
    sine = jnp.sin(angles)
    return jnp.cos(angles), jnp.where(lane % 2 == 0, -sine, sine)


def project_kernel(with_q, x_ref, w_ref, cos_ref, sin_ref, *outs):
    x = x_ref[...]
    cosine, sine = cos_ref[...], sin_ref[...]
    first = 0 if with_q else 1
    for j in range(first, 3):
        out = outs[j - first]
        full = dot(x, w_ref[j], NT)
        for pair in range(D // PAIR):
            cols = slice(pair * PAIR, (pair + 1) * PAIR)
            part = full[:, cols]
            if j < 2:
                part = turn(part, cosine, sine)
            if j == 0:
                part = part * (0.125 * LOG2E)
            out[:, cols] = part.astype(BF)


def project(x, weights, cosine, sine, with_q):
    rows = x.shape[0]
    block = 256
    count = 3 if with_q else 2
    spec = pl.BlockSpec((block, D), lambda i: (i, 0))
    table = pl.BlockSpec((block, PAIR), lambda i: (i, 0))
    return pl.pallas_call(
        functools.partial(project_kernel, with_q),
        grid=(rows // block,),
        in_specs=[spec, pl.BlockSpec((3, D, D), lambda i: (0, 0, 0)), table, table],
        out_specs=[spec] * count,
        out_shape=[jax.ShapeDtypeStruct((rows, D), BF)] * count,
        compiler_params=pltpu.CompilerParams(vmem_limit_bytes=VMEM_LIMIT),
        cost_estimate=pl.CostEstimate(
            flops=2 * rows * D * D * count, bytes_accessed=8 * rows * D + 6 * D * D, transcendentals=0
        ),
        name="project",
    )(x, weights, cosine, sine)


def attend_kernel(leads, *refs):
    q_ref, k_ref, v_ref, bias_ref = refs[:4]
    n = len(leads)
    o_ref, lse_ref = refs[4 + n : 6 + n]
    if n:
        gather_step(leads, refs[4 : 4 + n], refs[6 + n : 6 + 2 * n], *refs[6 + 2 * n :])
    keys = k_ref.shape[0]
    rows = q_ref.shape[0]
    q, k = q_ref[...], k_ref[...]
    bias = bias_ref[...]
    v_cols = jnp.transpose(v_ref[...].astype(F32)).astype(BF)
    outs = []
    for head in range(2):
        s = dot(k, pick(in_head(rows, head), q), NT) + bias
        peak = jnp.max(s, axis=0, keepdims=True)
        p = jnp.exp2(s - peak).astype(BF)
        v_aug = jnp.concatenate([v_cols[head * HD : (head + 1) * HD], jnp.ones((16, keys), BF)], axis=0)
        mixed = dot(v_aug, p, NN)
        total = mixed[HD : HD + 1]
        outs.append(mixed[:HD] / total)
        lse_ref[0, head : head + 1, :] = peak + jnp.log2(total)
    o_ref[...] = jnp.transpose(jnp.concatenate(outs, axis=0)).astype(BF)


def attend(q, k, v, bias, shards=(), leads=(), ident=None):
    rows, keys = q.shape[0], k.shape[0]
    block = min(512, rows)
    pairs = q.shape[1] // PAIR
    n = len(shards)
    q_spec = pl.BlockSpec((block, PAIR), lambda p, i: (i, p))
    k_spec = pl.BlockSpec((keys, PAIR), lambda p, i: (0, p))
    hbm = pl.BlockSpec(memory_space=pl.ANY)
    sems = [pltpu.SemaphoreType.DMA((n, 32))] * 2 if n else []
    params = dict(collective_id=ident, has_side_effects=True) if n else {}
    assert not n or (pairs * (rows // block) == GATHER_STEPS)
    out = pl.pallas_call(
        functools.partial(attend_kernel, leads),
        grid=(pairs, rows // block),
        in_specs=[q_spec, k_spec, k_spec, pl.BlockSpec((keys, 1), lambda p, i: (0, 0))] + [hbm] * n,
        out_specs=[q_spec, pl.BlockSpec((1, 8, block), lambda p, i: (p, 0, i))] + [hbm] * n,
        out_shape=[
            jax.ShapeDtypeStruct(q.shape, BF),
            jax.ShapeDtypeStruct((pairs, 8, rows), F32),
        ]
        + full_shapes(shards, leads),
        scratch_shapes=sems,
        compiler_params=pltpu.CompilerParams(vmem_limit_bytes=VMEM_LIMIT, **params),
        cost_estimate=pl.CostEstimate(
            flops=16 * rows * keys * D, bytes_accessed=4 * (rows + keys) * D, transcendentals=rows * keys * 12
        ),
        name="attend",
    )(q, k, v, bias, *shards)
    return out[0], out[1], flatten_full(out[2:], shards, leads)


def attend_back_kernel(
    q_ref, k_ref, v_ref, do_ref, o_ref, lse_ref, bias_ref, cosq_ref, sinq_ref, cosk_ref, sink_ref,
    dq_ref, dk_ref, dv_ref, dq_cols, delta,
):
    step = pl.program_id(1)
    rows, keys = q_ref.shape[0], k_ref.shape[0]
    part = min(256, rows)
    k, v, bias = k_ref[...], v_ref[...], bias_ref[...]
    k_cols = jnp.transpose(k.astype(F32)).astype(BF)

    @pl.when(step == 0)
    def _():
        dq_cols[...] = jnp.zeros_like(dq_cols)
        both = jnp.transpose(do_ref[...].astype(F32) * o_ref[...].astype(F32))
        delta[0:1, :] = jnp.sum(both[:HD], axis=0, keepdims=True)
        delta[1:2, :] = jnp.sum(both[HD:], axis=0, keepdims=True)

    dk = jnp.zeros((keys, PAIR), F32)
    dv = jnp.zeros((keys, PAIR), F32)
    for first in range(0, rows, part):
        here = slice(first, first + part)
        q, do = q_ref[here, :], do_ref[here, :]
        for head in range(2):
            mine = in_head(part, head)
            q_head, do_head = pick(mine, q), pick(mine, do)
            s = dot(k, q_head, NT)
            p = jnp.exp2(s - lse_ref[0, head : head + 1, here] + bias)
            dp = dot(v, do_head, NT)
            ds = (p * (dp - delta[head : head + 1, here])).astype(BF)
            dv += dot(p.astype(BF), do_head, NN)
            dk += dot(ds, q_head, NN)
            span = slice(head * HD, (head + 1) * HD)
            dq_cols[span, here] += dot(k_cols[span], ds, NN)
    dk_ref[...] = turn_back(dk * LN2, cosk_ref[...], sink_ref[...]).astype(BF)
    dv_ref[...] = dv.astype(BF)

    @pl.when(step == pl.num_programs(1) - 1)
    def _():
        dq = jnp.transpose(dq_cols[...]) * 0.125
        dq_ref[...] = turn_back(dq, cosq_ref[...], sinq_ref[...]).astype(BF)


def attend_back(q, k, v, do, o, lse, bias, cosine, sine):
    rows, keys = q.shape[0], k.shape[0]
    block = min(512, keys)
    pairs = q.shape[1] // PAIR
    q_spec = pl.BlockSpec((rows, PAIR), lambda p, i: (0, p))
    k_spec = pl.BlockSpec((block, PAIR), lambda p, i: (i, p))
    q_table = pl.BlockSpec((rows, PAIR), lambda p, i: (0, 0))
    k_table = pl.BlockSpec((block, PAIR), lambda p, i: (i, 0))
    return pl.pallas_call(
        attend_back_kernel,
        grid=(pairs, keys // block),
        in_specs=[
            q_spec, k_spec, k_spec, q_spec, q_spec,
            pl.BlockSpec((1, 8, rows), lambda p, i: (p, 0, 0)),
            pl.BlockSpec((block, 1), lambda p, i: (i, 0)),
            q_table, q_table, k_table, k_table,
        ],
        out_specs=[q_spec, k_spec, k_spec],
        out_shape=[
            jax.ShapeDtypeStruct(q.shape, BF),
            jax.ShapeDtypeStruct(k.shape, BF),
            jax.ShapeDtypeStruct(k.shape, BF),
        ],
        scratch_shapes=[pltpu.VMEM((PAIR, rows), F32), pltpu.VMEM((8, rows), F32)],
        compiler_params=pltpu.CompilerParams(vmem_limit_bytes=VMEM_LIMIT),
        cost_estimate=pl.CostEstimate(
            flops=40 * rows * keys * D, bytes_accessed=8 * (rows + keys) * D, transcendentals=rows * keys * 12
        ),
        name="attend_back",
    )(q, k, v, do, o, lse, bias, cosine, sine, cosine, sine)


MESH = pl.DeviceIdType.MESH
GRID = (2, 4, 2, 2)


def coords():
    dp = lax.axis_index("dp")
    return lax.axis_index("tensor"), dp // 4, (dp // 2) % 2, dp % 2


def device(y, z, x, c):
    return (z * 4 + x * 2 + c, y)


def greet():
    y, z, x, c = coords()
    barrier = pltpu.get_barrier_semaphore()
    peers = [device(y, (z + dz) % 4, x, c) for dz in (1, 2, 3)]
    peers += [device(1 - y, z, x, c), device(y, z, 1 - x, c), device(y, z, x, 1 - c)]
    for peer in peers:
        pl.semaphore_signal(barrier, inc=1, device_id=peer, device_id_type=MESH)
    pl.semaphore_wait(barrier, len(peers))


def gather_plan(shard, full, lead, send_sem, recv_sem):
    y, z, x, c = coords()
    at = (slice(None),) * lead

    def spot(dy, dz, dx, dc=0):
        yy = y if dy == 0 else 1 - y
        zz = (z + 4 - dz) % 4
        xx = x if dx == 0 else 1 - x
        cc = c if dc == 0 else 1 - c
        return full.at[at + (yy, zz, xx, cc)]

    def copy(slot, source, target, to):
        return pltpu.make_async_remote_copy(
            src_ref=source, dst_ref=target, send_sem=send_sem.at[slot], recv_sem=recv_sem.at[slot],
            device_id=to, device_id_type=MESH,
        )

    def own(dy, dz, dx):
        return shard if (dy, dz, dx) == (0, 0, 0) else spot(dy, dz, dx)

    def over_z(dz):
        return copy(dz - 1, shard, spot(0, 0, 0), device(y, (z + dz) % 4, x, c))

    def over_y(dz):
        return copy(3 + dz, own(0, dz, 0), spot(0, dz, 0), device(1 - y, z, x, c))

    def over_x(dy, dz):
        return copy(7 + 4 * dy + dz, own(dy, dz, 0), spot(dy, dz, 0), device(y, z, 1 - x, c))

    def over_c(dy, dz, dx):
        return copy(15 + 8 * dx + 4 * dy + dz, own(dy, dz, dx), spot(dy, dz, dx), device(y, z, x, 1 - c))

    local = pltpu.make_async_copy(shard, spot(0, 0, 0), send_sem.at[31])
    return over_z, over_y, over_x, over_c, local


def full_shapes(shards, leads):
    return [jax.ShapeDtypeStruct(s.shape[:l] + GRID + s.shape[l:], s.dtype) for s, l in zip(shards, leads)]


def flatten_full(full, shards, leads):
    return [f.reshape(s.shape[:l] + (32 * s.shape[l],) + s.shape[l + 1 :]) for f, s, l in zip(full, shards, leads)]


def gather_actions(leads, shards, fulls, send_sem, recv_sem):
    plans = [
        gather_plan(s, f, l, send_sem.at[i], recv_sem.at[i]) for i, (s, f, l) in enumerate(zip(shards, fulls, leads))
    ]

    def begin():
        greet()
        for over_z, over_y, over_x, over_c, local in plans:
            for dz in (1, 3, 2):
                over_z(dz).start()
            over_y(0).start()
            over_x(0, 0).start()
            over_c(0, 0, 0).start()
            local.start()

    def after_z(dz):
        for over_z, over_y, over_x, over_c, local in plans:
            over_z(dz).wait_recv()
            over_y(dz).start()
            over_x(0, dz).start()
            over_c(0, dz, 0).start()

    def after_y(dz):
        for over_z, over_y, over_x, over_c, local in plans:
            over_y(dz).wait_recv()
            over_x(1, dz).start()
            over_c(1, dz, 0).start()

    def after_x(dy, dz):
        for over_z, over_y, over_x, over_c, local in plans:
            over_x(dy, dz).wait_recv()
            over_c(dy, dz, 1).start()

    def finish():
        for over_z, over_y, over_x, over_c, local in plans:
            local.wait()
            for dz in (1, 2, 3):
                over_z(dz).wait_send()
            for dz in range(4):
                over_y(dz).wait_send()
                for dy in range(2):
                    over_x(dy, dz).wait_send()
                    for dx in range(2):
                        over_c(dy, dz, dx).wait()

    return begin, after_z, after_y, after_x, finish


def gather_kernel(leads, *refs):
    n = len(leads)
    begin, after_z, after_y, after_x, finish = gather_actions(leads, refs[:n], refs[n : 2 * n], *refs[2 * n :])
    begin()
    for dz in (1, 3, 2):
        after_z(dz)
    for dz in (0, 1, 3, 2):
        after_y(dz)
    for dy in (0, 1):
        for dz in (0, 1, 3, 2):
            after_x(dy, dz)
    finish()


GATHER_STEPS = 12


def gather_step(leads, shards, fulls, send_sem, recv_sem):
    step = pl.program_id(0) * pl.num_programs(1) + pl.program_id(1)
    begin, after_z, after_y, after_x, finish = gather_actions(leads, shards, fulls, send_sem, recv_sem)
    parts = [
        [begin],
        [lambda: after_z(1)],
        [lambda: after_z(3), lambda: after_y(0)],
        [lambda: after_z(2), lambda: after_y(1)],
        [lambda: after_y(3), lambda: after_x(0, 0)],
        [lambda: after_y(2), lambda: after_x(0, 1)],
        [lambda: after_x(0, 3)],
        [lambda: after_x(0, 2)],
        [lambda: after_x(1, 0)],
        [lambda: after_x(1, 1)],
        [lambda: after_x(1, 3)],
        [lambda: after_x(1, 2), finish],
    ]
    for at, part in enumerate(parts):

        @pl.when(step == at)
        def _(part=part):
            for action in part:
                action()


def gather_all(shards, leads, ident):
    n = len(shards)
    any_spec = pl.BlockSpec(memory_space=pl.ANY)
    full = pl.pallas_call(
        functools.partial(gather_kernel, leads),
        in_specs=[any_spec] * n,
        out_specs=[any_spec] * n,
        out_shape=full_shapes(shards, leads),
        scratch_shapes=[pltpu.SemaphoreType.DMA((n, 32)), pltpu.SemaphoreType.DMA((n, 32))],
        compiler_params=pltpu.CompilerParams(collective_id=ident, has_side_effects=True),
        name="gather",
    )(*shards)
    return flatten_full(full, shards, leads)


ORDER = (1, 3, 2, 0)


def scatter_kernel(leads, *refs):
    n = len(leads)
    grads, small_in = refs[:n], refs[n]
    outs, small_out = refs[n + 1 : 2 * n + 1], refs[2 * n + 1]
    bufs = refs[2 * n + 2 : 2 * n + 2 + 7 * n]
    small_bufs, send_sem, recv_sem, small_send, small_recv = refs[2 * n + 2 + 7 * n :]
    y, z, x, c = coords()
    greet()
    to_y, to_x, to_c = device(1 - y, z, x, c), device(y, z, 1 - x, c), device(y, z, x, 1 - c)

    def copy(i, slot, source, target, to):
        return pltpu.make_async_remote_copy(
            src_ref=source, dst_ref=target, send_sem=send_sem.at[i, slot], recv_sem=recv_sem.at[i, slot],
            device_id=to, device_id_type=MESH,
        )

    def zz(dz):
        return (z + dz) % 4

    def over_c(i, dz):
        at = (slice(None),) * leads[i]
        rc = bufs[7 * i]
        return copy(i, dz, grads[i].at[at + (slice(None), zz(dz), slice(None), 1 - c)], rc.at[dz], to_c)

    def over_x(i, dz):
        return copy(i, 4 + dz, bufs[7 * i + 1].at[dz], bufs[7 * i + 2].at[dz], to_x)

    def over_y(i, dz):
        return copy(i, 8 + dz, bufs[7 * i + 3].at[dz], bufs[7 * i + 4].at[dz], to_y)

    def over_z(i, dz):
        return copy(i, 12 + dz, bufs[7 * i + 5].at[dz], bufs[7 * i + 6].at[dz], device(y, zz(dz), x, c))

    for dz in ORDER:
        for i in range(n):
            over_c(i, dz).start()

    def small_copy(slot, to):
        return pltpu.make_async_remote_copy(
            src_ref=small_bufs.at[slot[0]], dst_ref=small_bufs.at[slot[1]], send_sem=small_send.at[slot[1]],
            recv_sem=small_recv.at[slot[1]], device_id=to, device_id_type=MESH,
        )

    small_bufs[0] = small_in[...]
    hop_c = small_copy((0, 1), to_c)
    hop_c.start()

    def add(a, b):
        return a.astype(F32) + b.astype(F32)

    for dz in ORDER:
        for i in range(n):
            at = (slice(None),) * leads[i]
            rc, sx, rx, sy, ry, sz, rz = bufs[7 * i : 7 * i + 7]
            over_c(i, dz).wait_recv()
            for dy in range(2):
                yy = y if dy == 0 else 1 - y
                sx[(dz,) + at + (dy,)] = add(grads[i][at + (yy, zz(dz), 1 - x, c)], rc[(dz,) + at + (yy, 1 - x)]).astype(BF)
            over_x(i, dz).start()
    hop_c.wait()
    small_bufs[2] = small_bufs[0] + small_bufs[1]
    hop_x = small_copy((2, 3), to_x)
    hop_x.start()
    for dz in ORDER:
        for i in range(n):
            at = (slice(None),) * leads[i]
            rc, sx, rx, sy, ry, sz, rz = bufs[7 * i : 7 * i + 7]
            over_x(i, dz).wait_recv()
            mine = add(grads[i][at + (1 - y, zz(dz), x, c)], rc[(dz,) + at + (1 - y, x)])
            sy[dz] = (mine + rx[(dz,) + at + (1,)].astype(F32)).astype(BF)
            over_y(i, dz).start()
    hop_x.wait()
    small_bufs[4] = small_bufs[2] + small_bufs[3]
    hop_y = small_copy((4, 5), to_y)
    hop_y.start()
    for dz in ORDER:
        for i in range(n):
            at = (slice(None),) * leads[i]
            rc, sx, rx, sy, ry, sz, rz = bufs[7 * i : 7 * i + 7]
            over_y(i, dz).wait_recv()
            mine = add(grads[i][at + (y, zz(dz), x, c)], rc[(dz,) + at + (y, x)])
            total = mine + rx[(dz,) + at + (0,)].astype(F32) + ry[dz].astype(F32)
            if dz == 0:
                outs[i][...] = total
            else:
                sz[dz] = total.astype(BF)
                over_z(i, dz).start()
    hop_y.wait()
    small_bufs[6] = small_bufs[4] + small_bufs[5]
    hops = [small_copy((6, 6 + dz), device(y, zz(dz), x, c)) for dz in (1, 2, 3)]
    for hop in hops:
        hop.start()
    for dz in (1, 3, 2):
        for i in range(n):
            over_z(i, dz).wait_recv()
            outs[i][...] += bufs[7 * i + 6][dz].astype(F32)
    for hop in hops:
        hop.wait()
    small_out[...] = (small_bufs[6] + small_bufs[8]) + (small_bufs[7] + small_bufs[9])
    for dz in ORDER:
        for i in range(n):
            over_c(i, dz).wait_send()
            over_x(i, dz).wait_send()
            over_y(i, dz).wait_send()
            if dz:
                over_z(i, dz).wait_send()


def scatter_all(grads, leads, small, ident):
    n = len(grads)
    shaped, outs, scratch = [], [], []
    for g, l in zip(grads, leads):
        head, rows, tail = g.shape[:l], g.shape[l] // 32, g.shape[l + 1 :]
        shaped.append(g.reshape(head + GRID + (rows,) + tail))
        shard = head + (rows,) + tail
        outs.append(jax.ShapeDtypeStruct(shard, F32))
        wide = pltpu.VMEM((4,) + head + (2, 2, rows) + tail, BF)
        pair = pltpu.VMEM((4,) + head + (2, rows) + tail, BF)
        one = pltpu.VMEM((4,) + shard, BF)
        scratch += [wide, pair, pair, one, one, one, one]
    vmem = pl.BlockSpec(memory_space=pltpu.VMEM)
    return pl.pallas_call(
        functools.partial(scatter_kernel, leads),
        in_specs=[vmem] * (n + 1),
        out_specs=[vmem] * (n + 1),
        out_shape=outs + [jax.ShapeDtypeStruct(small.shape, F32)],
        scratch_shapes=scratch
        + [
            pltpu.VMEM((10,) + small.shape, F32),
            pltpu.SemaphoreType.DMA((n, 16)),
            pltpu.SemaphoreType.DMA((n, 16)),
            pltpu.SemaphoreType.DMA((10,)),
            pltpu.SemaphoreType.DMA((10,)),
        ],
        compiler_params=pltpu.CompilerParams(collective_id=ident, has_side_effects=True, vmem_limit_bytes=56 << 20),
        name="scatter",
    )(*shaped, small)


def layer_norm(values, gain_vec, offset):
    centre = values - jnp.mean(values, axis=-1, keepdims=True)
    inverse = lax.rsqrt(jnp.mean(centre * centre, axis=-1, keepdims=True) + EPSILON)
    normed = centre * inverse
    return (normed * gain_vec + offset, normed, inverse)


def norm_back(grad_result, normed, inverse, gain_vec):
    scaled = grad_result * gain_vec
    grad_values = inverse * (
        scaled
        - jnp.mean(scaled, axis=-1, keepdims=True)
        - normed * jnp.mean(scaled * normed, axis=-1, keepdims=True)
    )
    return (grad_values, jnp.sum(grad_result * normed, axis=0), jnp.sum(grad_result, axis=0))


def gelu_exact(values):
    return 0.5 * values * (1.0 + jax.scipy.special.erf(values * INV_ROOT2))


def gelu_slope(values):
    return (
        0.5 * (1.0 + jax.scipy.special.erf(values * INV_ROOT2))
        + values * jnp.exp(-0.5 * values * values) * INV_ROOT_TWO_PI
    )


def on_device(
    layer_input, teacher, lengths, qkv_weight, out_weight, ln1_gain, ln1_bias,
    in_weight, down_weight, ln2_gain, ln2_bias,
):
    own_rows = layer_input.shape[0]
    data_size = lax.axis_size("dp")
    tensor_index = lax.axis_index("tensor")
    group_rows = own_rows * lax.axis_size("tensor")
    assert group_rows == SLOT and lax.axis_size("tensor") == 2 and lengths.shape[0] == 1

    def gather(values, axis):
        return lax.all_gather(values, EVERYONE, axis=axis, tiled=True)

    def gather_vec(values):
        return lax.all_gather(values, "dp", axis=0, tiled=True).astype(F32)

    def scatter(values, axis):
        return lax.psum_scatter(values, EVERYONE, scatter_dimension=axis, tiled=True)

    def swap(values):
        return lax.ppermute(values, "tensor", [(0, 1), (1, 0)])

    own_comm = (data_size, lax.axis_size("tensor")) == (16, 2)
    own_places = tensor_index * own_rows + jnp.arange(own_rows)
    other_places = (1 - tensor_index) * own_rows + jnp.arange(own_rows)
    places = jnp.concatenate([own_places, other_places])
    row_valid = own_places < lengths[0]
    bias = jnp.where(places < lengths[0], 0.0, NEG_LARGE).astype(F32)[:, None]
    cosine, sine = angle_tables(places)

    other_x = swap(layer_input)
    if own_comm:
        share = D // data_size
        small = jnp.zeros((8, 128), F32)
        for row, vec in enumerate((ln1_gain, ln1_bias, ln2_gain, ln2_bias)):
            small = small.at[row, :share].set(vec.astype(F32))
        small = small.at[4, 0].set(lengths[0].astype(F32))
        qkv_full, small_full = gather_all([qkv_weight, small], [1, 0], 0)
        small_full = small_full.reshape(2, data_size, 8, 128)[0]
        vectors = small_full[:, :4, :share].transpose(1, 0, 2).reshape(4, D)
        gain_one, bias_one, gain_two, bias_two = (vectors[i] for i in range(4))
        valid_count = jnp.sum(small_full[:, 4, 0])
    else:
        valid_count = lax.psum(jnp.sum(lengths).astype(F32), "dp")
        qkv_full = gather(qkv_weight, 1)
        gain_one, bias_one = gather_vec(ln1_gain), gather_vec(ln1_bias)
        gain_two, bias_two = gather_vec(ln2_gain), gather_vec(ln2_bias)
    down_full = gather(down_weight, 0)

    q, k_own, v_own = project(layer_input, qkv_full, cosine[:own_rows], sine[:own_rows], True)
    k_other, v_other = project(other_x, qkv_full, cosine[own_rows:], sine[own_rows:], False)
    k = jnp.concatenate([k_own, k_other])
    v = jnp.concatenate([v_own, v_other])
    if own_comm:
        context, lse, (in_full, out_full) = attend(q, k, v, bias, [in_weight, out_weight], [0, 0], 1)
    else:
        context, lse, _ = attend(q, k, v, bias)
        in_full, out_full = gather(in_weight, 0), gather(out_weight, 0)

    attended = jnp.dot(context, out_full, preferred_element_type=F32)
    hidden, normed_one, inverse_one = layer_norm(layer_input.astype(F32) + attended, gain_one, bias_one)
    hidden_in = hidden.astype(BF)
    pre_act = jnp.einsum("tc,fc->tf", hidden_in, in_full, preferred_element_type=F32)
    activated = gelu_exact(pre_act).astype(BF)
    branch = jnp.dot(activated, down_full, preferred_element_type=F32)
    final, normed_two, inverse_two = layer_norm(hidden + branch, gain_two, bias_two)
    misfit = jnp.where(row_valid[:, None], final - teacher.astype(F32), 0.0)
    loss_part = jnp.sum(misfit * misfit)
    grad_scale = group_rows * data_size * D // 4
    grad_final = misfit * (2.0 * grad_scale / (valid_count * D))
    grad_mid, ln2_gain_part, ln2_bias_part = norm_back(grad_final, normed_two, inverse_two, gain_two)
    g_branch = grad_mid.astype(BF)
    grad_down_w = jnp.einsum("tf,tc->fc", activated, g_branch, preferred_element_type=F32)
    grad_act = jnp.einsum("tc,fc->tf", g_branch, down_full, preferred_element_type=F32)
    grad_pre = (grad_act * gelu_slope(pre_act)).astype(BF)
    grad_in_w = jnp.einsum("tf,tc->fc", grad_pre, hidden_in, preferred_element_type=F32)
    grad_hidden = grad_mid + jnp.dot(grad_pre, in_full, preferred_element_type=F32)
    grad_res, ln1_gain_part, ln1_bias_part = norm_back(grad_hidden, normed_one, inverse_one, gain_one)
    g_att = grad_res.astype(BF)
    grad_out_w = jnp.einsum("th,tc->hc", context, g_att, preferred_element_type=F32)
    g_context = jnp.einsum("tc,hc->th", g_att, out_full, preferred_element_type=F32).astype(BF)

    nothing = jnp.zeros((8, 128), F32)
    if own_comm:
        grad_down = scatter(grad_down_w.astype(BF), 0).astype(F32)
        grad_in, grad_out, _ = scatter_all([grad_in_w.astype(BF), grad_out_w.astype(BF)], [0, 0], nothing, 2)
    else:
        grad_in, grad_down, grad_out = scatter(grad_in_w, 0), scatter(grad_down_w, 0), scatter(grad_out_w, 0)

    dq, dk, dv = attend_back(q, k, v, g_context, context, lse, bias, cosine, sine)
    pass_on = jnp.dot(dk[own_rows:], qkv_full[1], preferred_element_type=F32) + jnp.dot(
        dv[own_rows:], qkv_full[2], preferred_element_type=F32
    )
    from_other = swap(pass_on.astype(BF)).astype(F32)
    both_x = jnp.concatenate([layer_input, other_x])
    grad_q_w = jnp.einsum("th,tc->hc", dq, layer_input, preferred_element_type=F32)
    grad_k_w = jnp.einsum("th,tc->hc", dk, both_x, preferred_element_type=F32)
    grad_v_w = jnp.einsum("th,tc->hc", dv, both_x, preferred_element_type=F32)
    grad_qkv_w = jnp.stack([grad_q_w, grad_k_w, grad_v_w])
    input_grad = (
        grad_res
        + jnp.dot(dq, qkv_full[0], preferred_element_type=F32)
        + jnp.dot(dk[:own_rows], qkv_full[1], preferred_element_type=F32)
        + jnp.dot(dv[:own_rows], qkv_full[2], preferred_element_type=F32)
        + from_other
    )
    norm_parts = jnp.stack([ln1_gain_part, ln1_bias_part, ln2_gain_part, ln2_bias_part])
    if own_comm:
        parts = jnp.concatenate([norm_parts, jnp.full((4, D), loss_part)])
        grad_qkv, sums = scatter_all([grad_qkv_w.astype(BF)], [1], parts, 3)
        norm_sums, loss_total = sums[:4], sums[4, 0]
    else:
        grad_qkv = scatter(grad_qkv_w, 1)
        loss_total, norm_sums = lax.psum((loss_part, norm_parts), ("dp", "tensor"))
    loss_value = loss_total / (valid_count * D)
    own_share = D // data_size
    own_norms = lax.dynamic_slice_in_dim(norm_sums, lax.axis_index("dp") * own_share, own_share, 1)
    return (
        final.astype(BF), loss_value, input_grad, grad_qkv, grad_out,
        own_norms[0], own_norms[1], grad_in, grad_down, own_norms[2], own_norms[3],
    )


def solution(mesh):
    rows = P(("dp", "tensor"), None)
    shard = P(EVERYONE, None)
    in_specs = (
        rows, rows, P("dp"), P(None, EVERYONE, None), shard, P("dp"), P("dp"), shard, shard, P("dp"), P("dp"),
    )
    out_specs = (
        rows, P(), rows, P(None, EVERYONE, None), shard, P("dp"), P("dp"), shard, shard, P("dp"), P("dp"),
    )
    return jax.shard_map(on_device, mesh=mesh, in_specs=in_specs, out_specs=out_specs, check_vma=False)
```

```python
import functools

import jax
import jax.numpy as jnp
from jax import lax
from jax.experimental import pallas as pl
from jax.experimental.pallas import tpu as pltpu
from jax.sharding import PartitionSpec as P

D = 768
HD = 64
SLOT = 2048
PAIR = 2 * HD
EPSILON = 1e-05
NEG_LARGE = -1e30
ROPE_BASE = 10000.0
INV_ROOT2 = 0.7071067811865476
INV_ROOT_TWO_PI = 0.3989422804014327
LOG2E = 1.4426950408889634
LN2 = 0.6931471805599453
EVERYONE = ("tensor", "dp")

BF = jnp.bfloat16
F32 = jnp.float32
NT = (((1,), (1,)), ((), ()))
NN = (((1,), (0,)), ((), ()))
VMEM_LIMIT = 56 << 20
MESH = pl.DeviceIdType.MESH
HBM = pl.BlockSpec(memory_space=pl.ANY)
VMEM = pl.BlockSpec(memory_space=pltpu.VMEM)
SMEM = pl.BlockSpec(memory_space=pltpu.SMEM)


def dot(a, b, dims):
    return lax.dot_general(a, b, dims, preferred_element_type=F32)


GRID = (2, 4, 2, 2)
ORDER = (1, 3, 2, 0)


def coords():
    dp = lax.axis_index("dp")
    return lax.axis_index("tensor"), dp // 4, (dp // 2) % 2, dp % 2


def device(y, z, x, c):
    return (z * 4 + x * 2 + c, y)


def greet():
    y, z, x, c = coords()
    barrier = pltpu.get_barrier_semaphore()
    peers = [device(y, (z + dz) % 4, x, c) for dz in (1, 2, 3)]
    peers += [device(1 - y, z, x, c), device(y, z, 1 - x, c), device(y, z, x, 1 - c)]
    for peer in peers:
        pl.semaphore_signal(barrier, inc=1, device_id=peer, device_id_type=MESH)
    pl.semaphore_wait(barrier, len(peers))


def full_shapes(shards, leads):
    return [jax.ShapeDtypeStruct(s.shape[:l] + GRID + s.shape[l:], s.dtype) for s, l in zip(shards, leads)]


def flatten_full(full, shards, leads):
    return [f.reshape(s.shape[:l] + (32 * s.shape[l],) + s.shape[l + 1 :]) for f, s, l in zip(full, shards, leads)]


def gather_sems(count):
    return [pltpu.SemaphoreType.DMA((count, 32))] * 2


def gather_parts(leads, shards, fulls, send_sem, recv_sem, via_x):
    y, z, x, c = coords()

    def plan(i):
        at = (slice(None),) * leads[i]
        shard, full = shards[i], fulls[i]

        def spot(dy, dz, dx):
            return full.at[at + (y if dy == 0 else 1 - y, (z + 4 - dz) % 4, x if dx == 0 else 1 - x, c)]

        def copy(slot, dy, dz, dx, to):
            return pltpu.make_async_remote_copy(
                src_ref=shard if (dy, dz, dx) == (0, 0, 0) else spot(dy, dz, dx),
                dst_ref=spot(dy, dz, dx),
                send_sem=send_sem.at[i, slot],
                recv_sem=recv_sem.at[i, slot],
                device_id=to,
                device_id_type=MESH,
            )

        def over_z(dz):
            return pltpu.make_async_remote_copy(
                src_ref=shard, dst_ref=spot(0, 0, 0), send_sem=send_sem.at[i, dz - 1],
                recv_sem=recv_sem.at[i, dz - 1], device_id=device(y, (z + dz) % 4, x, c), device_id_type=MESH,
            )

        to_y, to_x, to_c = device(1 - y, z, x, c), device(y, z, 1 - x, c), device(y, z, x, 1 - c)
        over_y = lambda dz: copy(3 + dz, 0, dz, 0, to_y)
        over_x = lambda dz: copy(7 + dz, 0, dz, 0, to_x)
        diagonal = lambda dz: copy(11 + dz, 1, dz, 0, to_x) if dz in via_x else copy(11 + dz, 0, dz, 1, to_y)
        over_c = lambda dy, dz, dx: copy(15 + 8 * dx + 4 * dy + dz, dy, dz, dx, to_c)
        local = pltpu.make_async_copy(shard, spot(0, 0, 0), send_sem.at[i, 31])
        return over_z, over_y, over_x, diagonal, over_c, local

    plans = [plan(i) for i in range(len(shards))]

    def begin():
        greet()
        for over_z, over_y, over_x, diagonal, over_c, local in plans:
            for dz in (1, 3, 2):
                over_z(dz).start()
            over_y(0).start()
            over_x(0).start()
            over_c(0, 0, 0).start()
            local.start()

    def after_z(dz):
        for over_z, over_y, over_x, diagonal, over_c, local in plans:
            over_z(dz).wait_recv()
            over_y(dz).start()
            over_x(dz).start()
            over_c(0, dz, 0).start()

    def after_y(dz):
        for over_z, over_y, over_x, diagonal, over_c, local in plans:
            over_y(dz).wait_recv()
            if dz in via_x:
                diagonal(dz).start()
            over_c(1, dz, 0).start()

    def after_x(dz):
        for over_z, over_y, over_x, diagonal, over_c, local in plans:
            over_x(dz).wait_recv()
            if dz not in via_x:
                diagonal(dz).start()
            over_c(0, dz, 1).start()

    def after_diagonal(dz):
        for over_z, over_y, over_x, diagonal, over_c, local in plans:
            diagonal(dz).wait_recv()
            over_c(1, dz, 1).start()

    def finish():
        for over_z, over_y, over_x, diagonal, over_c, local in plans:
            local.wait()
            for dz in (1, 2, 3):
                over_z(dz).wait_send()
            for dz in range(4):
                over_y(dz).wait_send()
                over_x(dz).wait_send()
                diagonal(dz).wait_send()
                for dy in range(2):
                    for dx in range(2):
                        over_c(dy, dz, dx).wait()

    parts = [begin]
    parts += [functools.partial(after_z, dz) for dz in (1, 3, 2)]
    for dz in (0, 1, 3, 2):
        parts += [functools.partial(after_y, dz), functools.partial(after_x, dz)]
    parts += [functools.partial(after_diagonal, dz) for dz in (0, 1, 3, 2)]
    return parts + [finish]


def gather_kernel(leads, *refs):
    n = len(leads)
    for part in gather_parts(leads, refs[:n], refs[n : 2 * n], *refs[2 * n :], (0, 1)):
        part()


def gather_all(shards, leads, ident):
    n = len(shards)
    full = pl.pallas_call(
        functools.partial(gather_kernel, leads),
        in_specs=[HBM] * n,
        out_specs=[HBM] * n,
        out_shape=full_shapes(shards, leads),
        scratch_shapes=gather_sems(n),
        compiler_params=pltpu.CompilerParams(collective_id=ident, has_side_effects=True),
        name="gather",
    )(*shards)
    return flatten_full(full, shards, leads)


def scatter_shapes(grads, leads):
    views, outs, scratch = [], [], []
    for g, l in zip(grads, leads):
        head, rows, tail = g.shape[:l], g.shape[l] // 32, g.shape[l + 1 :]
        views.append(g.reshape(head + GRID + (rows,) + tail))
        shard = head + (rows,) + tail
        outs.append(jax.ShapeDtypeStruct(shard, F32))
        wide = pltpu.VMEM((4,) + head + (2, 2, rows) + tail, BF)
        pair = pltpu.VMEM((4,) + head + (2, rows) + tail, BF)
        one = pltpu.VMEM((4,) + shard, BF)
        scratch += [wide, pair, pair, one, one, one, one]
    count = len(grads)
    return views, outs, scratch + [pltpu.SemaphoreType.DMA((count, 16))] * 2


def scatter_parts(leads, grads, outs, bufs, send_sem, recv_sem, x_first):
    y, z, x, c = coords()
    n = len(leads)
    to_y, to_x, to_c = device(1 - y, z, x, c), device(y, z, 1 - x, c), device(y, z, x, 1 - c)

    def zz(dz):
        return (z + dz) % 4

    def lead(i):
        return (slice(None),) * leads[i]

    def copy(i, slot, source, target, to):
        return pltpu.make_async_remote_copy(
            src_ref=source, dst_ref=target, send_sem=send_sem.at[i, slot], recv_sem=recv_sem.at[i, slot],
            device_id=to, device_id_type=MESH,
        )

    def over_c(i, dz):
        return copy(i, dz, grads[i].at[lead(i) + (slice(None), zz(dz), slice(None), 1 - c)], bufs[7 * i].at[dz], to_c)

    def over_first(i, dz):
        to = to_x if dz in x_first else to_y
        return copy(i, 4 + dz, bufs[7 * i + 1].at[dz], bufs[7 * i + 2].at[dz], to)

    def over_second(i, dz):
        to = to_y if dz in x_first else to_x
        return copy(i, 8 + dz, bufs[7 * i + 3].at[dz], bufs[7 * i + 4].at[dz], to)

    def over_z(i, dz):
        return copy(i, 12 + dz, bufs[7 * i + 5].at[dz], bufs[7 * i + 6].at[dz], device(y, zz(dz), x, c))

    def chip_sum(i, dz, yy, xx):
        own = grads[i][lead(i) + (yy, zz(dz), xx, c)].astype(F32)
        return own + bufs[7 * i][(dz,) + lead(i) + (yy, xx)].astype(F32)

    def begin():
        for dz in ORDER:
            for i in range(n):
                over_c(i, dz).start()

    def after_c(dz):
        for i in range(n):
            over_c(i, dz).wait_recv()
            for far in range(2):
                yy, xx = ((1 - y if far else y), 1 - x) if dz in x_first else (1 - y, (1 - x if far else x))
                bufs[7 * i + 1][(dz,) + lead(i) + (far,)] = chip_sum(i, dz, yy, xx).astype(BF)
            over_first(i, dz).start()

    def after_first(dz):
        for i in range(n):
            over_first(i, dz).wait_recv()
            yy, xx = (1 - y, x) if dz in x_first else (y, 1 - x)
            total = chip_sum(i, dz, yy, xx) + bufs[7 * i + 2][(dz,) + lead(i) + (1,)].astype(F32)
            bufs[7 * i + 3][dz] = total.astype(BF)
            over_second(i, dz).start()

    def after_second(dz):
        for i in range(n):
            over_second(i, dz).wait_recv()
            total = chip_sum(i, dz, y, x) + bufs[7 * i + 2][(dz,) + lead(i) + (0,)].astype(F32)
            total = total + bufs[7 * i + 4][dz].astype(F32)
            if dz == 0:
                outs[i][...] = total
            else:
                bufs[7 * i + 5][dz] = total.astype(BF)
                over_z(i, dz).start()

    def after_z(dz):
        for i in range(n):
            over_z(i, dz).wait_recv()
            outs[i][...] += bufs[7 * i + 6][dz].astype(F32)

    def finish():
        for i in range(n):
            for dz in range(4):
                over_c(i, dz).wait_send()
                over_first(i, dz).wait_send()
                over_second(i, dz).wait_send()
                if dz:
                    over_z(i, dz).wait_send()

    stages = [[functools.partial(f, dz) for dz in ORDER] for f in (after_c, after_first, after_second)]
    last = [functools.partial(after_z, dz) for dz in (1, 3, 2)]
    return [begin], stages[0], stages[1], stages[2], last, [finish]


def scatter_kernel(leads, *refs):
    n = len(leads)
    grads, small_in = refs[:n], refs[n]
    outs, small_out = refs[n + 1 : 2 * n + 1], refs[2 * n + 1]
    bufs = refs[2 * n + 2 : 9 * n + 2]
    send_sem, recv_sem, hops, small_send, small_recv = refs[9 * n + 2 :]
    y, z, x, c = coords()
    greet()
    stages = scatter_parts(leads, grads, outs, bufs, send_sem, recv_sem, (0, 1))

    def hop(source, target, to):
        return pltpu.make_async_remote_copy(
            src_ref=hops.at[source], dst_ref=hops.at[target], send_sem=small_send.at[target],
            recv_sem=small_recv.at[target], device_id=to, device_id_type=MESH,
        )

    def run(stage):
        for part in stage:
            part()

    run(stages[0])
    hops[0] = small_in[...]
    over_c = hop(0, 1, device(y, z, x, 1 - c))
    over_c.start()
    run(stages[1])
    over_c.wait()
    hops[2] = hops[0] + hops[1]
    over_x = hop(2, 3, device(y, z, 1 - x, c))
    over_x.start()
    run(stages[2])
    over_x.wait()
    hops[4] = hops[2] + hops[3]
    over_y = hop(4, 5, device(1 - y, z, x, c))
    over_y.start()
    run(stages[3])
    over_y.wait()
    hops[6] = hops[4] + hops[5]
    over_z = [hop(6, 6 + dz, device(y, (z + dz) % 4, x, c)) for dz in (1, 2, 3)]
    for one in over_z:
        one.start()
    run(stages[4])
    for one in over_z:
        one.wait()
    small_out[...] = (hops[6] + hops[8]) + (hops[7] + hops[9])
    run(stages[5])


def scatter_all(grads, leads, small, ident):
    n = len(grads)
    views, outs, scratch = scatter_shapes(grads, leads)
    return pl.pallas_call(
        functools.partial(scatter_kernel, leads),
        in_specs=[VMEM] * (n + 1),
        out_specs=[VMEM] * (n + 1),
        out_shape=outs + [jax.ShapeDtypeStruct(small.shape, F32)],
        scratch_shapes=scratch
        + [pltpu.VMEM((10,) + small.shape, F32)]
        + [pltpu.SemaphoreType.DMA((10,))] * 2,
        compiler_params=pltpu.CompilerParams(collective_id=ident, has_side_effects=True, vmem_limit_bytes=VMEM_LIMIT),
        name="scatter",
    )(*views, small)


def run_at(step, schedule):
    for at, parts in enumerate(schedule):
        if parts:

            @pl.when(step == at)
            def _(parts=parts):
                for part in parts:
                    part()


def gather_schedule(parts, steps):
    return [parts[len(parts) * s // steps : len(parts) * (s + 1) // steps] for s in range(steps)]


def in_head(rows, head):
    lane = lax.broadcasted_iota(jnp.int32, (rows, PAIR), 1)
    return lane < HD if head == 0 else lane >= HD


def pick(mask, values):
    return jnp.where(mask, values, jnp.zeros_like(values))


def swap_pairs(values):
    even = lax.broadcasted_iota(jnp.int32, values.shape, 1) % 2 == 0
    return jnp.where(even, pltpu.roll(values, PAIR - 1, 1), pltpu.roll(values, 1, 1))


def turn(values, cosine, signed_sine):
    return values * cosine + swap_pairs(values) * signed_sine


def turn_back(values, cosine, signed_sine):
    return values * cosine - swap_pairs(values) * signed_sine


def angle_tables(places):
    lane = jnp.arange(PAIR)
    inverse_freq = ROPE_BASE ** (-2.0 * ((lane % HD) // 2).astype(F32) / HD)
    angles = places.astype(F32)[:, None] * inverse_freq[None, :]
    sine = jnp.sin(angles)
    return jnp.cos(angles), jnp.where(lane % 2 == 0, -sine, sine)


def project_kernel(with_q, x_ref, w_ref, cos_ref, sin_ref, *outs):
    x = x_ref[...]
    cosine, sine = cos_ref[...], sin_ref[...]
    first = 0 if with_q else 1
    for j in range(first, 3):
        out = outs[j - first]
        full = dot(x, w_ref[j], NT)
        for pair in range(D // PAIR):
            cols = slice(pair * PAIR, (pair + 1) * PAIR)
            part = full[:, cols]
            if j < 2:
                part = turn(part, cosine, sine)
            if j == 0:
                part = part * (0.125 * LOG2E)
            out[:, cols] = part.astype(BF)


def project(x, weights, tables, with_q):
    rows = x.shape[0]
    block = 256
    count = 3 if with_q else 2
    spec = pl.BlockSpec((block, D), lambda i: (i, 0))
    table = pl.BlockSpec((block, PAIR), lambda i: (i, 0))
    return pl.pallas_call(
        functools.partial(project_kernel, with_q),
        grid=(rows // block,),
        in_specs=[spec, pl.BlockSpec((3, D, D), lambda i: (0, 0, 0), pipeline_mode=pl.Buffered(1)), table, table],
        out_specs=[spec] * count,
        out_shape=[jax.ShapeDtypeStruct((rows, D), BF)] * count,
        compiler_params=pltpu.CompilerParams(vmem_limit_bytes=VMEM_LIMIT),
        cost_estimate=pl.CostEstimate(
            flops=2 * rows * D * D * count, bytes_accessed=8 * rows * D + 6 * D * D, transcendentals=0
        ),
        name="project",
    )(x, weights, *tables)


def attend_kernel(second, leads, via_x, *refs):
    n = len(leads)
    q_ref, k_ref, v_ref, bias_ref = refs[:4]
    used = 4
    if second:
        mixed_in, stats_in = refs[4:6]
        used = 6
    shards = refs[used : used + n]
    used += n
    out_a, out_b = refs[used : used + 2]
    used += 2
    if n:
        steps = 12
        parts = gather_parts(leads, shards, refs[used : used + n], *refs[used + n :], via_x)
        run_at(pl.program_id(0) * 2 + pl.program_id(1), gather_schedule(parts, steps))
    keys, rows = k_ref.shape[0], q_ref.shape[0]
    q, k = q_ref[...], k_ref[...]
    bias = bias_ref[...]
    v_cols = jnp.transpose(v_ref[...].astype(F32)).astype(BF)
    outs = []
    for head in range(2):
        span = slice(head * HD, (head + 1) * HD)
        one, two = slice(head, head + 1), slice(2 + head, 3 + head)
        s = dot(k, pick(in_head(rows, head), q), NT) + bias
        peak = jnp.max(s, axis=0, keepdims=True)
        if second:
            before = stats_in[0, one, :]
            peak = jnp.maximum(peak, before)
        p = jnp.exp2(s - peak).astype(BF)
        v_aug = jnp.concatenate([v_cols[span], jnp.ones((16, keys), BF)], axis=0)
        mixed = dot(v_aug, p, NN)
        total = mixed[HD : HD + 1]
        mixed = mixed[:HD]
        if second:
            shrink = jnp.exp2(before - peak)
            total = total + shrink * stats_in[0, two, :]
            mixed = mixed + shrink * mixed_in[span, :]
            outs.append(mixed / total)
            out_b[0, one, :] = peak + jnp.log2(total)
        else:
            out_a[span, :] = mixed
            out_b[0, one, :] = peak
            out_b[0, two, :] = total
    if second:
        out_a[...] = jnp.transpose(jnp.concatenate(outs, axis=0)).astype(BF)


def attend(q, k, v, bias, state=None, shards=(), leads=(), ident=None, via_x=()):
    rows, keys = q.shape[0], k.shape[0]
    block = rows // 2
    pairs = D // PAIR
    n = len(shards)
    q_spec = pl.BlockSpec((block, PAIR), lambda p, i: (i, p))
    k_spec = pl.BlockSpec((keys, PAIR), lambda p, i: (0, p))
    mix_spec = pl.BlockSpec((PAIR, block), lambda p, i: (p, i))
    stat_spec = pl.BlockSpec((1, 8, block), lambda p, i: (p, 0, i))
    stats = jax.ShapeDtypeStruct((pairs, 8, rows), F32)
    params = dict(collective_id=ident, has_side_effects=True) if n else {}
    second = state is not None
    out = pl.pallas_call(
        functools.partial(attend_kernel, second, leads, via_x),
        grid=(pairs, 2),
        in_specs=[q_spec, k_spec, k_spec, pl.BlockSpec((keys, 1), lambda p, i: (0, 0))]
        + ([mix_spec, stat_spec] if second else [])
        + [HBM] * n,
        out_specs=[q_spec if second else mix_spec, stat_spec] + [HBM] * n,
        out_shape=[jax.ShapeDtypeStruct(q.shape, BF) if second else jax.ShapeDtypeStruct((D, rows), F32), stats]
        + full_shapes(shards, leads),
        scratch_shapes=gather_sems(n) if n else [],
        compiler_params=pltpu.CompilerParams(vmem_limit_bytes=VMEM_LIMIT, **params),
        cost_estimate=pl.CostEstimate(
            flops=16 * rows * keys * D, bytes_accessed=8 * (rows + keys) * D, transcendentals=rows * keys * 12
        ),
        name="attend",
    )(q, k, v, bias, *(state or ()), *shards)
    return out[0], out[1], flatten_full(out[2:], shards, leads)


def attend_back_kernel(second, leads, *refs):
    n = len(leads)
    q_ref, k_ref, v_ref, do_ref, lse_ref, extra_ref, bias_ref, cosk_ref, sink_ref = refs[:9]
    used = 9
    if second:
        cosq_ref, sinq_ref, dq_in = refs[9:12]
        used = 12
    grads = refs[used : used + n]
    used += n
    dq_ref, dk_ref, dv_ref = refs[used : used + 3]
    used += 3
    if not second:
        delta_ref = refs[used]
        used += 1
    outs = refs[used : used + n]
    used += n
    if second:
        dq_cols = refs[used]
        used += 1
    else:
        dq_cols = dq_ref
    pair, step = pl.program_id(0), pl.program_id(1)
    if n:
        parts = scatter_parts(leads, grads, outs, refs[used : used + 7 * n], *refs[used + 7 * n :], (0, 1))
        start, cores, firsts, seconds, lasts, end = parts
        schedule = [
            [greet] + start, cores[:2], cores[2:], firsts[:1], firsts[1:2], firsts[2:3], firsts[3:] + seconds[:1],
            seconds[1:2], seconds[2:3], seconds[3:], lasts[:1], lasts[1:] + end,
        ]
        run_at(pair * 2 + step, schedule)
    rows, keys = q_ref.shape[0], k_ref.shape[0]
    part = min(256, rows)
    k, v, bias = k_ref[...], v_ref[...], bias_ref[...]
    k_cols = jnp.transpose(k.astype(F32)).astype(BF)

    @pl.when(step == 0)
    def _():
        if second:
            dq_cols[...] = dq_in[...]
        else:
            dq_cols[...] = jnp.zeros_like(dq_cols)
            both = jnp.transpose(do_ref[...].astype(F32) * extra_ref[...].astype(F32))
            delta_ref[0, 0:1, :] = jnp.sum(both[:HD], axis=0, keepdims=True)
            delta_ref[0, 1:2, :] = jnp.sum(both[HD:], axis=0, keepdims=True)

    delta = extra_ref if second else delta_ref
    dk = jnp.zeros((keys, PAIR), F32)
    dv = jnp.zeros((keys, PAIR), F32)
    for first in range(0, rows, part):
        here = slice(first, first + part)
        q, do = q_ref[here, :], do_ref[here, :]
        for head in range(2):
            mine = in_head(part, head)
            one = slice(head, head + 1)
            q_head, do_head = pick(mine, q), pick(mine, do)
            s = dot(k, q_head, NT)
            p = jnp.exp2(s - lse_ref[0, one, here] + bias)
            dp = dot(v, do_head, NT)
            ds = (p * (dp - delta[0, one, here])).astype(BF)
            dv += dot(p.astype(BF), do_head, NN)
            dk += dot(ds, q_head, NN)
            span = slice(head * HD, (head + 1) * HD)
            dq_cols[span, here] += dot(k_cols[span], ds, NN)
    dk_ref[...] = turn_back(dk * LN2, cosk_ref[...], sink_ref[...]).astype(BF)
    dv_ref[...] = dv.astype(BF)

    if second:

        @pl.when(step == pl.num_programs(1) - 1)
        def _():
            dq = jnp.transpose(dq_cols[...]) * 0.125
            dq_ref[...] = turn_back(dq, cosq_ref[...], sinq_ref[...]).astype(BF)


def attend_back(q, k, v, do, lse, extra, bias, k_tables, second=None, grads=(), leads=(), ident=None):
    rows, keys = q.shape[0], k.shape[0]
    block = keys // 2
    pairs = D // PAIR
    n = len(grads)
    q_spec = pl.BlockSpec((rows, PAIR), lambda p, i: (0, p))
    k_spec = pl.BlockSpec((block, PAIR), lambda p, i: (i, p))
    stat_spec = pl.BlockSpec((1, 8, rows), lambda p, i: (p, 0, 0))
    q_table = pl.BlockSpec((rows, PAIR), lambda p, i: (0, 0))
    k_table = pl.BlockSpec((block, PAIR), lambda p, i: (i, 0))
    col_spec = pl.BlockSpec((PAIR, rows), lambda p, i: (p, 0))
    kd = jax.ShapeDtypeStruct(k.shape, BF)
    stats = jax.ShapeDtypeStruct((pairs, 8, rows), F32)
    cols = jax.ShapeDtypeStruct((D, rows), F32)
    is_second = second is not None
    views, sums, scratch = scatter_shapes(grads, leads) if n else ([], [], [])
    more = (*second[0], second[1]) if is_second else ()
    params = dict(collective_id=ident, has_side_effects=True) if n else {}
    return pl.pallas_call(
        functools.partial(attend_back_kernel, is_second, leads),
        grid=(pairs, 2),
        in_specs=[
            q_spec, k_spec, k_spec, q_spec, stat_spec, stat_spec if is_second else q_spec,
            pl.BlockSpec((block, 1), lambda p, i: (i, 0)), k_table, k_table,
        ]
        + ([q_table, q_table, col_spec] if is_second else [])
        + [VMEM] * n,
        out_specs=[q_spec if is_second else col_spec, k_spec, k_spec]
        + ([] if is_second else [stat_spec])
        + [VMEM] * n,
        out_shape=[jax.ShapeDtypeStruct(q.shape, BF) if is_second else cols, kd, kd]
        + ([] if is_second else [stats])
        + sums,
        scratch_shapes=([pltpu.VMEM((PAIR, rows), F32)] if is_second else []) + scratch,
        compiler_params=pltpu.CompilerParams(vmem_limit_bytes=VMEM_LIMIT, **params),
        cost_estimate=pl.CostEstimate(
            flops=40 * rows * keys * D, bytes_accessed=8 * (rows + keys) * D, transcendentals=rows * keys * 12
        ),
        name="attend_back",
    )(q, k, v, do, lse, extra, bias, *k_tables, *more, *views)


def norm(values):
    centre = values - jnp.mean(values, axis=-1, keepdims=True)
    inverse = lax.rsqrt(jnp.mean(centre * centre, axis=-1, keepdims=True) + EPSILON)
    return centre * inverse, inverse


def norm_back(grad_result, normed, inverse, gain):
    scaled = grad_result * gain
    return inverse * (
        scaled
        - jnp.mean(scaled, axis=-1, keepdims=True)
        - normed * jnp.mean(scaled * normed, axis=-1, keepdims=True)
    )


def middle_kernel(
    ints, scale_ref, ctx_ref, x_ref, teacher_ref, vec_ref, wo_ref, wi_ref, wd_ref,
    out_ref, act_ref, hin_ref, gb_ref, gp_ref, ga_ref, gc_ref, gr_ref, part_ref, slope_ref,
):
    block = ctx_ref.shape[0]
    chunk = 512
    hidden_units = wi_ref.shape[0]
    gain_one, bias_one, gain_two, bias_two = (vec_ref[i : i + 1, :] for i in range(4))
    attended = dot(ctx_ref[...], wo_ref[...], NN)
    normed_one, inverse_one = norm(x_ref[...].astype(F32) + attended)
    hidden = normed_one * gain_one + bias_one
    hidden_in = hidden.astype(BF)
    hin_ref[...] = hidden_in
    total = hidden
    for first in range(0, hidden_units, chunk):
        here = slice(first, first + chunk)
        pre = dot(hidden_in, wi_ref[here, :], NT)
        below = 0.5 + 0.5 * lax.erf(pre * INV_ROOT2)
        act = (pre * below).astype(BF)
        act_ref[:, here] = act
        slope_ref[:, here] = below + pre * jnp.exp(-0.5 * pre * pre) * INV_ROOT_TWO_PI
        total = total + dot(act, wd_ref[here, :], NN)
    normed_two, inverse_two = norm(total)
    final = normed_two * gain_two + bias_two
    out_ref[...] = final.astype(BF)
    place = ints[1] + pl.program_id(0) * block + lax.broadcasted_iota(jnp.int32, (block, D), 0)
    misfit = jnp.where(place < ints[0], final - teacher_ref[...].astype(F32), 0.0)
    grad_final = misfit * scale_ref[0]
    grad_mid = norm_back(grad_final, normed_two, inverse_two, gain_two)
    g_branch = grad_mid.astype(BF)
    gb_ref[...] = g_branch
    grad_hidden = grad_mid
    for first in range(0, hidden_units, chunk):
        here = slice(first, first + chunk)
        grad_act = dot(g_branch, wd_ref[here, :], NT)
        g_pre = (grad_act * slope_ref[:, here]).astype(BF)
        gp_ref[:, here] = g_pre
        grad_hidden = grad_hidden + dot(g_pre, wi_ref[here, :], NN)
    grad_res = norm_back(grad_hidden, normed_one, inverse_one, gain_one)
    gr_ref[...] = grad_res
    g_att = grad_res.astype(BF)
    ga_ref[...] = g_att
    gc_ref[...] = dot(g_att, wo_ref[...], NT).astype(BF)

    @pl.when(pl.program_id(0) == 0)
    def _():
        part_ref[...] = jnp.zeros_like(part_ref)

    for row, term in enumerate(
        (grad_hidden * normed_one, grad_hidden, grad_final * normed_two, grad_final, misfit * misfit)
    ):
        part_ref[row : row + 1, :] += jnp.sum(term, axis=0, keepdims=True)


def middle(ints, scale, context, x, teacher, vectors, out_full, in_full, down_full):
    rows = x.shape[0]
    block = 256
    hidden_units = in_full.shape[0]
    row = pl.BlockSpec((block, D), lambda i: (i, 0))
    wide = pl.BlockSpec((block, hidden_units), lambda i: (i, 0))

    def fixed(shape):
        return pl.BlockSpec(shape, lambda i: (0, 0), pipeline_mode=pl.Buffered(1))

    narrow_out = jax.ShapeDtypeStruct((rows, D), BF)
    wide_out = jax.ShapeDtypeStruct((rows, hidden_units), BF)
    return pl.pallas_call(
        middle_kernel,
        grid=(rows // block,),
        in_specs=[
            SMEM, SMEM, row, row, row, fixed((8, D)), fixed((D, D)), fixed((hidden_units, D)), fixed((hidden_units, D)),
        ],
        out_specs=[row, wide, row, row, wide, row, row, row, pl.BlockSpec((8, D), lambda i: (0, 0))],
        out_shape=[
            narrow_out, wide_out, narrow_out, narrow_out, wide_out, narrow_out, narrow_out,
            jax.ShapeDtypeStruct((rows, D), F32), jax.ShapeDtypeStruct((8, D), F32),
        ],
        scratch_shapes=[pltpu.VMEM((block, hidden_units), F32)],
        compiler_params=pltpu.CompilerParams(vmem_limit_bytes=VMEM_LIMIT),
        cost_estimate=pl.CostEstimate(
            flops=2 * rows * D * (2 * D + 4 * hidden_units),
            bytes_accessed=30 * rows * D + 4 * hidden_units * (rows + D),
            transcendentals=2 * rows * hidden_units,
        ),
        name="middle",
    )(ints, scale, context, x, teacher, vectors, out_full, in_full, down_full)


def on_device(
    layer_input, teacher, lengths, qkv_weight, out_weight, ln1_gain, ln1_bias,
    in_weight, down_weight, ln2_gain, ln2_bias,
):
    own_rows = layer_input.shape[0]
    data_size = lax.axis_size("dp")
    tensor_index = lax.axis_index("tensor")
    group_rows = own_rows * lax.axis_size("tensor")
    assert group_rows == SLOT and lax.axis_size("tensor") == 2 and lengths.shape[0] == 1
    own_comm = data_size == 16

    def gather(values, axis):
        return lax.all_gather(values, EVERYONE, axis=axis, tiled=True)

    def scatter(values, axis):
        return lax.psum_scatter(values, EVERYONE, scatter_dimension=axis, tiled=True)

    def swap(values):
        return lax.ppermute(values, "tensor", [(0, 1), (1, 0)])

    share = D // data_size
    own_first = tensor_index * own_rows
    own_places = own_first + jnp.arange(own_rows)
    other_places = (own_rows - own_first) + jnp.arange(own_rows)

    def bias_of(places):
        return jnp.where(places < lengths[0], 0.0, NEG_LARGE).astype(F32)[:, None]

    own_bias, other_bias = bias_of(own_places), bias_of(other_places)
    own_tables, other_tables = angle_tables(own_places), angle_tables(other_places)

    other_x = swap(layer_input)
    norms = (ln1_gain, ln1_bias, ln2_gain, ln2_bias)
    if own_comm:
        small = jnp.zeros((8, 128), F32)
        for row, vec in enumerate(norms):
            small = small.at[row, :share].set(vec.astype(F32))
        small = small.at[4, 0].set(lengths[0].astype(F32))
        qkv_full, small_full = gather_all([qkv_weight, small], [1, 0], 0)
        small_full = small_full.reshape(2, data_size, 8, 128)[0]
        vectors = small_full[:, :, :share].transpose(1, 0, 2).reshape(8, D)
        valid_count = jnp.sum(small_full[:, 4, 0])
        down_shard, qkv_full = lax.optimization_barrier((down_weight, qkv_full))
    else:
        qkv_full = gather(qkv_weight, 1)
        vectors = jnp.stack([lax.all_gather(v, "dp", axis=0, tiled=True).astype(F32) for v in norms])
        vectors = jnp.concatenate([vectors, jnp.zeros((4, D), F32)])
        valid_count = lax.psum(jnp.sum(lengths).astype(F32), "dp")
        down_shard = down_weight
    down_full = gather(down_shard, 0)

    q, k_own, v_own = project(layer_input, qkv_full, own_tables, True)
    if own_comm:
        *state, (out_full,) = attend(q, k_own, v_own, own_bias, None, [out_weight], [0], 1, (0, 1, 2, 3))
    else:
        *state, _ = attend(q, k_own, v_own, own_bias)
        out_full, in_full = gather(out_weight, 0), gather(in_weight, 0)
    k_other, v_other = project(other_x, qkv_full, other_tables, False)
    if own_comm:
        context, lse, (in_full,) = attend(q, k_other, v_other, other_bias, state, [in_weight], [0], 2, (0, 1))
    else:
        context, lse, _ = attend(q, k_other, v_other, other_bias, state)

    grad_scale = group_rows * data_size * D // 4
    scale = (2.0 * grad_scale / (valid_count * D)).reshape(1)
    ints = jnp.stack([lengths[0], own_first.astype(jnp.int32)])
    final, activated, hidden_in, g_branch, g_pre, g_att, g_context, grad_res, parts = middle(
        ints, scale, context, layer_input, teacher, vectors, out_full, in_full, down_full
    )

    def over_rows(left, right):
        return lax.dot_general(left, right, (((0,), (0,)), ((), ())), preferred_element_type=F32)

    grad_down_w = over_rows(activated, g_branch)
    grad_in_w = over_rows(g_pre, hidden_in)
    grad_out_w = over_rows(context, g_att)
    if own_comm:
        grad_down = scatter(grad_down_w.astype(BF), 0).astype(F32)
        sum_first, sum_second = [grad_in_w.astype(BF)], [grad_out_w.astype(BF)]
    else:
        grad_down, grad_in, grad_out = scatter(grad_down_w, 0), scatter(grad_in_w, 0), scatter(grad_out_w, 0)
        sum_first, sum_second = [], []

    dq_part, dk_other, dv_other, delta, *sums = attend_back(
        q, k_other, v_other, g_context, lse, context, other_bias, other_tables, None, sum_first, [0] * len(sum_first), 3
    )
    if own_comm:
        grad_in = sums[0]
    pass_on = dot(dk_other, qkv_full[1], NN) + dot(dv_other, qkv_full[2], NN)
    from_other = swap(pass_on.astype(BF))
    dq, dk_own, dv_own, *sums = attend_back(
        q, k_own, v_own, g_context, lse, delta, own_bias, own_tables, (own_tables, dq_part),
        sum_second, [0] * len(sum_second), 4,
    )
    if own_comm:
        grad_out = sums[0]
    grad_qkv_w = jnp.stack(
        [
            over_rows(dq, layer_input),
            over_rows(dk_own, layer_input) + over_rows(dk_other, other_x),
            over_rows(dv_own, layer_input) + over_rows(dv_other, other_x),
        ]
    )
    if own_comm:
        grad_qkv, sums = scatter_all([grad_qkv_w.astype(BF)], [1], parts, 5)
    else:
        grad_qkv = scatter(grad_qkv_w, 1)
        sums = lax.psum(parts, ("dp", "tensor"))
    input_grad = (
        grad_res
        + dot(dq, qkv_full[0], NN)
        + dot(dk_own, qkv_full[1], NN)
        + dot(dv_own, qkv_full[2], NN)
        + from_other.astype(F32)
    )
    loss_value = jnp.sum(sums[4]) / (valid_count * D)
    own_norms = lax.dynamic_slice_in_dim(sums, lax.axis_index("dp") * share, share, 1)
    return (
        final, loss_value, input_grad, grad_qkv, grad_out,
        own_norms[0], own_norms[1], grad_in, grad_down, own_norms[2], own_norms[3],
    )


def solution(mesh):
    rows = P(("dp", "tensor"), None)
    shard = P(EVERYONE, None)
    in_specs = (
        rows, rows, P("dp"), P(None, EVERYONE, None), shard, P("dp"), P("dp"), shard, shard, P("dp"), P("dp"),
    )
    out_specs = (
        rows, P(), rows, P(None, EVERYONE, None), shard, P("dp"), P("dp"), shard, shard, P("dp"), P("dp"),
    )
    return jax.shard_map(on_device, mesh=mesh, in_specs=in_specs, out_specs=out_specs, check_vma=False)
```

```python
import functools

import jax
import jax.numpy as jnp
from jax import lax
from jax.experimental import pallas as pl
from jax.experimental.pallas import tpu as pltpu
from jax.sharding import PartitionSpec as P

D = 768
HD = 64
SLOT = 2048
PAIR = 2 * HD
EPSILON = 1e-05
NEG_LARGE = -1e30
ROPE_BASE = 10000.0
INV_ROOT2 = 0.7071067811865476
INV_ROOT_TWO_PI = 0.3989422804014327
LOG2E = 1.4426950408889634
LN2 = 0.6931471805599453
EVERYONE = ("tensor", "dp")

BF = jnp.bfloat16
F32 = jnp.float32
NT = (((1,), (1,)), ((), ()))
NN = (((1,), (0,)), ((), ()))
VMEM_LIMIT = 56 << 20
MESH = pl.DeviceIdType.MESH
HBM = pl.BlockSpec(memory_space=pl.ANY)
VMEM = pl.BlockSpec(memory_space=pltpu.VMEM)
SMEM = pl.BlockSpec(memory_space=pltpu.SMEM)


def dot(a, b, dims):
    return lax.dot_general(a, b, dims, preferred_element_type=F32)


GRID = (2, 4, 2, 2)
ORDER = (2, 1, 3, 0)


def coords():
    dp = lax.axis_index("dp")
    return lax.axis_index("tensor"), dp // 4, (dp // 2) % 2, dp % 2


def device(y, z, x, c):
    return (z * 4 + x * 2 + c, y)


def greet():
    y, z, x, c = coords()
    barrier = pltpu.get_barrier_semaphore()
    peers = [device(y, (z + dz) % 4, x, c) for dz in (1, 2, 3)]
    peers += [device(1 - y, z, x, c), device(y, z, 1 - x, c), device(y, z, x, 1 - c)]
    for peer in peers:
        pl.semaphore_signal(barrier, inc=1, device_id=peer, device_id_type=MESH)
    pl.semaphore_wait(barrier, len(peers))


def full_shapes(shards, leads):
    return [jax.ShapeDtypeStruct(s.shape[:l] + (32 * s.shape[l],) + s.shape[l + 1 :], s.dtype) for s, l in zip(shards, leads)]


DELTAS = (0, -1, 1, -2, 2, -3, 3)


def gather_sems(count):
    return [pltpu.SemaphoreType.DMA((count, 81)), pltpu.SemaphoreType.DMA((count, 32))]


def gather_parts(order, leads, shards, fulls, send_sem, recv_sem):
    y, z, x, c = coords()
    to_y, to_x, to_c = device(1 - y, z, x, c), device(y, z, 1 - x, c), device(y, z, x, 1 - c)
    own = (0, 0, 0)

    def arrives_over(block):
        apart = dict(zip("yzx", block))
        return [axis for axis in order if apart[axis]][-1]

    def plan(i):
        at = (slice(None),) * leads[i]
        shard, full = shards[i], fulls[i]
        count = shard.shape[leads[i]]

        def spot(block):
            dy, delta, dx = block
            place = (y if dy == 0 else 1 - y) * 16 + (z + delta) * 4 + (x if dx == 0 else 1 - x) * 2 + c
            return full.at[at + (pl.ds(pl.multiple_of(place * count, 8), count),)]

        def copy(block, send_slot, dy, dx, to, recv_base=0):
            place = z + block[1]
            return pltpu.make_async_remote_copy(
                src_ref=shard if block == own else spot(block),
                dst_ref=spot(block),
                send_sem=send_sem.at[i, send_slot + 8 * block[2] + 4 * block[0] + place],
                recv_sem=recv_sem.at[i, recv_base + 8 * dx + 4 * dy + place],
                device_id=to,
                device_id_type=MESH,
            )

        return dict(
            right=lambda b: copy(b, 0, b[0], b[2], device(y, z + 1, x, c)),
            left=lambda b: copy(b, 16, b[0], b[2], device(y, z - 1, x, c)),
            y=lambda b: copy(b, 32, 1, b[2], to_y),
            x=lambda b: copy(b, 48, b[0], 1, to_x),
            core=lambda b: copy(b, 64, b[0], b[2], to_c, 16),
            landed=lambda b: copy(b, 64, b[0], b[2], to_c),
            local=lambda: pltpu.make_async_copy(shard, spot(own), send_sem.at[i, 80]),
        )

    plans = [plan(i) for i in range(len(shards))]

    def when_there(block, action):
        if block[1] == 0:
            action()
        else:
            pl.when((z + block[1] >= 0) & (z + block[1] <= 3))(action)

    def onward(p, block, run, axes=None):
        axis = None if block == own else arrives_over(block)
        if axes is None:
            axes = order if axis is None else order[order.index(axis) + (axis != "z") :]
        for later in axes:
            if later != "z":
                run(p[later](block))
                continue
            if block[1] <= 0:
                pl.when(z < 3)(lambda: run(p["right"](block)))
            if block[1] >= 0:
                pl.when(z > 0)(lambda: run(p["left"](block)))

    def begin(axes, last):
        for p in plans:
            onward(p, own, lambda copy: copy.start(), axes)
            if last:
                p["core"](own).start()
                p["local"]().start()

    def after(block):
        def action():
            for p in plans:
                p["landed"](block).wait_recv()
                onward(p, block, lambda copy: copy.start())
                p["core"](block).start()

        when_there(block, action)

    def finish():
        def action_of(block):
            def action():
                for p in plans:
                    onward(p, block, lambda copy: copy.wait_send())
                    p["core"](block).wait()

            return action

        for dy in range(2):
            for dx in range(2):
                for delta in DELTAS:
                    when_there((dy, delta, dx), action_of((dy, delta, dx)))
        for p in plans:
            p["local"]().wait()

    return begin, after, finish


def both_ways(dy, distance, dx):
    return [(dy, delta, dx) for delta in ((0,) if distance == 0 else (-distance, distance))]


def scatter_shapes(grads, leads):
    views, outs, scratch = [], [], []
    for g, l in zip(grads, leads):
        head, rows, tail = g.shape[:l], g.shape[l] // 32, g.shape[l + 1 :]
        if not isinstance(g, jax.ShapeDtypeStruct):
            views.append(g.reshape(head + GRID + (rows,) + tail))
        shard = head + (rows,) + tail
        outs.append(jax.ShapeDtypeStruct(shard, F32))
        wide = pltpu.VMEM((4,) + head + (2, 2, rows) + tail, BF)
        pair = pltpu.VMEM((4,) + head + (2, rows) + tail, BF)
        one = pltpu.VMEM((4,) + shard, BF)
        scratch += [wide, pair, pair, one, one, one, one]
    count = len(grads)
    return views, outs, scratch + [pltpu.SemaphoreType.DMA((count, 16))] * 2


def scatter_parts(leads, grads, outs, bufs, send_sem, recv_sem, x_first):
    y, z, x, c = coords()
    n = len(leads)
    to_y, to_x, to_c = device(1 - y, z, x, c), device(y, z, 1 - x, c), device(y, z, x, 1 - c)

    def zz(dz):
        return (z + dz) % 4

    def lead(i):
        return (slice(None),) * leads[i]

    def copy(i, slot, source, target, to):
        return pltpu.make_async_remote_copy(
            src_ref=source, dst_ref=target, send_sem=send_sem.at[i, slot], recv_sem=recv_sem.at[i, slot],
            device_id=to, device_id_type=MESH,
        )

    def over_c(i, dz):
        return copy(i, dz, grads[i].at[lead(i) + (slice(None), zz(dz), slice(None), 1 - c)], bufs[7 * i].at[dz], to_c)

    def over_first(i, dz):
        to = to_x if dz in x_first else to_y
        return copy(i, 4 + dz, bufs[7 * i + 1].at[dz], bufs[7 * i + 2].at[dz], to)

    def over_second(i, dz):
        to = to_y if dz in x_first else to_x
        return copy(i, 8 + dz, bufs[7 * i + 3].at[dz], bufs[7 * i + 4].at[dz], to)

    def over_z(i, dz):
        return copy(i, 12 + dz, bufs[7 * i + 5].at[dz], bufs[7 * i + 6].at[dz], device(y, zz(dz), x, c))

    def chip_sum(i, dz, yy, xx):
        own = grads[i][lead(i) + (yy, zz(dz), xx, c)].astype(F32)
        return own + bufs[7 * i][(dz,) + lead(i) + (yy, xx)].astype(F32)

    def begin():
        for dz in ORDER:
            for i in range(n):
                over_c(i, dz).start()

    def after_c(dz):
        for i in range(n):
            over_c(i, dz).wait_recv()
            for far in range(2):
                yy, xx = ((1 - y if far else y), 1 - x) if dz in x_first else (1 - y, (1 - x if far else x))
                bufs[7 * i + 1][(dz,) + lead(i) + (far,)] = chip_sum(i, dz, yy, xx).astype(BF)
            over_first(i, dz).start()

    def after_first(dz):
        for i in range(n):
            over_first(i, dz).wait_recv()
            yy, xx = (1 - y, x) if dz in x_first else (y, 1 - x)
            total = chip_sum(i, dz, yy, xx) + bufs[7 * i + 2][(dz,) + lead(i) + (1,)].astype(F32)
            bufs[7 * i + 3][dz] = total.astype(BF)
            over_second(i, dz).start()

    def after_second(dz):
        for i in range(n):
            over_second(i, dz).wait_recv()
            total = chip_sum(i, dz, y, x) + bufs[7 * i + 2][(dz,) + lead(i) + (0,)].astype(F32)
            total = total + bufs[7 * i + 4][dz].astype(F32)
            if dz == 0:
                outs[i][...] = total
            else:
                bufs[7 * i + 5][dz] = total.astype(BF)
                over_z(i, dz).start()

    def after_z(dz):
        for i in range(n):
            over_z(i, dz).wait_recv()
            outs[i][...] += bufs[7 * i + 6][dz].astype(F32)

    def finish():
        for i in range(n):
            for dz in range(4):
                over_c(i, dz).wait_send()
                over_first(i, dz).wait_send()
                over_second(i, dz).wait_send()
                if dz:
                    over_z(i, dz).wait_send()

    stages = [[functools.partial(f, dz) for dz in ORDER] for f in (after_c, after_first, after_second)]
    last = [functools.partial(after_z, dz) for dz in ORDER[:3]]
    return [begin], stages[0], stages[1], stages[2], last, [finish]


def tail_kernel(
    dq_hbm, dk_hbm, dv_hbm, dk_far_hbm, dv_far_hbm, x_hbm, far_hbm, w_hbm, res_hbm, small_in,
    out_q, out_k, out_v, small_out, input_hbm,
    dq, dk, dv, dk_far, dv_far, x, far, w, res, load_sem, store_sem, grad_q, grad_k, grad_v, *refs,
):
    sums = (out_q, out_k, out_v)
    grads = (grad_q, grad_k, grad_v)
    per = 9
    hops, small_send, small_recv = refs[3 * per :]
    y, z, at_x, c = coords()
    rows = x.shape[0]
    pairs = (
        (dq_hbm, dq), (x_hbm, x), (dk_hbm, dk), (dk_far_hbm, dk_far), (far_hbm, far), (dv_hbm, dv),
        (dv_far_hbm, dv_far), (w_hbm, w), (res_hbm, res),
    )
    loads = [pltpu.make_async_copy(src, dst, load_sem.at[i]) for i, (src, dst) in enumerate(pairs)]
    for load in loads:
        load.start()
    greet()
    stages = [
        scatter_parts([0], grads[j : j + 1], sums[j : j + 1], refs[per * j : per * j + 7], *refs[per * j + 7 : per * j + 9], (0, 1))
        for j in range(3)
    ]

    def run(j, stage):
        for part in stages[j][stage]:
            part()

    def hop(source, target, to):
        return pltpu.make_async_remote_copy(
            src_ref=hops.at[source], dst_ref=hops.at[target], send_sem=small_send.at[target],
            recv_sem=small_recv.at[target], device_id=to, device_id_type=MESH,
        )

    hops[0] = small_in[...]
    over_c = hop(0, 1, device(y, z, at_x, 1 - c))
    over_c.start()

    def weight_grad(j, terms):
        half = D // 2
        for yy in range(2):
            cols = slice(yy * half, (yy + 1) * half)
            total = None
            for left, right in terms:
                part = dot(left[:, cols], right[...], (((0,), (0,)), ((), ())))
                total = part if total is None else total + part
            grads[j][yy] = total.astype(BF).reshape(grads[j].shape[1:])
        run(j, 0)

    def input_block(block):
        here = slice(block * ROWS_STEP, (block + 1) * ROWS_STEP)
        total = res[here, :]
        for j, left in enumerate((dq, dk, dv)):
            total = total + dot(left[here, :], w[j], NN)
        res[here, :] = total
        pltpu.make_async_copy(res.at[here], input_hbm.at[here], store_sem.at[block]).start()

    loads[0].wait()
    loads[1].wait()
    weight_grad(0, [(dq, x)])
    for i in (2, 3, 4):
        loads[i].wait()
    weight_grad(1, [(dk, x), (dk_far, far)])
    run(0, 1)
    loads[5].wait()
    loads[6].wait()
    weight_grad(2, [(dv, x), (dv_far, far)])
    run(1, 1)
    over_c.wait()
    hops[2] = hops[0] + hops[1]
    over_x = hop(2, 3, device(y, z, 1 - at_x, c))
    over_x.start()
    run(0, 2)
    run(2, 1)
    for i in (7, 8):
        loads[i].wait()
    input_block(0)
    over_x.wait()
    hops[4] = hops[2] + hops[3]
    over_y = hop(4, 5, device(1 - y, z, at_x, c))
    over_y.start()
    run(0, 3)
    run(1, 2)
    input_block(1)
    run(1, 3)
    run(2, 2)
    over_y.wait()
    hops[6] = hops[4] + hops[5]
    over_z = [hop(6, 6 + dz, device(y, (z + dz) % 4, at_x, c)) for dz in (1, 2, 3)]
    for one in over_z:
        one.start()
    input_block(2)
    run(2, 3)
    run(0, 4)
    input_block(3)
    run(1, 4)
    run(2, 4)
    for one in over_z:
        one.wait()
    small_out[...] = (hops[6] + hops[8]) + (hops[7] + hops[9])
    for j in range(3):
        run(j, 5)
    for block in range(rows // ROWS_STEP):
        here = slice(block * ROWS_STEP, (block + 1) * ROWS_STEP)
        pltpu.make_async_copy(res.at[here], input_hbm.at[here], store_sem.at[block]).wait()


def tail(dq, dk, dv, dk_far, dv_far, x, far, w, res, small, ident):
    rows = x.shape[0]
    share = D // 32
    grad = jax.ShapeDtypeStruct((D, D), BF)
    outs, scratch = [], []
    for _ in range(3):
        _, out, bufs = scatter_shapes([grad], [0])
        outs += out
        scratch += bufs
    narrow = pltpu.VMEM((rows, D), BF)
    out = pl.pallas_call(
        tail_kernel,
        in_specs=[HBM] * 9 + [VMEM],
        out_specs=[VMEM] * 4 + [HBM],
        out_shape=outs + [jax.ShapeDtypeStruct(small.shape, F32), jax.ShapeDtypeStruct((rows, D), F32)],
        scratch_shapes=[narrow] * 7
        + [pltpu.VMEM((3, D, D), BF), pltpu.VMEM((rows, D), F32)]
        + [pltpu.SemaphoreType.DMA((9,)), pltpu.SemaphoreType.DMA((rows // ROWS_STEP,))]
        + [pltpu.VMEM(GRID + (share, D), BF)] * 3
        + scratch
        + [pltpu.VMEM((10,) + small.shape, F32)]
        + [pltpu.SemaphoreType.DMA((10,))] * 2,
        compiler_params=pltpu.CompilerParams(collective_id=ident, has_side_effects=True, vmem_limit_bytes=VMEM_LIMIT),
        name="tail",
    )(dq, dk, dv, dk_far, dv_far, x, far, w, res, small)
    return jnp.stack(out[:3]), out[3], out[4]


def run_at(step, schedule):
    for at, parts in enumerate(schedule):
        if parts:

            @pl.when(step == at)
            def _(parts=parts):
                for part in parts:
                    part()


def in_head(rows, head):
    lane = lax.broadcasted_iota(jnp.int32, (rows, PAIR), 1)
    return lane < HD if head == 0 else lane >= HD


def pick(mask, values):
    return jnp.where(mask, values, jnp.zeros_like(values))


def swap_pairs(values):
    even = lax.broadcasted_iota(jnp.int32, values.shape, 1) % 2 == 0
    return jnp.where(even, pltpu.roll(values, PAIR - 1, 1), pltpu.roll(values, 1, 1))


def turn(values, cosine, signed_sine):
    return values * cosine + swap_pairs(values) * signed_sine


def turn_back(values, cosine, signed_sine):
    return values * cosine - swap_pairs(values) * signed_sine


def angle_tables():
    lane = jnp.arange(PAIR)
    inverse_freq = ROPE_BASE ** (-2.0 * ((lane % HD) // 2).astype(F32) / HD)
    places = jnp.concatenate([jnp.arange(SLOT // 64) * 64, jnp.arange(64)]).astype(F32)
    angles = places[:, None] * inverse_freq[None, :]
    return jnp.stack([jnp.cos(angles), jnp.sin(angles)])


ROWS_STEP = 256
QUERY_STEP = 512


def front_plan(rows):
    project_steps = rows // ROWS_STEP
    attend_steps = (D // PAIR) * (rows // QUERY_STEP)
    return project_steps, attend_steps


def project_step(side, block, x_ref, w_ref, cos_ref, sin_ref, q_ref, k_ref, v_ref):
    rows = x_ref.shape[0]
    here = pl.ds(pl.multiple_of(block * ROWS_STEP, ROWS_STEP), ROWS_STEP)
    x = x_ref[here, :]
    table = pl.ds(pl.multiple_of(side * rows + block * ROWS_STEP, ROWS_STEP), ROWS_STEP)
    cosine, sine = cos_ref[table, :], sin_ref[table, :]
    for j in range(0 if side == 0 else 1, 3):
        full = dot(x, w_ref[j], NT)
        for pair in range(D // PAIR):
            part = full[:, pair * PAIR : (pair + 1) * PAIR]
            if j < 2:
                part = turn(part, cosine, sine)
            if j == 0:
                q_ref[pair, here, :] = (part * (0.125 * LOG2E)).astype(BF)
            elif j == 1:
                k_ref[side, pair, here, :] = part.astype(BF)
            else:
                v_ref[side, pair, here, :] = part.astype(BF)


def attend_step(side, place, bias, q_ref, k_ref, v_ref, mix_ref, stat_ref, ctx_ref, lse_ref):
    rows = q_ref.shape[1]
    blocks = rows // QUERY_STEP
    pair, block = place // blocks, lax.rem(place, blocks)
    here = pl.ds(pl.multiple_of(block * QUERY_STEP, QUERY_STEP), QUERY_STEP)
    q, k = q_ref[pair, here, :], k_ref[side, pair]
    keys = k.shape[0]
    v_cols = jnp.transpose(v_ref[side, pair].astype(F32)).astype(BF)
    outs = []
    for head in range(2):
        span = slice(head * HD, (head + 1) * HD)
        one, two = slice(head, head + 1), slice(2 + head, 3 + head)
        s = dot(k, pick(in_head(QUERY_STEP, head), q), NT) + bias
        peak = jnp.max(s, axis=0, keepdims=True)
        if side:
            before = stat_ref[pair, one, here]
            peak = jnp.maximum(peak, before)
        p = jnp.exp2(s - peak).astype(BF)
        v_aug = jnp.concatenate([v_cols[span], jnp.ones((16, keys), BF)], axis=0)
        mixed = dot(v_aug, p, NN)
        total = mixed[HD : HD + 1]
        mixed = mixed[:HD]
        if side:
            shrink = jnp.exp2(before - peak)
            total = total + shrink * stat_ref[pair, two, here]
            mixed = mixed + shrink * mix_ref[pair, span, here]
            outs.append(mixed / total)
            lse_ref[pair, one, here] = peak + jnp.log2(total)
        else:
            mix_ref[pair, span, here] = mixed
            stat_ref[pair, one, here] = peak
            stat_ref[pair, two, here] = total
    if side:
        columns = pl.ds(pl.multiple_of(pair * PAIR, PAIR), PAIR)
        ctx_ref[here, columns] = jnp.transpose(jnp.concatenate(outs, axis=0)).astype(BF)


def fill_tables(coarse_fine, first, cos_ref, sin_ref):
    rows = cos_ref.shape[0] // 2
    lane = lax.broadcasted_iota(jnp.int32, (64, PAIR), 1)
    sign = jnp.where(lane % 2 == 0, -1.0, 1.0)
    fine = pl.ds(SLOT // 64, 64)
    fine_cos, fine_sin = coarse_fine[0, fine, :], coarse_fine[1, fine, :]
    for side in range(2):
        start = first if side == 0 else rows - first
        for at in range(rows // 64):
            place = pl.ds(start // 64 + at, 1)
            cos_a, sin_a = coarse_fine[0, place, :], coarse_fine[1, place, :]
            target = slice(side * rows + at * 64, side * rows + (at + 1) * 64)
            cos_ref[target, :] = cos_a * fine_cos - sin_a * fine_sin
            sin_ref[target, :] = (sin_a * fine_cos + cos_a * fine_sin) * sign


def front_kernel(comm, *refs):
    step = pl.program_id(0)
    y, z, x, c = coords()
    if comm:
        ints, x_ref, angle_ref, qkv_shard, small_shard, out_shard, in_shard, down_shard = refs[:8]
        q_ref, k_ref, v_ref, ctx_ref, lse_ref, cos_ref, sin_ref, other_hbm = refs[8:16]
        qkv_full, small_full, out_full, in_full, down_full = refs[16:21]
        mix_ref, stat_ref, w_ref, other_ref, first_send, first_recv, send_sem, recv_sem, swap_sem, load_sem = refs[21:]
        first_begin, first_after, first_finish = gather_parts(
            "zyx", [1, 0], [qkv_shard, small_shard], [qkv_full, small_full], first_send, first_recv
        )
        rest_begin, rest_after, rest_finish = gather_parts(
            "yzx", [0, 0, 0], [out_shard, in_shard, down_shard], [out_full, in_full, down_full], send_sem, recv_sem
        )
        swap = pltpu.make_async_remote_copy(
            src_ref=x_ref, dst_ref=other_ref, send_sem=swap_sem.at[0], recv_sem=swap_sem.at[1],
            device_id=device(1 - y, z, x, c), device_id_type=MESH,
        )
        load = pltpu.make_async_copy(qkv_full, w_ref, load_sem.at[0])
        keep = pltpu.make_async_copy(other_ref, other_hbm, load_sem.at[1])
    else:
        ints, x_ref, angle_ref, w_ref, other_ref = refs[:5]
        q_ref, k_ref, v_ref, ctx_ref, lse_ref, cos_ref, sin_ref = refs[5:12]
        mix_ref, stat_ref = refs[12:]
    rows = x_ref.shape[0]
    projects, attends = front_plan(rows)

    @pl.when(step == 0)
    def _():
        if comm:
            greet()
            first_begin("zyx", True)
        fill_tables(angle_ref, y * rows, cos_ref, sin_ref)
        if comm:
            for places in (
                ((0, 1, 0), (1, 0, 0), (0, 0, 1), (0, 2, 0), (1, 1, 0), (0, 3, 0)),
                ((0, 1, 1), (1, 0, 1), (1, 2, 0), (1, 3, 0), (0, 2, 1), (1, 1, 1), (0, 3, 1), (1, 2, 1), (1, 3, 1)),
            ):
                for where in places:
                    for block in both_ways(*where):
                        first_after(block)
                if places[0] == (0, 1, 0):
                    rest_begin("y", False)
                    swap.start()
            rest_begin("zx", True)
            first_finish()
            load.start()
            load.wait()

    if comm:

        schedule = {
            1: [(1, 0, 0)], 4: [(1, 1, 0)], 8: [(0, 1, 0)], 12: [(1, 2, 0)], 14: [(1, 0, 1), (0, 0, 1)], 16: [(0, 2, 0)],
            18: [(1, 1, 1)], 19: [(1, 3, 0)], 23: [(0, 3, 0)], 24: [(0, 1, 1)], 27: [(1, 2, 1)], 28: [(1, 3, 1)],
            31: [(0, 2, 1)],
        }
        for at, places in schedule.items():

            @pl.when(step == at)
            def _(places=places):
                for where in places:
                    for block in both_ways(*where):
                        rest_after(block)

    begin = 1
    for side in range(2):
        source = x_ref if side == 0 else other_ref
        start = y * rows if side == 0 else (1 - y) * rows
        if side and comm:

            @pl.when(step == begin)
            def _():
                swap.wait()
                keep.start()


        @pl.when((step >= begin) & (step < begin + projects))
        def _(side=side, begin=begin, source=source):
            project_step(side, step - begin, source, w_ref, cos_ref, sin_ref, q_ref, k_ref, v_ref)

        begin += projects

        @pl.when((step >= begin) & (step < begin + attends))
        def _(side=side, begin=begin, start=start):
            place = start + lax.broadcasted_iota(jnp.int32, (rows, 1), 0)
            bias = jnp.where(place < ints[0], 0.0, NEG_LARGE)
            attend_step(side, step - begin, bias, q_ref, k_ref, v_ref, mix_ref, stat_ref, ctx_ref, lse_ref)

        begin += attends

    if comm:

        @pl.when(step == begin - 1)
        def _():
            for block in both_ways(0, 3, 1):
                rest_after(block)
            rest_finish()
            keep.wait()


def front(ints, x, angles, shards=None, gathered=None):
    rows = x.shape[0]
    pairs = D // PAIR
    projects, attends = front_plan(rows)
    heads = jax.ShapeDtypeStruct((2, pairs, rows, PAIR), BF)
    table = jax.ShapeDtypeStruct((2 * rows, PAIR), F32)
    narrow = jax.ShapeDtypeStruct((rows, D), BF)
    outs = [
        jax.ShapeDtypeStruct((pairs, rows, PAIR), BF), heads, heads, narrow,
        jax.ShapeDtypeStruct((pairs, 8, rows), F32), table, table,
    ]
    scratch = [pltpu.VMEM((pairs, PAIR, rows), F32), pltpu.VMEM((pairs, 8, rows), F32)]
    params = {}
    comm = shards is not None
    if comm:
        leads = [1, 0, 0, 0, 0]
        outs += [narrow] + full_shapes(shards, leads)
        scratch += [pltpu.VMEM((3, D, D), BF), pltpu.VMEM((rows, D), BF)] + gather_sems(2) + gather_sems(3)
        scratch += [pltpu.SemaphoreType.DMA((2,)), pltpu.SemaphoreType.DMA((2,))]
        params = dict(collective_id=0, has_side_effects=True)
    out = pl.pallas_call(
        functools.partial(front_kernel, comm),
        grid=(1 + 2 * (projects + attends),),
        in_specs=[SMEM, VMEM, VMEM] + ([HBM] * 5 if comm else [VMEM] * 2),
        out_specs=[VMEM] * 7 + ([HBM] * 6 if comm else []),
        out_shape=outs,
        scratch_shapes=scratch,
        compiler_params=pltpu.CompilerParams(vmem_limit_bytes=VMEM_LIMIT, **params),
        cost_estimate=pl.CostEstimate(
            flops=2 * rows * D * D * 5 + 16 * rows * SLOT * D,
            bytes_accessed=60 * rows * D,
            transcendentals=rows * SLOT * 12,
        ),
        name="front",
    )(ints, x, angles, *(shards if comm else gathered))
    if comm:
        return out
    return (*out, gathered[1], gathered[0])


def attend_back_kernel(side, leads, *refs):
    n = len(leads)
    ints, q_ref, k_ref, v_ref, do_ref, lse_ref, extra_ref, cosk_ref, sink_ref = refs[:9]
    used = 9
    second = side == 0
    if second:
        cosq_ref, sinq_ref, dq_in = refs[9:12]
        used = 12
    grads = refs[used : used + n]
    used += n
    dq_ref, dk_ref, dv_ref = refs[used : used + 3]
    used += 3
    if not second:
        delta_ref = refs[used]
        used += 1
    outs = refs[used : used + n]
    used += n
    if second:
        dq_cols = refs[used]
        used += 1
    else:
        dq_cols = dq_ref
    pair, step = pl.program_id(0), pl.program_id(1)
    if n:
        parts = scatter_parts(leads, grads, outs, refs[used : used + 7 * n], *refs[used + 7 * n :], (0, 1) if side else ORDER)
        start, cores, firsts, seconds, lasts, end = parts
        schedule = [
            [greet] + start, cores[:2], cores[2:], firsts[:1], firsts[1:2], firsts[2:3], firsts[3:] + seconds[:1],
            seconds[1:2], seconds[2:3], seconds[3:], lasts[:1], lasts[1:] + end,
        ]
        run_at(pair * 2 + step, schedule)
    rows, keys = q_ref.shape[1], k_ref.shape[2]
    part = min(256, rows)
    k, v = k_ref[0, 0], v_ref[0, 0]
    y = lax.axis_index("tensor")
    place = (y if second else 1 - y) * rows + step * keys + lax.broadcasted_iota(jnp.int32, (keys, 1), 0)
    bias = jnp.where(place < ints[0], 0.0, NEG_LARGE)
    k_cols = jnp.transpose(k.astype(F32)).astype(BF)

    @pl.when(step == 0)
    def _():
        if second:
            dq_cols[...] = dq_in[...]
        else:
            dq_cols[...] = jnp.zeros_like(dq_cols)
            both = jnp.transpose(do_ref[...].astype(F32) * extra_ref[...].astype(F32))
            delta_ref[0, 0:1, :] = jnp.sum(both[:HD], axis=0, keepdims=True)
            delta_ref[0, 1:2, :] = jnp.sum(both[HD:], axis=0, keepdims=True)

    delta = extra_ref if second else delta_ref
    dk = jnp.zeros((keys, PAIR), F32)
    dv = jnp.zeros((keys, PAIR), F32)
    for first in range(0, rows, part):
        here = slice(first, first + part)
        q, do = q_ref[0, here, :], do_ref[here, :]
        for head in range(2):
            mine = in_head(part, head)
            one = slice(head, head + 1)
            q_head, do_head = pick(mine, q), pick(mine, do)
            s = dot(k, q_head, NT)
            p = jnp.exp2(s - lse_ref[0, one, here] + bias)
            dp = dot(v, do_head, NT)
            ds = (p * (dp - delta[0, one, here])).astype(BF)
            dv += dot(p.astype(BF), do_head, NN)
            dk += dot(ds, q_head, NN)
            span = slice(head * HD, (head + 1) * HD)
            dq_cols[span, here] += dot(k_cols[span], ds, NN)
    dk_ref[...] = turn_back(dk * LN2, cosk_ref[...], sink_ref[...]).astype(BF)
    dv_ref[...] = dv.astype(BF)

    if second:

        @pl.when(step == pl.num_programs(1) - 1)
        def _():
            dq = jnp.transpose(dq_cols[...]) * 0.125
            dq_ref[...] = turn_back(dq, cosq_ref[...], sinq_ref[...]).astype(BF)


def attend_back(side, ints, q, k, v, do, lse, extra, tables, dq_part=None, grads=(), ident=None):
    pairs, rows = q.shape[:2]
    block = rows // 2
    n = len(grads)
    leads = [0] * n
    second = side == 0
    row_spec = pl.BlockSpec((rows, PAIR), lambda p, i: (0, p))
    key_spec = pl.BlockSpec((block, PAIR), lambda p, i: (i, p))
    k_spec = pl.BlockSpec((1, 1, block, PAIR), lambda p, i: (side, p, i, 0))
    stat_spec = pl.BlockSpec((1, 8, rows), lambda p, i: (p, 0, 0))
    q_table = pl.BlockSpec((rows, PAIR), lambda p, i: (0, 0))
    k_table = pl.BlockSpec((block, PAIR), lambda p, i: (2 * side + i, 0))
    col_spec = pl.BlockSpec((PAIR, rows), lambda p, i: (p, 0))
    narrow = jax.ShapeDtypeStruct((rows, D), BF)
    stats = jax.ShapeDtypeStruct((pairs, 8, rows), F32)
    cols = jax.ShapeDtypeStruct((D, rows), F32)
    views, sums, scratch = scatter_shapes(grads, leads) if n else ([], [], [])
    params = dict(collective_id=ident, has_side_effects=True) if n else {}
    return pl.pallas_call(
        functools.partial(attend_back_kernel, side, leads),
        grid=(pairs, 2),
        in_specs=[
            SMEM, pl.BlockSpec((1, rows, PAIR), lambda p, i: (p, 0, 0)), k_spec, k_spec, row_spec, stat_spec,
            stat_spec if second else row_spec, k_table, k_table,
        ]
        + ([q_table, q_table, col_spec] if second else [])
        + [VMEM] * n,
        out_specs=[row_spec if second else col_spec, key_spec, key_spec]
        + ([] if second else [stat_spec])
        + [VMEM] * n,
        out_shape=[narrow if second else cols, narrow, narrow] + ([] if second else [stats]) + sums,
        scratch_shapes=([pltpu.VMEM((PAIR, rows), F32)] if second else []) + scratch,
        compiler_params=pltpu.CompilerParams(vmem_limit_bytes=VMEM_LIMIT, **params),
        cost_estimate=pl.CostEstimate(
            flops=40 * rows * rows * D, bytes_accessed=16 * rows * D, transcendentals=rows * rows * 12
        ),
        name="attend_back",
    )(ints, q, k, v, do, lse, extra, *tables, *((*tables, dq_part) if second else ()), *views)


def norm(values):
    centre = values - jnp.mean(values, axis=-1, keepdims=True)
    inverse = lax.rsqrt(jnp.mean(centre * centre, axis=-1, keepdims=True) + EPSILON)
    return centre * inverse, inverse


def norm_back(grad_result, normed, inverse, gain):
    scaled = grad_result * gain
    return inverse * (
        scaled
        - jnp.mean(scaled, axis=-1, keepdims=True)
        - normed * jnp.mean(scaled * normed, axis=-1, keepdims=True)
    )


def middle_kernel(
    ints, scale_ref, ctx_ref, x_ref, teacher_ref, vec_ref, wo_ref, wi_ref, wd_ref,
    out_ref, act_ref, hin_ref, gb_ref, gp_ref, ga_ref, gc_ref, gr_ref, part_ref, slope_ref,
):
    block = ctx_ref.shape[0]
    chunk = 512
    hidden_units = wi_ref.shape[0]
    gain_one, bias_one, gain_two, bias_two = (vec_ref[i : i + 1, :] for i in range(4))
    attended = dot(ctx_ref[...], wo_ref[...], NN)
    normed_one, inverse_one = norm(x_ref[...].astype(F32) + attended)
    hidden = normed_one * gain_one + bias_one
    hidden_in = hidden.astype(BF)
    hin_ref[...] = hidden_in
    total = hidden
    for first in range(0, hidden_units, chunk):
        here = slice(first, first + chunk)
        pre = dot(hidden_in, wi_ref[here, :], NT)
        below = 0.5 + 0.5 * lax.erf(pre * INV_ROOT2)
        act = (pre * below).astype(BF)
        act_ref[:, here] = act
        slope_ref[:, here] = below + pre * jnp.exp(-0.5 * pre * pre) * INV_ROOT_TWO_PI
        total = total + dot(act, wd_ref[here, :], NN)
    normed_two, inverse_two = norm(total)
    final = normed_two * gain_two + bias_two
    out_ref[...] = final.astype(BF)
    place = ints[1] + pl.program_id(0) * block + lax.broadcasted_iota(jnp.int32, (block, D), 0)
    misfit = jnp.where(place < ints[0], final - teacher_ref[...].astype(F32), 0.0)
    grad_final = misfit * scale_ref[0]
    grad_mid = norm_back(grad_final, normed_two, inverse_two, gain_two)
    g_branch = grad_mid.astype(BF)
    gb_ref[...] = g_branch
    grad_hidden = grad_mid
    for first in range(0, hidden_units, chunk):
        here = slice(first, first + chunk)
        grad_act = dot(g_branch, wd_ref[here, :], NT)
        g_pre = (grad_act * slope_ref[:, here]).astype(BF)
        gp_ref[:, here] = g_pre
        grad_hidden = grad_hidden + dot(g_pre, wi_ref[here, :], NN)
    grad_res = norm_back(grad_hidden, normed_one, inverse_one, gain_one)
    gr_ref[...] = grad_res
    g_att = grad_res.astype(BF)
    ga_ref[...] = g_att
    gc_ref[...] = dot(g_att, wo_ref[...], NT).astype(BF)

    @pl.when(pl.program_id(0) == 0)
    def _():
        part_ref[...] = jnp.zeros_like(part_ref)

    for row, term in enumerate(
        (grad_hidden * normed_one, grad_hidden, grad_final * normed_two, grad_final, misfit * misfit)
    ):
        part_ref[row : row + 1, :] += jnp.sum(term, axis=0, keepdims=True)


def middle(ints, scale, context, x, teacher, vectors, out_full, in_full, down_full):
    rows = x.shape[0]
    block = 256
    hidden_units = in_full.shape[0]
    row = pl.BlockSpec((block, D), lambda i: (i, 0))
    wide = pl.BlockSpec((block, hidden_units), lambda i: (i, 0))

    def fixed(shape):
        return pl.BlockSpec(shape, lambda i: (0, 0), pipeline_mode=pl.Buffered(1))

    narrow_out = jax.ShapeDtypeStruct((rows, D), BF)
    wide_out = jax.ShapeDtypeStruct((rows, hidden_units), BF)
    return pl.pallas_call(
        middle_kernel,
        grid=(rows // block,),
        in_specs=[
            SMEM, SMEM, row, row, row, fixed((8, D)), fixed((D, D)), fixed((hidden_units, D)), fixed((hidden_units, D)),
        ],
        out_specs=[row, wide, row, row, wide, row, row, row, pl.BlockSpec((8, D), lambda i: (0, 0))],
        out_shape=[
            narrow_out, wide_out, narrow_out, narrow_out, wide_out, narrow_out, narrow_out,
            jax.ShapeDtypeStruct((rows, D), F32), jax.ShapeDtypeStruct((8, D), F32),
        ],
        scratch_shapes=[pltpu.VMEM((block, hidden_units), F32)],
        compiler_params=pltpu.CompilerParams(vmem_limit_bytes=VMEM_LIMIT),
        cost_estimate=pl.CostEstimate(
            flops=2 * rows * D * (2 * D + 4 * hidden_units),
            bytes_accessed=30 * rows * D + 4 * hidden_units * (rows + D),
            transcendentals=2 * rows * hidden_units,
        ),
        name="middle",
    )(ints, scale, context, x, teacher, vectors, out_full, in_full, down_full)


def on_device(
    layer_input, teacher, lengths, qkv_weight, out_weight, ln1_gain, ln1_bias,
    in_weight, down_weight, ln2_gain, ln2_bias,
):
    own_rows = layer_input.shape[0]
    data_size = lax.axis_size("dp")
    tensor_index = lax.axis_index("tensor")
    group_rows = own_rows * lax.axis_size("tensor")
    assert group_rows == SLOT and lax.axis_size("tensor") == 2 and lengths.shape[0] == 1
    own_comm = data_size == 16

    def gather(values, axis):
        return lax.all_gather(values, EVERYONE, axis=axis, tiled=True)

    def scatter(values, axis):
        return lax.psum_scatter(values, EVERYONE, scatter_dimension=axis, tiled=True)

    def swap(values):
        return lax.ppermute(values, "tensor", [(0, 1), (1, 0)])

    share = D // data_size
    norms = (ln1_gain, ln1_bias, ln2_gain, ln2_bias)
    angles = angle_tables()
    ints = jnp.stack([lengths[0], (tensor_index * own_rows).astype(jnp.int32)])
    if own_comm:
        small = jnp.pad(jnp.stack(norms).astype(F32), ((0, 4), (0, 128 - share)))
        small = jnp.where(lax.broadcasted_iota(jnp.int32, small.shape, 0) == 4, lengths[0].astype(F32), small)
        q, k, v, context, lse, cosine, sine, other_x, qkv_full, small_full, out_full, in_full, down_full = front(
            ints, layer_input, angles, [qkv_weight, small, out_weight, in_weight, down_weight]
        )
        small_full = small_full.reshape(2, data_size, 8, 128)[0]
        vectors = small_full[:, :, :share].transpose(1, 0, 2).reshape(8, D)
        valid_count = jnp.sum(small_full[:, 4, 0])
    else:
        vectors = jnp.stack([lax.all_gather(v, "dp", axis=0, tiled=True).astype(F32) for v in norms])
        vectors = jnp.concatenate([vectors, jnp.zeros((4, D), F32)])
        valid_count = lax.psum(jnp.sum(lengths).astype(F32), "dp")
        out_full, in_full, down_full = gather(out_weight, 0), gather(in_weight, 0), gather(down_weight, 0)
        q, k, v, context, lse, cosine, sine, other_x, qkv_full = front(
            ints, layer_input, angles, gathered=(gather(qkv_weight, 1), swap(layer_input))
        )

    grad_scale = group_rows * data_size * D // 4
    scale = (2.0 * grad_scale / (valid_count * D)).reshape(1)
    final, activated, hidden_in, g_branch, g_pre, g_att, g_context, grad_res, parts = middle(
        ints, scale, context, layer_input, teacher, vectors, out_full, in_full, down_full
    )

    def over_rows(left, right):
        return lax.dot_general(left, right, (((0,), (0,)), ((), ())), preferred_element_type=F32)

    grad_down_w = over_rows(activated, g_branch)
    grad_in_w = over_rows(g_pre, hidden_in)
    grad_out_w = over_rows(context, g_att)
    tables = (cosine, sine)
    if own_comm:
        sum_first, sum_second = [grad_down_w.astype(BF), grad_out_w.astype(BF)], [grad_in_w.astype(BF)]
    else:
        grad_down, grad_in, grad_out = scatter(grad_down_w, 0), scatter(grad_in_w, 0), scatter(grad_out_w, 0)
        sum_first, sum_second = [], []
    dq_part, dk_other, dv_other, delta, *sums = attend_back(
        1, ints, q, k, v, g_context, lse, context, tables, None, sum_first, 1
    )
    if own_comm:
        grad_down, grad_out = sums
    pass_on = dot(dk_other, qkv_full[1], NN) + dot(dv_other, qkv_full[2], NN)
    from_other = swap(pass_on.astype(BF))
    dq, dk_own, dv_own, *sums = attend_back(
        0, ints, q, k, v, g_context, lse, delta, tables, dq_part, sum_second, 2
    )
    if own_comm:
        grad_in = sums[0]
    if own_comm:
        grad_qkv, sums, input_grad = tail(
            dq, dk_own, dv_own, dk_other, dv_other, layer_input, other_x, qkv_full, grad_res, parts, 3
        )
        input_grad = input_grad + from_other.astype(F32)
    else:
        grad_qkv_w = [
            over_rows(dq, layer_input),
            over_rows(dk_own, layer_input) + over_rows(dk_other, other_x),
            over_rows(dv_own, layer_input) + over_rows(dv_other, other_x),
        ]
        grad_qkv = scatter(jnp.stack(grad_qkv_w), 1)
        sums = lax.psum(parts, ("dp", "tensor"))
        input_grad = (
            grad_res
            + dot(dq, qkv_full[0], NN)
            + dot(dk_own, qkv_full[1], NN)
            + dot(dv_own, qkv_full[2], NN)
            + from_other.astype(F32)
        )
    loss_value = jnp.sum(sums[4]) / (valid_count * D)
    own_norms = lax.dynamic_slice_in_dim(sums, lax.axis_index("dp") * share, share, 1)
    return (
        final, loss_value, input_grad, grad_qkv, grad_out,
        own_norms[0], own_norms[1], grad_in, grad_down, own_norms[2], own_norms[3],
    )


def solution(mesh):
    rows = P(("dp", "tensor"), None)
    shard = P(EVERYONE, None)
    in_specs = (
        rows, rows, P("dp"), P(None, EVERYONE, None), shard, P("dp"), P("dp"), shard, shard, P("dp"), P("dp"),
    )
    out_specs = (
        rows, P(), rows, P(None, EVERYONE, None), shard, P("dp"), P("dp"), shard, shard, P("dp"), P("dp"),
    )
    return jax.shard_map(on_device, mesh=mesh, in_specs=in_specs, out_specs=out_specs, check_vma=False)
```

```python
import functools

import jax
import jax.numpy as jnp
from jax import lax
from jax.experimental import pallas as pl
from jax.experimental.pallas import tpu as pltpu
from jax.sharding import PartitionSpec as P

D = 768
HD = 64
SLOT = 2048
PAIR = 2 * HD
EPSILON = 1e-05
NEG_LARGE = -1e30
ROPE_BASE = 10000.0
INV_ROOT2 = 0.7071067811865476
INV_ROOT_TWO_PI = 0.3989422804014327
LOG2E = 1.4426950408889634
LN2 = 0.6931471805599453
EVERYONE = ("tensor", "dp")

BF = jnp.bfloat16
F32 = jnp.float32
NT = (((1,), (1,)), ((), ()))
NN = (((1,), (0,)), ((), ()))
VMEM_LIMIT = 56 << 20
MESH = pl.DeviceIdType.MESH
HBM = pl.BlockSpec(memory_space=pl.ANY)
VMEM = pl.BlockSpec(memory_space=pltpu.VMEM)
SMEM = pl.BlockSpec(memory_space=pltpu.SMEM)


def dot(a, b, dims):
    return lax.dot_general(a, b, dims, preferred_element_type=F32)


GRID = (2, 4, 2, 2)
ORDER = (2, 1, 3, 0)


def coords():
    dp = lax.axis_index("dp")
    return lax.axis_index("tensor"), dp // 4, (dp // 2) % 2, dp % 2


def device(y, z, x, c):
    return (z * 4 + x * 2 + c, y)


def greet():
    y, z, x, c = coords()
    barrier = pltpu.get_barrier_semaphore()
    peers = [device(y, (z + dz) % 4, x, c) for dz in (1, 2, 3)]
    peers += [device(1 - y, z, x, c), device(y, z, 1 - x, c), device(y, z, x, 1 - c)]
    for peer in peers:
        pl.semaphore_signal(barrier, inc=1, device_id=peer, device_id_type=MESH)
    pl.semaphore_wait(barrier, len(peers))


def full_shapes(shards, leads):
    return [jax.ShapeDtypeStruct(s.shape[:l] + (32 * s.shape[l],) + s.shape[l + 1 :], s.dtype) for s, l in zip(shards, leads)]


DELTAS = (0, -1, 1, -2, 2, -3, 3)


def gather_sems(count):
    return [pltpu.SemaphoreType.DMA((count, 81)), pltpu.SemaphoreType.DMA((count, 32))]


def gather_parts(order, leads, shards, fulls, send_sem, recv_sem):
    y, z, x, c = coords()
    to_y, to_x, to_c = device(1 - y, z, x, c), device(y, z, 1 - x, c), device(y, z, x, 1 - c)
    own = (0, 0, 0)

    def arrives_over(block):
        apart = dict(zip("yzx", block))
        return [axis for axis in order if apart[axis]][-1]

    def plan(i):
        at = (slice(None),) * leads[i]
        shard, full = shards[i], fulls[i]
        count = shard.shape[leads[i]]

        def spot(block):
            dy, delta, dx = block
            place = (y if dy == 0 else 1 - y) * 16 + (z + delta) * 4 + (x if dx == 0 else 1 - x) * 2 + c
            return full.at[at + (pl.ds(pl.multiple_of(place * count, 8), count),)]

        def copy(block, send_slot, dy, dx, to, recv_base=0):
            place = z + block[1]
            return pltpu.make_async_remote_copy(
                src_ref=shard if block == own else spot(block),
                dst_ref=spot(block),
                send_sem=send_sem.at[i, send_slot + 8 * block[2] + 4 * block[0] + place],
                recv_sem=recv_sem.at[i, recv_base + 8 * dx + 4 * dy + place],
                device_id=to,
                device_id_type=MESH,
            )

        return dict(
            right=lambda b: copy(b, 0, b[0], b[2], device(y, z + 1, x, c)),
            left=lambda b: copy(b, 16, b[0], b[2], device(y, z - 1, x, c)),
            y=lambda b: copy(b, 32, 1, b[2], to_y),
            x=lambda b: copy(b, 48, b[0], 1, to_x),
            core=lambda b: copy(b, 64, b[0], b[2], to_c, 16),
            landed=lambda b: copy(b, 64, b[0], b[2], to_c),
            local=lambda: pltpu.make_async_copy(shard, spot(own), send_sem.at[i, 80]),
        )

    plans = [plan(i) for i in range(len(shards))]

    def when_there(block, action):
        if block[1] == 0:
            action()
        else:
            pl.when((z + block[1] >= 0) & (z + block[1] <= 3))(action)

    def onward(p, block, run, axes=None):
        axis = None if block == own else arrives_over(block)
        if axes is None:
            axes = order if axis is None else order[order.index(axis) + (axis != "z") :]
        for later in axes:
            if later != "z":
                run(p[later](block))
                continue
            if block[1] <= 0:
                pl.when(z < 3)(lambda: run(p["right"](block)))
            if block[1] >= 0:
                pl.when(z > 0)(lambda: run(p["left"](block)))

    def begin(axes, last):
        for p in plans:
            onward(p, own, lambda copy: copy.start(), axes)
            if last:
                p["core"](own).start()
                p["local"]().start()

    def after(block):
        def action():
            for p in plans:
                p["landed"](block).wait_recv()
                onward(p, block, lambda copy: copy.start())
                p["core"](block).start()

        when_there(block, action)

    def finish():
        def action_of(block):
            def action():
                for p in plans:
                    onward(p, block, lambda copy: copy.wait_send())
                    p["core"](block).wait()

            return action

        for dy in range(2):
            for dx in range(2):
                for delta in DELTAS:
                    when_there((dy, delta, dx), action_of((dy, delta, dx)))
        for p in plans:
            p["local"]().wait()

    return begin, after, finish


def both_ways(dy, distance, dx):
    return [(dy, delta, dx) for delta in ((0,) if distance == 0 else (-distance, distance))]


def scatter_shapes(grads, leads):
    views, outs, scratch = [], [], []
    for g, l in zip(grads, leads):
        head, rows, tail = g.shape[:l], g.shape[l] // 32, g.shape[l + 1 :]
        if not isinstance(g, jax.ShapeDtypeStruct):
            views.append(g.reshape(head + GRID + (rows,) + tail))
        shard = head + (rows,) + tail
        outs.append(jax.ShapeDtypeStruct(shard, F32))
        wide = pltpu.VMEM((4,) + head + (2, 2, rows) + tail, BF)
        pair = pltpu.VMEM((4,) + head + (2, rows) + tail, BF)
        one = pltpu.VMEM((4,) + shard, BF)
        scratch += [wide, pair, pair, one, one, one, one]
    count = len(grads)
    return views, outs, scratch + [pltpu.SemaphoreType.DMA((count, 16))] * 2


def scatter_parts(leads, grads, outs, bufs, send_sem, recv_sem, x_first):
    y, z, x, c = coords()
    n = len(leads)
    to_y, to_x, to_c = device(1 - y, z, x, c), device(y, z, 1 - x, c), device(y, z, x, 1 - c)

    def zz(dz):
        return (z + dz) % 4

    def lead(i):
        return (slice(None),) * leads[i]

    def copy(i, slot, source, target, to):
        return pltpu.make_async_remote_copy(
            src_ref=source, dst_ref=target, send_sem=send_sem.at[i, slot], recv_sem=recv_sem.at[i, slot],
            device_id=to, device_id_type=MESH,
        )

    def over_c(i, dz):
        return copy(i, dz, grads[i].at[lead(i) + (slice(None), zz(dz), slice(None), 1 - c)], bufs[7 * i].at[dz], to_c)

    def over_first(i, dz):
        to = to_x if dz in x_first else to_y
        return copy(i, 4 + dz, bufs[7 * i + 1].at[dz], bufs[7 * i + 2].at[dz], to)

    def over_second(i, dz):
        to = to_y if dz in x_first else to_x
        return copy(i, 8 + dz, bufs[7 * i + 3].at[dz], bufs[7 * i + 4].at[dz], to)

    def over_z(i, dz):
        return copy(i, 12 + dz, bufs[7 * i + 5].at[dz], bufs[7 * i + 6].at[dz], device(y, zz(dz), x, c))

    def chip_sum(i, dz, yy, xx):
        own = grads[i][lead(i) + (yy, zz(dz), xx, c)].astype(F32)
        return own + bufs[7 * i][(dz,) + lead(i) + (yy, xx)].astype(F32)

    def begin():
        for dz in ORDER:
            for i in range(n):
                over_c(i, dz).start()

    def after_c(dz):
        for i in range(n):
            over_c(i, dz).wait_recv()
            for far in range(2):
                yy, xx = ((1 - y if far else y), 1 - x) if dz in x_first else (1 - y, (1 - x if far else x))
                bufs[7 * i + 1][(dz,) + lead(i) + (far,)] = chip_sum(i, dz, yy, xx).astype(BF)
            over_first(i, dz).start()

    def after_first(dz):
        for i in range(n):
            over_first(i, dz).wait_recv()
            yy, xx = (1 - y, x) if dz in x_first else (y, 1 - x)
            total = chip_sum(i, dz, yy, xx) + bufs[7 * i + 2][(dz,) + lead(i) + (1,)].astype(F32)
            bufs[7 * i + 3][dz] = total.astype(BF)
            over_second(i, dz).start()

    def after_second(dz):
        for i in range(n):
            over_second(i, dz).wait_recv()
            total = chip_sum(i, dz, y, x) + bufs[7 * i + 2][(dz,) + lead(i) + (0,)].astype(F32)
            total = total + bufs[7 * i + 4][dz].astype(F32)
            if dz == 0:
                outs[i][...] = total
            else:
                bufs[7 * i + 5][dz] = total.astype(BF)
                over_z(i, dz).start()

    def after_z(dz):
        for i in range(n):
            over_z(i, dz).wait_recv()
            outs[i][...] += bufs[7 * i + 6][dz].astype(F32)

    def finish():
        for i in range(n):
            for dz in range(4):
                over_c(i, dz).wait_send()
                over_first(i, dz).wait_send()
                over_second(i, dz).wait_send()
                if dz:
                    over_z(i, dz).wait_send()

    stages = [[functools.partial(f, dz) for dz in ORDER] for f in (after_c, after_first, after_second)]
    last = [functools.partial(after_z, dz) for dz in ORDER[:3]]
    return [begin], stages[0], stages[1], stages[2], last, [finish]


def scatter_xzy_shapes(grads):
    views, outs, scratch = [], [], []
    for g in grads:
        rows = g.shape[0] // 32
        shard = (rows,) + g.shape[1:]
        views.append(g.reshape(GRID + shard))
        outs.append(jax.ShapeDtypeStruct(shard, F32))
        pair = pltpu.VMEM((4, 2) + shard, BF)
        scratch += [pltpu.VMEM((4, 2, 2) + shard, BF), pair, pair, pair, pair]
        scratch += [pltpu.VMEM((2,) + shard, F32), pltpu.VMEM((2,) + shard, BF)]
    count = len(grads)
    return views, outs, scratch + [pltpu.SemaphoreType.DMA((count, 16))] * 2


def scatter_xzy_parts(grads, outs, bufs, send_sem, recv_sem):
    y, z, x, c = coords()
    n = len(grads)

    def zz(dz):
        return (z + dz) % 4

    def copy(i, slot, source, target, to):
        return pltpu.make_async_remote_copy(
            src_ref=source, dst_ref=target, send_sem=send_sem.at[i, slot], recv_sem=recv_sem.at[i, slot],
            device_id=to, device_id_type=MESH,
        )

    def over_c(i, dz):
        source = grads[i].at[:, zz(dz), :, 1 - c]
        return copy(i, dz, source, bufs[7 * i].at[dz], device(y, z, x, 1 - c))

    def over_x(i, dz):
        return copy(i, 4 + dz, bufs[7 * i + 1].at[dz], bufs[7 * i + 2].at[dz], device(y, z, 1 - x, c))

    def over_z(i, dz):
        return copy(i, 8 + dz, bufs[7 * i + 3].at[dz], bufs[7 * i + 4].at[dz], device(y, zz(dz), x, c))

    def over_y(i):
        return copy(i, 12, bufs[7 * i + 6].at[0], bufs[7 * i + 6].at[1], device(1 - y, z, x, c))

    def chip_sum(i, dz, yy, xx):
        return grads[i][yy, zz(dz), xx, c].astype(F32) + bufs[7 * i][dz, yy, xx].astype(F32)

    def begin():
        for dz in ORDER:
            for i in range(n):
                over_c(i, dz).start()

    def after_c(dz):
        for i in range(n):
            over_c(i, dz).wait_recv()
            for yy in range(2):
                bufs[7 * i + 1][dz, yy] = chip_sum(i, dz, yy, 1 - x).astype(BF)
            over_x(i, dz).start()

    def after_x(dz):
        for i in range(n):
            over_x(i, dz).wait_recv()
            for yy in range(2):
                total = chip_sum(i, dz, yy, x) + bufs[7 * i + 2][dz, yy].astype(F32)
                if dz:
                    bufs[7 * i + 3][dz, yy] = total.astype(BF)
                else:
                    bufs[7 * i + 5][yy] = total
            if dz:
                over_z(i, dz).start()

    def after_z(dz):
        for i in range(n):
            over_z(i, dz).wait_recv()
            for yy in range(2):
                bufs[7 * i + 5][yy] += bufs[7 * i + 4][dz, yy].astype(F32)

    def send_y():
        for i in range(n):
            bufs[7 * i + 6][0] = bufs[7 * i + 5][1 - y].astype(BF)
            over_y(i).start()

    def finish():
        for i in range(n):
            over_y(i).wait()
            outs[i][...] = bufs[7 * i + 5][y] + bufs[7 * i + 6][1].astype(F32)
            for dz in range(4):
                over_c(i, dz).wait_send()
                over_x(i, dz).wait_send()
                if dz:
                    over_z(i, dz).wait_send()

    return begin, after_c, after_x, after_z, send_y, finish


def tail_kernel(
    dq_hbm, dk_hbm, dv_hbm, dk_far_hbm, dv_far_hbm, x_hbm, far_hbm, w_hbm, res_hbm, small_in,
    out_q, out_k, out_v, small_out, input_hbm,
    dq, dk, dv, dk_far, dv_far, x, far, w, res, load_sem, store_sem, grad_q, grad_k, grad_v, *refs,
):
    sums = (out_q, out_k, out_v)
    grads = (grad_q, grad_k, grad_v)
    per = 9
    hops, small_send, small_recv = refs[3 * per :]
    y, z, at_x, c = coords()
    rows = x.shape[0]
    pairs = (
        (dq_hbm, dq), (x_hbm, x), (dk_hbm, dk), (dk_far_hbm, dk_far), (far_hbm, far), (dv_hbm, dv),
        (dv_far_hbm, dv_far), (w_hbm, w), (res_hbm, res),
    )
    loads = [pltpu.make_async_copy(src, dst, load_sem.at[i]) for i, (src, dst) in enumerate(pairs)]
    for load in loads:
        load.start()
    greet()
    stages = [
        scatter_parts([0], grads[j : j + 1], sums[j : j + 1], refs[per * j : per * j + 7], *refs[per * j + 7 : per * j + 9], (0, 1))
        for j in range(3)
    ]

    def run(j, stage):
        for part in stages[j][stage]:
            part()

    def hop(source, target, to):
        return pltpu.make_async_remote_copy(
            src_ref=hops.at[source], dst_ref=hops.at[target], send_sem=small_send.at[target],
            recv_sem=small_recv.at[target], device_id=to, device_id_type=MESH,
        )

    hops[0] = small_in[...]
    over_c = hop(0, 1, device(y, z, at_x, 1 - c))
    over_c.start()

    def weight_grad(j, terms):
        half = D // 2
        for yy in range(2):
            cols = slice(yy * half, (yy + 1) * half)
            total = None
            for left, right in terms:
                part = dot(left[:, cols], right[...], (((0,), (0,)), ((), ())))
                total = part if total is None else total + part
            grads[j][yy] = total.astype(BF).reshape(grads[j].shape[1:])
        run(j, 0)

    def input_block(block):
        here = slice(block * ROWS_STEP, (block + 1) * ROWS_STEP)
        total = res[here, :]
        for j, left in enumerate((dq, dk, dv)):
            total = total + dot(left[here, :], w[j], NN)
        res[here, :] = total
        pltpu.make_async_copy(res.at[here], input_hbm.at[here], store_sem.at[block]).start()

    loads[0].wait()
    loads[1].wait()
    weight_grad(0, [(dq, x)])
    for i in (2, 3, 4):
        loads[i].wait()
    weight_grad(1, [(dk, x), (dk_far, far)])
    run(0, 1)
    loads[5].wait()
    loads[6].wait()
    weight_grad(2, [(dv, x), (dv_far, far)])
    run(1, 1)
    over_c.wait()
    hops[2] = hops[0] + hops[1]
    over_x = hop(2, 3, device(y, z, 1 - at_x, c))
    over_x.start()
    run(0, 2)
    run(2, 1)
    for i in (7, 8):
        loads[i].wait()
    input_block(0)
    over_x.wait()
    hops[4] = hops[2] + hops[3]
    over_y = hop(4, 5, device(1 - y, z, at_x, c))
    over_y.start()
    run(0, 3)
    run(1, 2)
    input_block(1)
    run(1, 3)
    run(2, 2)
    over_y.wait()
    hops[6] = hops[4] + hops[5]
    over_z = [hop(6, 6 + dz, device(y, (z + dz) % 4, at_x, c)) for dz in (1, 2, 3)]
    for one in over_z:
        one.start()
    input_block(2)
    run(2, 3)
    run(0, 4)
    input_block(3)
    run(1, 4)
    run(2, 4)
    for one in over_z:
        one.wait()
    small_out[...] = (hops[6] + hops[8]) + (hops[7] + hops[9])
    for j in range(3):
        run(j, 5)
    for block in range(rows // ROWS_STEP):
        here = slice(block * ROWS_STEP, (block + 1) * ROWS_STEP)
        pltpu.make_async_copy(res.at[here], input_hbm.at[here], store_sem.at[block]).wait()


def tail(dq, dk, dv, dk_far, dv_far, x, far, w, res, small, ident):
    rows = x.shape[0]
    share = D // 32
    grad = jax.ShapeDtypeStruct((D, D), BF)
    outs, scratch = [], []
    for _ in range(3):
        _, out, bufs = scatter_shapes([grad], [0])
        outs += out
        scratch += bufs
    narrow = pltpu.VMEM((rows, D), BF)
    out = pl.pallas_call(
        tail_kernel,
        in_specs=[HBM] * 9 + [VMEM],
        out_specs=[VMEM] * 4 + [HBM],
        out_shape=outs + [jax.ShapeDtypeStruct(small.shape, F32), jax.ShapeDtypeStruct((rows, D), F32)],
        scratch_shapes=[narrow] * 7
        + [pltpu.VMEM((3, D, D), BF), pltpu.VMEM((rows, D), F32)]
        + [pltpu.SemaphoreType.DMA((9,)), pltpu.SemaphoreType.DMA((rows // ROWS_STEP,))]
        + [pltpu.VMEM(GRID + (share, D), BF)] * 3
        + scratch
        + [pltpu.VMEM((10,) + small.shape, F32)]
        + [pltpu.SemaphoreType.DMA((10,))] * 2,
        compiler_params=pltpu.CompilerParams(collective_id=ident, has_side_effects=True, vmem_limit_bytes=VMEM_LIMIT),
        name="tail",
    )(dq, dk, dv, dk_far, dv_far, x, far, w, res, small)
    return jnp.stack(out[:3]), out[3], out[4]


def in_head(rows, head):
    lane = lax.broadcasted_iota(jnp.int32, (rows, PAIR), 1)
    return lane < HD if head == 0 else lane >= HD


def pick(mask, values):
    return jnp.where(mask, values, jnp.zeros_like(values))


def swap_pairs(values):
    even = lax.broadcasted_iota(jnp.int32, values.shape, 1) % 2 == 0
    return jnp.where(even, pltpu.roll(values, PAIR - 1, 1), pltpu.roll(values, 1, 1))


def turn(values, cosine, signed_sine):
    return values * cosine + swap_pairs(values) * signed_sine


def turn_back(values, cosine, signed_sine):
    return values * cosine - swap_pairs(values) * signed_sine


def angle_tables():
    lane = jnp.arange(PAIR)
    inverse_freq = ROPE_BASE ** (-2.0 * ((lane % HD) // 2).astype(F32) / HD)
    places = jnp.concatenate([jnp.arange(SLOT // 64) * 64, jnp.arange(64)]).astype(F32)
    angles = places[:, None] * inverse_freq[None, :]
    return jnp.stack([jnp.cos(angles), jnp.sin(angles)])


ROWS_STEP = 256
QUERY_STEP = 512


def front_plan(rows):
    project_steps = rows // ROWS_STEP
    attend_steps = (D // PAIR) * (rows // QUERY_STEP)
    return project_steps, attend_steps


def project_step(side, block, x_ref, w_ref, cos_ref, sin_ref, q_ref, k_ref, v_ref):
    rows = x_ref.shape[0]
    here = pl.ds(pl.multiple_of(block * ROWS_STEP, ROWS_STEP), ROWS_STEP)
    x = x_ref[here, :]
    table = pl.ds(pl.multiple_of(side * rows + block * ROWS_STEP, ROWS_STEP), ROWS_STEP)
    cosine, sine = cos_ref[table, :], sin_ref[table, :]
    for j in range(0 if side == 0 else 1, 3):
        full = dot(x, w_ref[j], NT)
        for pair in range(D // PAIR):
            part = full[:, pair * PAIR : (pair + 1) * PAIR]
            if j < 2:
                part = turn(part, cosine, sine)
            if j == 0:
                q_ref[pair, here, :] = (part * (0.125 * LOG2E)).astype(BF)
            elif j == 1:
                k_ref[side, pair, here, :] = part.astype(BF)
            else:
                v_ref[side, pair, here, :] = part.astype(BF)


def attend_step(side, place, bias, q_ref, k_ref, v_ref, mix_ref, stat_ref, ctx_ref, lse_ref):
    rows = q_ref.shape[1]
    blocks = rows // QUERY_STEP
    pair, block = place // blocks, lax.rem(place, blocks)
    here = pl.ds(pl.multiple_of(block * QUERY_STEP, QUERY_STEP), QUERY_STEP)
    q, k = q_ref[pair, here, :], k_ref[side, pair]
    keys = k.shape[0]
    v_cols = jnp.transpose(v_ref[side, pair].astype(F32)).astype(BF)
    outs = []
    for head in range(2):
        span = slice(head * HD, (head + 1) * HD)
        one, two = slice(head, head + 1), slice(2 + head, 3 + head)
        s = dot(k, pick(in_head(QUERY_STEP, head), q), NT) + bias
        peak = jnp.max(s, axis=0, keepdims=True)
        if side:
            before = stat_ref[pair, one, here]
            peak = jnp.maximum(peak, before)
        p = jnp.exp2(s - peak).astype(BF)
        v_aug = jnp.concatenate([v_cols[span], jnp.ones((16, keys), BF)], axis=0)
        mixed = dot(v_aug, p, NN)
        total = mixed[HD : HD + 1]
        mixed = mixed[:HD]
        if side:
            shrink = jnp.exp2(before - peak)
            total = total + shrink * stat_ref[pair, two, here]
            mixed = mixed + shrink * mix_ref[pair, span, here]
            outs.append(mixed / total)
            lse_ref[pair, one, here] = peak + jnp.log2(total)
        else:
            mix_ref[pair, span, here] = mixed
            stat_ref[pair, one, here] = peak
            stat_ref[pair, two, here] = total
    if side:
        columns = pl.ds(pl.multiple_of(pair * PAIR, PAIR), PAIR)
        ctx_ref[here, columns] = jnp.transpose(jnp.concatenate(outs, axis=0)).astype(BF)


def fill_tables(coarse_fine, first, cos_ref, sin_ref):
    rows = cos_ref.shape[0] // 2
    lane = lax.broadcasted_iota(jnp.int32, (64, PAIR), 1)
    sign = jnp.where(lane % 2 == 0, -1.0, 1.0)
    fine = pl.ds(SLOT // 64, 64)
    fine_cos, fine_sin = coarse_fine[0, fine, :], coarse_fine[1, fine, :]
    for side in range(2):
        start = first if side == 0 else rows - first
        for at in range(rows // 64):
            place = pl.ds(start // 64 + at, 1)
            cos_a, sin_a = coarse_fine[0, place, :], coarse_fine[1, place, :]
            target = slice(side * rows + at * 64, side * rows + (at + 1) * 64)
            cos_ref[target, :] = cos_a * fine_cos - sin_a * fine_sin
            sin_ref[target, :] = (sin_a * fine_cos + cos_a * fine_sin) * sign


def front_kernel(comm, *refs):
    step = pl.program_id(0)
    y, z, x, c = coords()
    if comm:
        ints, x_ref, angle_ref, qkv_shard, small_shard, out_shard, in_shard, down_shard = refs[:8]
        q_ref, k_ref, v_ref, ctx_ref, lse_ref, cos_ref, sin_ref, other_hbm = refs[8:16]
        qkv_full, small_full, out_full, in_full, down_full = refs[16:21]
        mix_ref, stat_ref, w_ref, other_ref, first_send, first_recv, send_sem, recv_sem, swap_sem, load_sem = refs[21:]
        first_begin, first_after, first_finish = gather_parts(
            "zyx", [1, 0], [qkv_shard, small_shard], [qkv_full, small_full], first_send, first_recv
        )
        rest_begin, rest_after, rest_finish = gather_parts(
            "yzx", [0, 0, 0], [out_shard, in_shard, down_shard], [out_full, in_full, down_full], send_sem, recv_sem
        )
        swap = pltpu.make_async_remote_copy(
            src_ref=x_ref, dst_ref=other_ref, send_sem=swap_sem.at[0], recv_sem=swap_sem.at[1],
            device_id=device(1 - y, z, x, c), device_id_type=MESH,
        )
        load = pltpu.make_async_copy(qkv_full, w_ref, load_sem.at[0])
        keep = pltpu.make_async_copy(other_ref, other_hbm, load_sem.at[1])
    else:
        ints, x_ref, angle_ref, w_ref, other_ref = refs[:5]
        q_ref, k_ref, v_ref, ctx_ref, lse_ref, cos_ref, sin_ref = refs[5:12]
        mix_ref, stat_ref = refs[12:]
    rows = x_ref.shape[0]
    projects, attends = front_plan(rows)

    @pl.when(step == 0)
    def _():
        if comm:
            greet()
            first_begin("zyx", True)
        fill_tables(angle_ref, y * rows, cos_ref, sin_ref)
        if comm:
            for places in (
                ((0, 1, 0), (1, 0, 0), (0, 0, 1), (0, 2, 0), (1, 1, 0), (0, 3, 0)),
                ((0, 1, 1), (1, 0, 1), (1, 2, 0), (1, 3, 0), (0, 2, 1), (1, 1, 1), (0, 3, 1), (1, 2, 1), (1, 3, 1)),
            ):
                for where in places:
                    for block in both_ways(*where):
                        first_after(block)
                if places[0] == (0, 1, 0):
                    rest_begin("y", False)
                    swap.start()
            rest_begin("zx", True)
            first_finish()
            load.start()
            load.wait()

    if comm:

        schedule = {
            1: [(1, 0, 0)], 4: [(1, 1, 0)], 8: [(0, 1, 0)], 12: [(1, 2, 0)], 14: [(1, 0, 1), (0, 0, 1)], 16: [(0, 2, 0)],
            18: [(1, 1, 1)], 19: [(1, 3, 0)], 23: [(0, 3, 0)], 24: [(0, 1, 1)], 27: [(1, 2, 1)], 28: [(1, 3, 1)],
            31: [(0, 2, 1)],
        }
        for at, places in schedule.items():

            @pl.when(step == at)
            def _(places=places):
                for where in places:
                    for block in both_ways(*where):
                        rest_after(block)

    begin = 1
    for side in range(2):
        source = x_ref if side == 0 else other_ref
        start = y * rows if side == 0 else (1 - y) * rows
        if side and comm:

            @pl.when(step == begin)
            def _():
                swap.wait()
                keep.start()


        @pl.when((step >= begin) & (step < begin + projects))
        def _(side=side, begin=begin, source=source):
            project_step(side, step - begin, source, w_ref, cos_ref, sin_ref, q_ref, k_ref, v_ref)

        begin += projects

        @pl.when((step >= begin) & (step < begin + attends))
        def _(side=side, begin=begin, start=start):
            place = start + lax.broadcasted_iota(jnp.int32, (rows, 1), 0)
            bias = jnp.where(place < ints[0], 0.0, NEG_LARGE)
            attend_step(side, step - begin, bias, q_ref, k_ref, v_ref, mix_ref, stat_ref, ctx_ref, lse_ref)

        begin += attends

    if comm:

        @pl.when(step == begin - 1)
        def _():
            for block in both_ways(0, 3, 1):
                rest_after(block)
            rest_finish()
            keep.wait()


def front(ints, x, angles, shards=None, gathered=None):
    rows = x.shape[0]
    pairs = D // PAIR
    projects, attends = front_plan(rows)
    heads = jax.ShapeDtypeStruct((2, pairs, rows, PAIR), BF)
    table = jax.ShapeDtypeStruct((2 * rows, PAIR), F32)
    narrow = jax.ShapeDtypeStruct((rows, D), BF)
    outs = [
        jax.ShapeDtypeStruct((pairs, rows, PAIR), BF), heads, heads, narrow,
        jax.ShapeDtypeStruct((pairs, 8, rows), F32), table, table,
    ]
    scratch = [pltpu.VMEM((pairs, PAIR, rows), F32), pltpu.VMEM((pairs, 8, rows), F32)]
    params = {}
    comm = shards is not None
    if comm:
        leads = [1, 0, 0, 0, 0]
        outs += [narrow] + full_shapes(shards, leads)
        scratch += [pltpu.VMEM((3, D, D), BF), pltpu.VMEM((rows, D), BF)] + gather_sems(2) + gather_sems(3)
        scratch += [pltpu.SemaphoreType.DMA((2,)), pltpu.SemaphoreType.DMA((2,))]
        params = dict(collective_id=0, has_side_effects=True)
    out = pl.pallas_call(
        functools.partial(front_kernel, comm),
        grid=(1 + 2 * (projects + attends),),
        in_specs=[SMEM, VMEM, VMEM] + ([HBM] * 5 if comm else [VMEM] * 2),
        out_specs=[VMEM] * 7 + ([HBM] * 6 if comm else []),
        out_shape=outs,
        scratch_shapes=scratch,
        compiler_params=pltpu.CompilerParams(vmem_limit_bytes=VMEM_LIMIT, **params),
        cost_estimate=pl.CostEstimate(
            flops=2 * rows * D * D * 5 + 16 * rows * SLOT * D,
            bytes_accessed=60 * rows * D,
            transcendentals=rows * SLOT * 12,
        ),
        name="front",
    )(ints, x, angles, *(shards if comm else gathered))
    if comm:
        return out
    return (*out, gathered[1], gathered[0])


def attend_back_kernel(side, leads, *refs):
    n = len(leads)
    ints, q_ref, k_ref, v_ref, do_ref, lse_ref, extra_ref, cosk_ref, sink_ref = refs[:9]
    used = 9
    second = side == 0
    if second:
        cosq_ref, sinq_ref, dq_in = refs[9:12]
        used = 12
    grads = refs[used : used + n]
    used += n
    dq_ref, dk_ref, dv_ref = refs[used : used + 3]
    used += 3
    if not second:
        delta_ref = refs[used]
        used += 1
    outs = refs[used : used + n]
    used += n
    if second:
        dq_cols = refs[used]
        used += 1
    else:
        dq_cols = dq_ref
    pair, step = pl.program_id(0), pl.program_id(1)
    schedule, last = {}, []
    if n and side:
        begin, cores, firsts, seconds, lasts, end = scatter_parts(
            leads, grads, outs, refs[used : used + 7 * n], *refs[used + 7 * n :], (0, 1)
        )
        schedule = {
            0: [greet] + begin, 5: cores[:2], 16: firsts[:2] + cores[2:], 22: seconds[:2], 32: firsts[2:],
            38: seconds[2:] + lasts[:1], 40: lasts[1:2],
        }
        last = lasts[2:] + end
    elif n:
        begin, after_c, after_x, after_z, send_y, end = scatter_xzy_parts(
            grads, outs, refs[used : used + 7 * n], *refs[used + 7 * n :]
        )
        schedule = {0: [greet, begin], 2: [functools.partial(after_c, 2)], 4: [functools.partial(after_c, dz) for dz in ORDER[1:]]}
        for slot, dz in zip((13, 21, 29, 37), ORDER):
            schedule[slot] = [functools.partial(after_x, dz)]
        schedule[38] = [functools.partial(after_z, dz) for dz in ORDER[:2]]
        schedule[46] = [functools.partial(after_z, ORDER[2]), send_y]
        last = [end]
    rows, keys = q_ref.shape[1], k_ref.shape[2]
    part = min(256, rows)
    k, v = k_ref[0, 0], v_ref[0, 0]
    y = lax.axis_index("tensor")
    place = (y if second else 1 - y) * rows + step * keys + lax.broadcasted_iota(jnp.int32, (keys, 1), 0)
    bias = jnp.where(place < ints[0], 0.0, NEG_LARGE)
    k_cols = jnp.transpose(k.astype(F32)).astype(BF)

    @pl.when(step == 0)
    def _():
        if second:
            dq_cols[...] = dq_in[...]
        else:
            dq_cols[...] = jnp.zeros_like(dq_cols)
            both = jnp.transpose(do_ref[...].astype(F32) * extra_ref[...].astype(F32))
            delta_ref[0, 0:1, :] = jnp.sum(both[:HD], axis=0, keepdims=True)
            delta_ref[0, 1:2, :] = jnp.sum(both[HD:], axis=0, keepdims=True)

    delta = extra_ref if second else delta_ref
    dk = jnp.zeros((keys, PAIR), F32)
    dv = jnp.zeros((keys, PAIR), F32)
    for at, first in enumerate(range(0, rows, part)):
        for slot, todo in schedule.items():
            if slot % 4 == at:

                @pl.when(pair * 2 + step == slot // 4)
                def _(todo=todo):
                    for one in todo:
                        one()

        here = slice(first, first + part)
        q, do = q_ref[0, here, :], do_ref[here, :]
        for head in range(2):
            mine = in_head(part, head)
            one = slice(head, head + 1)
            q_head, do_head = pick(mine, q), pick(mine, do)
            s = dot(k, q_head, NT)
            p = jnp.exp2(s - lse_ref[0, one, here] + bias)
            dp = dot(v, do_head, NT)
            ds = (p * (dp - delta[0, one, here])).astype(BF)
            dv += dot(p.astype(BF), do_head, NN)
            dk += dot(ds, q_head, NN)
            span = slice(head * HD, (head + 1) * HD)
            dq_cols[span, here] += dot(k_cols[span], ds, NN)
    dk_ref[...] = turn_back(dk * LN2, cosk_ref[...], sink_ref[...]).astype(BF)
    dv_ref[...] = dv.astype(BF)

    if second:

        @pl.when(step == pl.num_programs(1) - 1)
        def _():
            dq = jnp.transpose(dq_cols[...]) * 0.125
            dq_ref[...] = turn_back(dq, cosq_ref[...], sinq_ref[...]).astype(BF)

    if n:

        @pl.when(pair * 2 + step == 11)
        def _():
            for one in last:
                one()


def attend_back(side, ints, q, k, v, do, lse, extra, tables, dq_part=None, grads=(), ident=None):
    pairs, rows = q.shape[:2]
    block = rows // 2
    n = len(grads)
    leads = [0] * n
    second = side == 0
    row_spec = pl.BlockSpec((rows, PAIR), lambda p, i: (0, p))
    key_spec = pl.BlockSpec((block, PAIR), lambda p, i: (i, p))
    k_spec = pl.BlockSpec((1, 1, block, PAIR), lambda p, i: (side, p, i, 0))
    stat_spec = pl.BlockSpec((1, 8, rows), lambda p, i: (p, 0, 0))
    q_table = pl.BlockSpec((rows, PAIR), lambda p, i: (0, 0))
    k_table = pl.BlockSpec((block, PAIR), lambda p, i: (2 * side + i, 0))
    col_spec = pl.BlockSpec((PAIR, rows), lambda p, i: (p, 0))
    narrow = jax.ShapeDtypeStruct((rows, D), BF)
    stats = jax.ShapeDtypeStruct((pairs, 8, rows), F32)
    cols = jax.ShapeDtypeStruct((D, rows), F32)
    views, sums, scratch = [], [], []
    if n:
        views, sums, scratch = scatter_xzy_shapes(grads) if second else scatter_shapes(grads, leads)
    params = dict(collective_id=ident, has_side_effects=True) if n else {}
    return pl.pallas_call(
        functools.partial(attend_back_kernel, side, leads),
        grid=(pairs, 2),
        in_specs=[
            SMEM, pl.BlockSpec((1, rows, PAIR), lambda p, i: (p, 0, 0)), k_spec, k_spec, row_spec, stat_spec,
            stat_spec if second else row_spec, k_table, k_table,
        ]
        + ([q_table, q_table, col_spec] if second else [])
        + [VMEM] * n,
        out_specs=[row_spec if second else col_spec, key_spec, key_spec]
        + ([] if second else [stat_spec])
        + [VMEM] * n,
        out_shape=[narrow if second else cols, narrow, narrow] + ([] if second else [stats]) + sums,
        scratch_shapes=([pltpu.VMEM((PAIR, rows), F32)] if second else []) + scratch,
        compiler_params=pltpu.CompilerParams(vmem_limit_bytes=VMEM_LIMIT, **params),
        cost_estimate=pl.CostEstimate(
            flops=40 * rows * rows * D, bytes_accessed=16 * rows * D, transcendentals=rows * rows * 12
        ),
        name="attend_back",
    )(ints, q, k, v, do, lse, extra, *tables, *((*tables, dq_part) if second else ()), *views)


def norm(values):
    centre = values - jnp.mean(values, axis=-1, keepdims=True)
    inverse = lax.rsqrt(jnp.mean(centre * centre, axis=-1, keepdims=True) + EPSILON)
    return centre * inverse, inverse


def norm_back(grad_result, normed, inverse, gain):
    scaled = grad_result * gain
    return inverse * (
        scaled
        - jnp.mean(scaled, axis=-1, keepdims=True)
        - normed * jnp.mean(scaled * normed, axis=-1, keepdims=True)
    )


def middle_kernel(
    ints, scale_ref, ctx_ref, x_ref, teacher_ref, vec_ref, wo_ref, wi_ref, wd_ref,
    out_ref, act_ref, hin_ref, gb_ref, gp_ref, ga_ref, gc_ref, gr_ref, part_ref, slope_ref,
):
    block = ctx_ref.shape[0]
    chunk = 1024
    hidden_units = wi_ref.shape[0]
    gain_one, bias_one, gain_two, bias_two = (vec_ref[i : i + 1, :] for i in range(4))
    attended = dot(ctx_ref[...], wo_ref[...], NN)
    normed_one, inverse_one = norm(x_ref[...].astype(F32) + attended)
    hidden = normed_one * gain_one + bias_one
    hidden_in = hidden.astype(BF)
    hin_ref[...] = hidden_in
    total = hidden
    for first in range(0, hidden_units, chunk):
        here = slice(first, first + chunk)
        pre = dot(hidden_in, wi_ref[here, :], NT)
        below = 0.5 + 0.5 * lax.erf(pre * INV_ROOT2)
        act = (pre * below).astype(BF)
        act_ref[:, here] = act
        slope_ref[:, here] = below + pre * jnp.exp(-0.5 * pre * pre) * INV_ROOT_TWO_PI
        total = total + dot(act, wd_ref[here, :], NN)
    normed_two, inverse_two = norm(total)
    final = normed_two * gain_two + bias_two
    out_ref[...] = final.astype(BF)
    place = ints[1] + pl.program_id(0) * block + lax.broadcasted_iota(jnp.int32, (block, D), 0)
    misfit = jnp.where(place < ints[0], final - teacher_ref[...].astype(F32), 0.0)
    grad_final = misfit * scale_ref[0]
    grad_mid = norm_back(grad_final, normed_two, inverse_two, gain_two)
    g_branch = grad_mid.astype(BF)
    gb_ref[...] = g_branch
    grad_hidden = grad_mid
    for first in range(0, hidden_units, chunk):
        here = slice(first, first + chunk)
        grad_act = dot(g_branch, wd_ref[here, :], NT)
        g_pre = (grad_act * slope_ref[:, here]).astype(BF)
        gp_ref[:, here] = g_pre
        grad_hidden = grad_hidden + dot(g_pre, wi_ref[here, :], NN)
    grad_res = norm_back(grad_hidden, normed_one, inverse_one, gain_one)
    gr_ref[...] = grad_res
    g_att = grad_res.astype(BF)
    ga_ref[...] = g_att
    gc_ref[...] = dot(g_att, wo_ref[...], NT).astype(BF)

    @pl.when(pl.program_id(0) == 0)
    def _():
        part_ref[...] = jnp.zeros_like(part_ref)

    for row, term in enumerate(
        (grad_hidden * normed_one, grad_hidden, grad_final * normed_two, grad_final, misfit * misfit)
    ):
        part_ref[row : row + 1, :] += jnp.sum(term, axis=0, keepdims=True)


def middle(ints, scale, context, x, teacher, vectors, out_full, in_full, down_full):
    rows = x.shape[0]
    block = 256
    hidden_units = in_full.shape[0]
    row = pl.BlockSpec((block, D), lambda i: (i, 0))
    wide = pl.BlockSpec((block, hidden_units), lambda i: (i, 0))

    def fixed(shape):
        return pl.BlockSpec(shape, lambda i: (0, 0), pipeline_mode=pl.Buffered(1))

    narrow_out = jax.ShapeDtypeStruct((rows, D), BF)
    wide_out = jax.ShapeDtypeStruct((rows, hidden_units), BF)
    return pl.pallas_call(
        middle_kernel,
        grid=(rows // block,),
        in_specs=[
            SMEM, SMEM, row, row, row, fixed((8, D)), fixed((D, D)), fixed((hidden_units, D)), fixed((hidden_units, D)),
        ],
        out_specs=[row, wide, row, row, wide, row, row, row, pl.BlockSpec((8, D), lambda i: (0, 0))],
        out_shape=[
            narrow_out, wide_out, narrow_out, narrow_out, wide_out, narrow_out, narrow_out,
            jax.ShapeDtypeStruct((rows, D), F32), jax.ShapeDtypeStruct((8, D), F32),
        ],
        scratch_shapes=[pltpu.VMEM((block, hidden_units), F32)],
        compiler_params=pltpu.CompilerParams(vmem_limit_bytes=VMEM_LIMIT),
        cost_estimate=pl.CostEstimate(
            flops=2 * rows * D * (2 * D + 4 * hidden_units),
            bytes_accessed=30 * rows * D + 4 * hidden_units * (rows + D),
            transcendentals=2 * rows * hidden_units,
        ),
        name="middle",
    )(ints, scale, context, x, teacher, vectors, out_full, in_full, down_full)


def on_device(
    layer_input, teacher, lengths, qkv_weight, out_weight, ln1_gain, ln1_bias,
    in_weight, down_weight, ln2_gain, ln2_bias,
):
    own_rows = layer_input.shape[0]
    data_size = lax.axis_size("dp")
    tensor_index = lax.axis_index("tensor")
    group_rows = own_rows * lax.axis_size("tensor")
    assert group_rows == SLOT and lax.axis_size("tensor") == 2 and lengths.shape[0] == 1
    own_comm = data_size == 16

    def gather(values, axis):
        return lax.all_gather(values, EVERYONE, axis=axis, tiled=True)

    def scatter(values, axis):
        return lax.psum_scatter(values, EVERYONE, scatter_dimension=axis, tiled=True)

    def swap(values):
        return lax.ppermute(values, "tensor", [(0, 1), (1, 0)])

    share = D // data_size
    norms = (ln1_gain, ln1_bias, ln2_gain, ln2_bias)
    angles = angle_tables()
    ints = jnp.stack([lengths[0], (tensor_index * own_rows).astype(jnp.int32)])
    if own_comm:
        small = jnp.pad(jnp.stack(norms).astype(F32), ((0, 4), (0, 128 - share)))
        small = jnp.where(lax.broadcasted_iota(jnp.int32, small.shape, 0) == 4, lengths[0].astype(F32), small)
        q, k, v, context, lse, cosine, sine, other_x, qkv_full, small_full, out_full, in_full, down_full = front(
            ints, layer_input, angles, [qkv_weight, small, out_weight, in_weight, down_weight]
        )
        small_full = small_full.reshape(2, data_size, 8, 128)[0]
        vectors = small_full[:, :, :share].transpose(1, 0, 2).reshape(8, D)
        valid_count = jnp.sum(small_full[:, 4, 0])
    else:
        vectors = jnp.stack([lax.all_gather(v, "dp", axis=0, tiled=True).astype(F32) for v in norms])
        vectors = jnp.concatenate([vectors, jnp.zeros((4, D), F32)])
        valid_count = lax.psum(jnp.sum(lengths).astype(F32), "dp")
        out_full, in_full, down_full = gather(out_weight, 0), gather(in_weight, 0), gather(down_weight, 0)
        q, k, v, context, lse, cosine, sine, other_x, qkv_full = front(
            ints, layer_input, angles, gathered=(gather(qkv_weight, 1), swap(layer_input))
        )

    grad_scale = group_rows * data_size * D // 4
    scale = (2.0 * grad_scale / (valid_count * D)).reshape(1)
    final, activated, hidden_in, g_branch, g_pre, g_att, g_context, grad_res, parts = middle(
        ints, scale, context, layer_input, teacher, vectors, out_full, in_full, down_full
    )

    def over_rows(left, right):
        return lax.dot_general(left, right, (((0,), (0,)), ((), ())), preferred_element_type=F32)

    grad_down_w = over_rows(activated, g_branch)
    grad_in_w = over_rows(g_pre, hidden_in)
    grad_out_w = over_rows(context, g_att)
    tables = (cosine, sine)
    if own_comm:
        sum_first, sum_second = [grad_down_w.astype(BF), grad_out_w.astype(BF)], [grad_in_w.astype(BF)]
    else:
        grad_down, grad_in, grad_out = scatter(grad_down_w, 0), scatter(grad_in_w, 0), scatter(grad_out_w, 0)
        sum_first, sum_second = [], []
    dq_part, dk_other, dv_other, delta, *sums = attend_back(
        1, ints, q, k, v, g_context, lse, context, tables, None, sum_first, 1
    )
    if own_comm:
        grad_down, grad_out = sums
    pass_on = dot(dk_other, qkv_full[1], NN) + dot(dv_other, qkv_full[2], NN)
    from_other = swap(pass_on.astype(BF))
    dq, dk_own, dv_own, *sums = attend_back(
        0, ints, q, k, v, g_context, lse, delta, tables, dq_part, sum_second, 2
    )
    if own_comm:
        grad_in = sums[0]
    if own_comm:
        grad_qkv, sums, input_grad = tail(
            dq, dk_own, dv_own, dk_other, dv_other, layer_input, other_x, qkv_full, grad_res, parts, 3
        )
        input_grad = input_grad + from_other.astype(F32)
    else:
        grad_qkv_w = [
            over_rows(dq, layer_input),
            over_rows(dk_own, layer_input) + over_rows(dk_other, other_x),
            over_rows(dv_own, layer_input) + over_rows(dv_other, other_x),
        ]
        grad_qkv = scatter(jnp.stack(grad_qkv_w), 1)
        sums = lax.psum(parts, ("dp", "tensor"))
        input_grad = (
            grad_res
            + dot(dq, qkv_full[0], NN)
            + dot(dk_own, qkv_full[1], NN)
            + dot(dv_own, qkv_full[2], NN)
            + from_other.astype(F32)
        )
    loss_value = jnp.sum(sums[4]) / (valid_count * D)
    own_norms = lax.dynamic_slice_in_dim(sums, lax.axis_index("dp") * share, share, 1)
    return (
        final, loss_value, input_grad, grad_qkv, grad_out,
        own_norms[0], own_norms[1], grad_in, grad_down, own_norms[2], own_norms[3],
    )


def solution(mesh):
    rows = P(("dp", "tensor"), None)
    shard = P(EVERYONE, None)
    in_specs = (
        rows, rows, P("dp"), P(None, EVERYONE, None), shard, P("dp"), P("dp"), shard, shard, P("dp"), P("dp"),
    )
    out_specs = (
        rows, P(), rows, P(None, EVERYONE, None), shard, P("dp"), P("dp"), shard, shard, P("dp"), P("dp"),
    )
    return jax.shard_map(on_device, mesh=mesh, in_specs=in_specs, out_specs=out_specs, check_vma=False)
```

```python
import functools

import jax
import jax.numpy as jnp
from jax import lax
from jax.experimental import pallas as pl
from jax.experimental.pallas import tpu as pltpu
from jax.sharding import PartitionSpec as P

D = 768
HD = 64
SLOT = 2048
PAIR = 2 * HD
EPSILON = 1e-05
NEG_LARGE = -1e30
ROPE_BASE = 10000.0
INV_ROOT2 = 0.7071067811865476
INV_ROOT_TWO_PI = 0.3989422804014327
LOG2E = 1.4426950408889634
LN2 = 0.6931471805599453
EVERYONE = ("tensor", "dp")

BF = jnp.bfloat16
F32 = jnp.float32
NT = (((1,), (1,)), ((), ()))
NN = (((1,), (0,)), ((), ()))
VMEM_LIMIT = 56 << 20
MESH = pl.DeviceIdType.MESH
HBM = pl.BlockSpec(memory_space=pl.ANY)
VMEM = pl.BlockSpec(memory_space=pltpu.VMEM)
SMEM = pl.BlockSpec(memory_space=pltpu.SMEM)


def dot(a, b, dims):
    return lax.dot_general(a, b, dims, preferred_element_type=F32)


GRID = (2, 4, 2, 2)
ORDER = (2, 1, 3, 0)


def coords():
    dp = lax.axis_index("dp")
    return lax.axis_index("tensor"), dp // 4, (dp // 2) % 2, dp % 2


def device(y, z, x, c):
    return (z * 4 + x * 2 + c, y)


def greet():
    y, z, x, c = coords()
    barrier = pltpu.get_barrier_semaphore()
    peers = [device(y, (z + dz) % 4, x, c) for dz in (1, 2, 3)]
    peers += [device(1 - y, z, x, c), device(y, z, 1 - x, c), device(y, z, x, 1 - c)]
    for peer in peers:
        pl.semaphore_signal(barrier, inc=1, device_id=peer, device_id_type=MESH)
    pl.semaphore_wait(barrier, len(peers))


def full_shapes(shards, leads):
    return [jax.ShapeDtypeStruct(s.shape[:l] + (32 * s.shape[l],) + s.shape[l + 1 :], s.dtype) for s, l in zip(shards, leads)]


DELTAS = (0, -1, 1, -2, 2, -3, 3)


def gather_sems(count):
    return [pltpu.SemaphoreType.DMA((count, 81)), pltpu.SemaphoreType.DMA((count, 32))]


def gather_parts(order, leads, shards, fulls, send_sem, recv_sem):
    y, z, x, c = coords()
    to_y, to_x, to_c = device(1 - y, z, x, c), device(y, z, 1 - x, c), device(y, z, x, 1 - c)
    own = (0, 0, 0)

    def arrives_over(block):
        apart = dict(zip("yzx", block))
        return [axis for axis in order if apart[axis]][-1]

    def plan(i):
        at = (slice(None),) * leads[i]
        shard, full = shards[i], fulls[i]
        count = shard.shape[leads[i]]

        def spot(block):
            dy, delta, dx = block
            place = (y if dy == 0 else 1 - y) * 16 + (z + delta) * 4 + (x if dx == 0 else 1 - x) * 2 + c
            return full.at[at + (pl.ds(pl.multiple_of(place * count, 8), count),)]

        def copy(block, send_slot, dy, dx, to, recv_base=0):
            place = z + block[1]
            return pltpu.make_async_remote_copy(
                src_ref=shard if block == own else spot(block),
                dst_ref=spot(block),
                send_sem=send_sem.at[i, send_slot + 8 * block[2] + 4 * block[0] + place],
                recv_sem=recv_sem.at[i, recv_base + 8 * dx + 4 * dy + place],
                device_id=to,
                device_id_type=MESH,
            )

        return dict(
            right=lambda b: copy(b, 0, b[0], b[2], device(y, z + 1, x, c)),
            left=lambda b: copy(b, 16, b[0], b[2], device(y, z - 1, x, c)),
            y=lambda b: copy(b, 32, 1, b[2], to_y),
            x=lambda b: copy(b, 48, b[0], 1, to_x),
            core=lambda b: copy(b, 64, b[0], b[2], to_c, 16),
            landed=lambda b: copy(b, 64, b[0], b[2], to_c),
            local=lambda: pltpu.make_async_copy(shard, spot(own), send_sem.at[i, 80]),
        )

    plans = [plan(i) for i in range(len(shards))]

    def when_there(block, action):
        if block[1] == 0:
            action()
        else:
            pl.when((z + block[1] >= 0) & (z + block[1] <= 3))(action)

    def onward(p, block, run, axes=None):
        axis = None if block == own else arrives_over(block)
        if axes is None:
            axes = order if axis is None else order[order.index(axis) + (axis != "z") :]
        for later in axes:
            if later != "z":
                run(p[later](block))
                continue
            if block[1] <= 0:
                pl.when(z < 3)(lambda: run(p["right"](block)))
            if block[1] >= 0:
                pl.when(z > 0)(lambda: run(p["left"](block)))

    def begin(axes, last):
        for p in plans:
            onward(p, own, lambda copy: copy.start(), axes)
            if last:
                p["core"](own).start()
                p["local"]().start()

    def after(block):
        def action():
            for p in plans:
                p["landed"](block).wait_recv()
                onward(p, block, lambda copy: copy.start())
                p["core"](block).start()

        when_there(block, action)

    def finish():
        def action_of(block):
            def action():
                for p in plans:
                    onward(p, block, lambda copy: copy.wait_send())
                    p["core"](block).wait()

            return action

        for dy in range(2):
            for dx in range(2):
                for delta in DELTAS:
                    when_there((dy, delta, dx), action_of((dy, delta, dx)))
        for p in plans:
            p["local"]().wait()

    return begin, after, finish


def both_ways(dy, distance, dx):
    return [(dy, delta, dx) for delta in ((0,) if distance == 0 else (-distance, distance))]


def scatter_shapes(grads, leads):
    views, outs, scratch = [], [], []
    for g, l in zip(grads, leads):
        head, rows, tail = g.shape[:l], g.shape[l] // 32, g.shape[l + 1 :]
        if not isinstance(g, jax.ShapeDtypeStruct):
            views.append(g.reshape(head + GRID + (rows,) + tail))
        shard = head + (rows,) + tail
        outs.append(jax.ShapeDtypeStruct(shard, F32))
        wide = pltpu.VMEM((4,) + head + (2, 2, rows) + tail, BF)
        pair = pltpu.VMEM((4,) + head + (2, rows) + tail, BF)
        one = pltpu.VMEM((4,) + shard, BF)
        scratch += [wide, pair, pair, one, one, one, one]
    count = len(grads)
    return views, outs, scratch + [pltpu.SemaphoreType.DMA((count, 16))] * 2


def scatter_parts(leads, grads, outs, bufs, send_sem, recv_sem, x_first):
    y, z, x, c = coords()
    n = len(leads)
    to_y, to_x, to_c = device(1 - y, z, x, c), device(y, z, 1 - x, c), device(y, z, x, 1 - c)

    def zz(dz):
        return (z + dz) % 4

    def lead(i):
        return (slice(None),) * leads[i]

    def copy(i, slot, source, target, to):
        return pltpu.make_async_remote_copy(
            src_ref=source, dst_ref=target, send_sem=send_sem.at[i, slot], recv_sem=recv_sem.at[i, slot],
            device_id=to, device_id_type=MESH,
        )

    def over_c(i, dz):
        return copy(i, dz, grads[i].at[lead(i) + (slice(None), zz(dz), slice(None), 1 - c)], bufs[7 * i].at[dz], to_c)

    def over_first(i, dz):
        to = to_x if dz in x_first else to_y
        return copy(i, 4 + dz, bufs[7 * i + 1].at[dz], bufs[7 * i + 2].at[dz], to)

    def over_second(i, dz):
        to = to_y if dz in x_first else to_x
        return copy(i, 8 + dz, bufs[7 * i + 3].at[dz], bufs[7 * i + 4].at[dz], to)

    def over_z(i, dz):
        return copy(i, 12 + dz, bufs[7 * i + 5].at[dz], bufs[7 * i + 6].at[dz], device(y, zz(dz), x, c))

    def chip_sum(i, dz, yy, xx):
        own = grads[i][lead(i) + (yy, zz(dz), xx, c)].astype(F32)
        return own + bufs[7 * i][(dz,) + lead(i) + (yy, xx)].astype(F32)

    def begin():
        for dz in ORDER:
            for i in range(n):
                over_c(i, dz).start()

    def after_c(dz):
        for i in range(n):
            over_c(i, dz).wait_recv()
            for far in range(2):
                yy, xx = ((1 - y if far else y), 1 - x) if dz in x_first else (1 - y, (1 - x if far else x))
                bufs[7 * i + 1][(dz,) + lead(i) + (far,)] = chip_sum(i, dz, yy, xx).astype(BF)
            over_first(i, dz).start()

    def after_first(dz):
        for i in range(n):
            over_first(i, dz).wait_recv()
            yy, xx = (1 - y, x) if dz in x_first else (y, 1 - x)
            total = chip_sum(i, dz, yy, xx) + bufs[7 * i + 2][(dz,) + lead(i) + (1,)].astype(F32)
            bufs[7 * i + 3][dz] = total.astype(BF)
            over_second(i, dz).start()

    def after_second(dz):
        for i in range(n):
            over_second(i, dz).wait_recv()
            total = chip_sum(i, dz, y, x) + bufs[7 * i + 2][(dz,) + lead(i) + (0,)].astype(F32)
            total = total + bufs[7 * i + 4][dz].astype(F32)
            if dz == 0:
                outs[i][...] = total
            else:
                bufs[7 * i + 5][dz] = total.astype(BF)
                over_z(i, dz).start()

    def after_z(dz):
        for i in range(n):
            over_z(i, dz).wait_recv()
            outs[i][...] += bufs[7 * i + 6][dz].astype(F32)

    def finish():
        for i in range(n):
            for dz in range(4):
                over_c(i, dz).wait_send()
                over_first(i, dz).wait_send()
                over_second(i, dz).wait_send()
                if dz:
                    over_z(i, dz).wait_send()

    stages = [[functools.partial(f, dz) for dz in ORDER] for f in (after_c, after_first, after_second)]
    last = [functools.partial(after_z, dz) for dz in ORDER[:3]]
    return [begin], stages[0], stages[1], stages[2], last, [finish]


def scatter_xzy_shapes(grads):
    views, outs, scratch = [], [], []
    for g in grads:
        rows = g.shape[0] // 32
        shard = (rows,) + g.shape[1:]
        views.append(g.reshape(GRID + shard))
        outs.append(jax.ShapeDtypeStruct(shard, F32))
        pair = pltpu.VMEM((4, 2) + shard, BF)
        scratch += [pltpu.VMEM((4, 2, 2) + shard, BF), pair, pair, pair, pair]
        scratch += [pltpu.VMEM((2,) + shard, F32), pltpu.VMEM((2,) + shard, BF)]
    count = len(grads)
    return views, outs, scratch + [pltpu.SemaphoreType.DMA((count, 16))] * 2


def scatter_xzy_parts(grads, outs, bufs, send_sem, recv_sem):
    y, z, x, c = coords()
    n = len(grads)

    def zz(dz):
        return (z + dz) % 4

    def copy(i, slot, source, target, to):
        return pltpu.make_async_remote_copy(
            src_ref=source, dst_ref=target, send_sem=send_sem.at[i, slot], recv_sem=recv_sem.at[i, slot],
            device_id=to, device_id_type=MESH,
        )

    def over_c(i, dz):
        source = grads[i].at[:, zz(dz), :, 1 - c]
        return copy(i, dz, source, bufs[7 * i].at[dz], device(y, z, x, 1 - c))

    def over_x(i, dz):
        return copy(i, 4 + dz, bufs[7 * i + 1].at[dz], bufs[7 * i + 2].at[dz], device(y, z, 1 - x, c))

    def over_z(i, dz):
        return copy(i, 8 + dz, bufs[7 * i + 3].at[dz], bufs[7 * i + 4].at[dz], device(y, zz(dz), x, c))

    def over_y(i):
        return copy(i, 12, bufs[7 * i + 6].at[0], bufs[7 * i + 6].at[1], device(1 - y, z, x, c))

    def chip_sum(i, dz, yy, xx):
        return grads[i][yy, zz(dz), xx, c].astype(F32) + bufs[7 * i][dz, yy, xx].astype(F32)

    def begin():
        for dz in ORDER:
            for i in range(n):
                over_c(i, dz).start()

    def after_c(dz):
        for i in range(n):
            over_c(i, dz).wait_recv()
            for yy in range(2):
                bufs[7 * i + 1][dz, yy] = chip_sum(i, dz, yy, 1 - x).astype(BF)
            over_x(i, dz).start()

    def after_x(dz):
        for i in range(n):
            over_x(i, dz).wait_recv()
            for yy in range(2):
                total = chip_sum(i, dz, yy, x) + bufs[7 * i + 2][dz, yy].astype(F32)
                if dz:
                    bufs[7 * i + 3][dz, yy] = total.astype(BF)
                else:
                    bufs[7 * i + 5][yy] = total
            if dz:
                over_z(i, dz).start()

    def after_z(dz):
        for i in range(n):
            over_z(i, dz).wait_recv()
            for yy in range(2):
                bufs[7 * i + 5][yy] += bufs[7 * i + 4][dz, yy].astype(F32)

    def send_y():
        for i in range(n):
            bufs[7 * i + 6][0] = bufs[7 * i + 5][1 - y].astype(BF)
            over_y(i).start()

    def finish():
        for i in range(n):
            over_y(i).wait()
            outs[i][...] = bufs[7 * i + 5][y] + bufs[7 * i + 6][1].astype(F32)
            for dz in range(4):
                over_c(i, dz).wait_send()
                over_x(i, dz).wait_send()
                if dz:
                    over_z(i, dz).wait_send()

    return begin, after_c, after_x, after_z, send_y, finish


def tail_kernel(
    dq_hbm, dk_hbm, dv_hbm, dk_far_hbm, dv_far_hbm, x_hbm, far_hbm, w_hbm, res_hbm, small_in,
    out_q, out_k, out_v, small_out, input_hbm,
    dq, dk, dv, dk_far, dv_far, x, far, w, res, load_sem, store_sem, grad_q, grad_k, grad_v, *refs,
):
    sums = (out_q, out_k, out_v)
    grads = (grad_q, grad_k, grad_v)
    per = 9
    hops, small_send, small_recv = refs[3 * per :]
    y, z, at_x, c = coords()
    rows = x.shape[0]
    pairs = (
        (dq_hbm, dq), (x_hbm, x), (dk_hbm, dk), (dk_far_hbm, dk_far), (far_hbm, far), (dv_hbm, dv),
        (dv_far_hbm, dv_far), (w_hbm, w), (res_hbm, res),
    )
    loads = [pltpu.make_async_copy(src, dst, load_sem.at[i]) for i, (src, dst) in enumerate(pairs)]
    for load in loads:
        load.start()
    greet()
    stages = [
        scatter_parts([0], grads[j : j + 1], sums[j : j + 1], refs[per * j : per * j + 7], *refs[per * j + 7 : per * j + 9], (0, 1))
        for j in range(3)
    ]

    def run(j, stage):
        for part in stages[j][stage]:
            part()

    def hop(source, target, to):
        return pltpu.make_async_remote_copy(
            src_ref=hops.at[source], dst_ref=hops.at[target], send_sem=small_send.at[target],
            recv_sem=small_recv.at[target], device_id=to, device_id_type=MESH,
        )

    hops[0] = small_in[...]
    over_c = hop(0, 1, device(y, z, at_x, 1 - c))
    over_c.start()

    def weight_grad(j, terms):
        half = D // 2
        for yy in range(2):
            cols = slice(yy * half, (yy + 1) * half)
            total = None
            for left, right in terms:
                part = dot(left[:, cols], right[...], (((0,), (0,)), ((), ())))
                total = part if total is None else total + part
            grads[j][yy] = total.astype(BF).reshape(grads[j].shape[1:])
        run(j, 0)

    def input_block(block):
        here = slice(block * ROWS_STEP, (block + 1) * ROWS_STEP)
        total = res[here, :]
        for j, left in enumerate((dq, dk, dv)):
            total = total + dot(left[here, :], w[j], NN)
        res[here, :] = total
        pltpu.make_async_copy(res.at[here], input_hbm.at[here], store_sem.at[block]).start()

    loads[0].wait()
    loads[1].wait()
    weight_grad(0, [(dq, x)])
    for i in (2, 3, 4):
        loads[i].wait()
    weight_grad(1, [(dk, x), (dk_far, far)])
    run(0, 1)
    loads[5].wait()
    loads[6].wait()
    weight_grad(2, [(dv, x), (dv_far, far)])
    run(1, 1)
    over_c.wait()
    hops[2] = hops[0] + hops[1]
    over_x = hop(2, 3, device(y, z, 1 - at_x, c))
    over_x.start()
    run(0, 2)
    run(2, 1)
    for i in (7, 8):
        loads[i].wait()
    input_block(0)
    over_x.wait()
    hops[4] = hops[2] + hops[3]
    over_y = hop(4, 5, device(1 - y, z, at_x, c))
    over_y.start()
    run(0, 3)
    run(1, 2)
    input_block(1)
    run(1, 3)
    run(2, 2)
    over_y.wait()
    hops[6] = hops[4] + hops[5]
    over_z = [hop(6, 6 + dz, device(y, (z + dz) % 4, at_x, c)) for dz in (1, 2, 3)]
    for one in over_z:
        one.start()
    input_block(2)
    run(2, 3)
    run(0, 4)
    input_block(3)
    run(1, 4)
    run(2, 4)
    for one in over_z:
        one.wait()
    small_out[...] = (hops[6] + hops[8]) + (hops[7] + hops[9])
    for j in range(3):
        run(j, 5)
    for block in range(rows // ROWS_STEP):
        here = slice(block * ROWS_STEP, (block + 1) * ROWS_STEP)
        pltpu.make_async_copy(res.at[here], input_hbm.at[here], store_sem.at[block]).wait()


def tail(dq, dk, dv, dk_far, dv_far, x, far, w, res, small, ident):
    rows = x.shape[0]
    share = D // 32
    grad = jax.ShapeDtypeStruct((D, D), BF)
    outs, scratch = [], []
    for _ in range(3):
        _, out, bufs = scatter_shapes([grad], [0])
        outs += out
        scratch += bufs
    narrow = pltpu.VMEM((rows, D), BF)
    out = pl.pallas_call(
        tail_kernel,
        in_specs=[HBM] * 9 + [VMEM],
        out_specs=[VMEM] * 4 + [HBM],
        out_shape=outs + [jax.ShapeDtypeStruct(small.shape, F32), jax.ShapeDtypeStruct((rows, D), F32)],
        scratch_shapes=[narrow] * 7
        + [pltpu.VMEM((3, D, D), BF), pltpu.VMEM((rows, D), F32)]
        + [pltpu.SemaphoreType.DMA((9,)), pltpu.SemaphoreType.DMA((rows // ROWS_STEP,))]
        + [pltpu.VMEM(GRID + (share, D), BF)] * 3
        + scratch
        + [pltpu.VMEM((10,) + small.shape, F32)]
        + [pltpu.SemaphoreType.DMA((10,))] * 2,
        compiler_params=pltpu.CompilerParams(collective_id=ident, has_side_effects=True, vmem_limit_bytes=VMEM_LIMIT),
        name="tail",
    )(dq, dk, dv, dk_far, dv_far, x, far, w, res, small)
    return jnp.stack(out[:3]), out[3], out[4]


def in_head(rows, head):
    lane = lax.broadcasted_iota(jnp.int32, (rows, PAIR), 1)
    return lane < HD if head == 0 else lane >= HD


def pick(mask, values):
    return jnp.where(mask, values, jnp.zeros_like(values))


def swap_pairs(values):
    even = lax.broadcasted_iota(jnp.int32, values.shape, 1) % 2 == 0
    return jnp.where(even, pltpu.roll(values, PAIR - 1, 1), pltpu.roll(values, 1, 1))


def turn(values, cosine, signed_sine):
    return values * cosine + swap_pairs(values) * signed_sine


def turn_back(values, cosine, signed_sine):
    return values * cosine - swap_pairs(values) * signed_sine


def angle_tables():
    lane = jnp.arange(PAIR)
    inverse_freq = ROPE_BASE ** (-2.0 * ((lane % HD) // 2).astype(F32) / HD)
    places = jnp.concatenate([jnp.arange(SLOT // 64) * 64, jnp.arange(64)]).astype(F32)
    angles = places[:, None] * inverse_freq[None, :]
    return jnp.stack([jnp.cos(angles), jnp.sin(angles)])


ROWS_STEP = 256
QUERY_STEP = 1024


def front_plan(rows):
    project_steps = rows // ROWS_STEP
    attend_steps = (D // PAIR) * (rows // QUERY_STEP)
    return project_steps, attend_steps


def project_step(side, block, x_ref, w_ref, cos_ref, sin_ref, q_ref, k_ref, v_ref):
    rows = x_ref.shape[0]
    here = pl.ds(pl.multiple_of(block * ROWS_STEP, ROWS_STEP), ROWS_STEP)
    x = x_ref[here, :]
    table = pl.ds(pl.multiple_of(side * rows + block * ROWS_STEP, ROWS_STEP), ROWS_STEP)
    cosine, sine = cos_ref[table, :], sin_ref[table, :]
    for j in range(0 if side == 0 else 1, 3):
        full = dot(x, w_ref[j], NT)
        for pair in range(D // PAIR):
            part = full[:, pair * PAIR : (pair + 1) * PAIR]
            if j < 2:
                part = turn(part, cosine, sine)
            if j == 0:
                q_ref[pair, here, :] = (part * (0.125 * LOG2E)).astype(BF)
            elif j == 1:
                k_ref[side, pair, here, :] = part.astype(BF)
            else:
                v_ref[side, pair, here, :] = part.astype(BF)


def attend_step(side, place, bias, q_ref, k_ref, v_ref, mix_ref, stat_ref, ctx_ref, lse_ref):
    rows = q_ref.shape[1]
    blocks = rows // QUERY_STEP
    pair, block = place // blocks, lax.rem(place, blocks)
    here = pl.ds(pl.multiple_of(block * QUERY_STEP, QUERY_STEP), QUERY_STEP)
    q, k = q_ref[pair, here, :], k_ref[side, pair]
    keys = k.shape[0]
    v_cols = jnp.transpose(v_ref[side, pair].astype(F32)).astype(BF)
    scores = [dot(k, pick(in_head(QUERY_STEP, head), q), NT) + bias for head in range(2)]
    outs = []
    for head, s in enumerate(scores):
        span = slice(head * HD, (head + 1) * HD)
        one, two = slice(head, head + 1), slice(2 + head, 3 + head)
        peak = jnp.max(s, axis=0, keepdims=True)
        if side:
            before = stat_ref[pair, one, here]
            peak = jnp.maximum(peak, before)
        p = jnp.exp2(s - peak).astype(BF)
        v_aug = jnp.concatenate([v_cols[span], jnp.ones((16, keys), BF)], axis=0)
        mixed = dot(v_aug, p, NN)
        total = mixed[HD : HD + 1]
        mixed = mixed[:HD]
        if side:
            shrink = jnp.exp2(before - peak)
            total = total + shrink * stat_ref[pair, two, here]
            mixed = mixed + shrink * mix_ref[pair, span, here]
            outs.append(mixed / total)
            lse_ref[pair, one, here] = peak + jnp.log2(total)
        else:
            mix_ref[pair, span, here] = mixed
            stat_ref[pair, one, here] = peak
            stat_ref[pair, two, here] = total
    if side:
        columns = pl.ds(pl.multiple_of(pair * PAIR, PAIR), PAIR)
        ctx_ref[here, columns] = jnp.transpose(jnp.concatenate(outs, axis=0)).astype(BF)


def fill_tables(coarse_fine, first, cos_ref, sin_ref):
    rows = cos_ref.shape[0] // 2
    lane = lax.broadcasted_iota(jnp.int32, (64, PAIR), 1)
    sign = jnp.where(lane % 2 == 0, -1.0, 1.0)
    fine = pl.ds(SLOT // 64, 64)
    fine_cos, fine_sin = coarse_fine[0, fine, :], coarse_fine[1, fine, :]
    for side in range(2):
        start = first if side == 0 else rows - first
        for at in range(rows // 64):
            place = pl.ds(start // 64 + at, 1)
            cos_a, sin_a = coarse_fine[0, place, :], coarse_fine[1, place, :]
            target = slice(side * rows + at * 64, side * rows + (at + 1) * 64)
            cos_ref[target, :] = cos_a * fine_cos - sin_a * fine_sin
            sin_ref[target, :] = (sin_a * fine_cos + cos_a * fine_sin) * sign


def front_kernel(comm, *refs):
    step = pl.program_id(0)
    y, z, x, c = coords()
    if comm:
        ints, x_ref, angle_ref, qkv_shard, small_shard, out_shard, in_shard, down_shard = refs[:8]
        q_ref, k_ref, v_ref, ctx_ref, lse_ref, cos_ref, sin_ref, other_hbm = refs[8:16]
        qkv_full, small_full, out_full, in_full, down_full = refs[16:21]
        mix_ref, stat_ref, w_ref, other_ref, first_send, first_recv, send_sem, recv_sem, swap_sem, load_sem = refs[21:]
        first_begin, first_after, first_finish = gather_parts(
            "zyx", [1, 0], [qkv_shard, small_shard], [qkv_full, small_full], first_send, first_recv
        )
        rest_begin, rest_after, rest_finish = gather_parts(
            "yzx", [0, 0, 0], [out_shard, in_shard, down_shard], [out_full, in_full, down_full], send_sem, recv_sem
        )
        swap = pltpu.make_async_remote_copy(
            src_ref=x_ref, dst_ref=other_ref, send_sem=swap_sem.at[0], recv_sem=swap_sem.at[1],
            device_id=device(1 - y, z, x, c), device_id_type=MESH,
        )
        load = pltpu.make_async_copy(qkv_full, w_ref, load_sem.at[0])
        keep = pltpu.make_async_copy(other_ref, other_hbm, load_sem.at[1])
    else:
        ints, x_ref, angle_ref, w_ref, other_ref = refs[:5]
        q_ref, k_ref, v_ref, ctx_ref, lse_ref, cos_ref, sin_ref = refs[5:12]
        mix_ref, stat_ref = refs[12:]
    rows = x_ref.shape[0]
    projects, attends = front_plan(rows)

    @pl.when(step == 0)
    def _():
        if comm:
            greet()
            first_begin("zyx", True)
        fill_tables(angle_ref, y * rows, cos_ref, sin_ref)
        if comm:
            for places in (
                ((0, 1, 0), (1, 0, 0), (0, 0, 1), (0, 2, 0), (1, 1, 0), (0, 3, 0)),
                ((0, 1, 1), (1, 0, 1), (1, 2, 0), (1, 3, 0), (0, 2, 1), (1, 1, 1), (0, 3, 1), (1, 2, 1), (1, 3, 1)),
            ):
                for where in places:
                    for block in both_ways(*where):
                        first_after(block)
                if places[0] == (0, 1, 0):
                    rest_begin("y", False)
                    swap.start()
            rest_begin("zx", True)
            first_finish()
            load.start()
            load.wait()

    if comm:

        schedule = {
            1: [(1, 0, 0)], 4: [(1, 1, 0)], 7: [(0, 1, 0)], 9: [(1, 2, 0)], 10: [(1, 0, 1), (0, 0, 1)], 11: [(0, 2, 0)],
            12: [(1, 1, 1)], 13: [(1, 3, 0)], 16: [(0, 3, 0)], 17: [(0, 1, 1)], 19: [(1, 2, 1), (1, 3, 1)],
        }
        for at, places in schedule.items():

            @pl.when(step == at)
            def _(places=places):
                for where in places:
                    for block in both_ways(*where):
                        rest_after(block)

    begin = 1
    for side in range(2):
        source = x_ref if side == 0 else other_ref
        start = y * rows if side == 0 else (1 - y) * rows
        if side and comm:

            @pl.when(step == begin)
            def _():
                swap.wait()
                keep.start()


        @pl.when((step >= begin) & (step < begin + projects))
        def _(side=side, begin=begin, source=source):
            project_step(side, step - begin, source, w_ref, cos_ref, sin_ref, q_ref, k_ref, v_ref)

        begin += projects

        @pl.when((step >= begin) & (step < begin + attends))
        def _(side=side, begin=begin, start=start):
            place = start + lax.broadcasted_iota(jnp.int32, (rows, 1), 0)
            bias = jnp.where(place < ints[0], 0.0, NEG_LARGE)
            attend_step(side, step - begin, bias, q_ref, k_ref, v_ref, mix_ref, stat_ref, ctx_ref, lse_ref)

        begin += attends

    if comm:

        @pl.when(step == begin - 1)
        def _():
            for block in both_ways(0, 2, 1) + both_ways(0, 3, 1):
                rest_after(block)
            rest_finish()
            keep.wait()


def front(ints, x, angles, shards=None, gathered=None):
    rows = x.shape[0]
    pairs = D // PAIR
    projects, attends = front_plan(rows)
    heads = jax.ShapeDtypeStruct((2, pairs, rows, PAIR), BF)
    table = jax.ShapeDtypeStruct((2 * rows, PAIR), F32)
    narrow = jax.ShapeDtypeStruct((rows, D), BF)
    outs = [
        jax.ShapeDtypeStruct((pairs, rows, PAIR), BF), heads, heads, narrow,
        jax.ShapeDtypeStruct((pairs, 8, rows), F32), table, table,
    ]
    scratch = [pltpu.VMEM((pairs, PAIR, rows), F32), pltpu.VMEM((pairs, 8, rows), F32)]
    params = {}
    comm = shards is not None
    if comm:
        leads = [1, 0, 0, 0, 0]
        outs += [narrow] + full_shapes(shards, leads)
        scratch += [pltpu.VMEM((3, D, D), BF), pltpu.VMEM((rows, D), BF)] + gather_sems(2) + gather_sems(3)
        scratch += [pltpu.SemaphoreType.DMA((2,)), pltpu.SemaphoreType.DMA((2,))]
        params = dict(collective_id=0, has_side_effects=True)
    out = pl.pallas_call(
        functools.partial(front_kernel, comm),
        grid=(1 + 2 * (projects + attends),),
        in_specs=[SMEM, VMEM, VMEM] + ([HBM] * 5 if comm else [VMEM] * 2),
        out_specs=[VMEM] * 7 + ([HBM] * 6 if comm else []),
        out_shape=outs,
        scratch_shapes=scratch,
        compiler_params=pltpu.CompilerParams(vmem_limit_bytes=VMEM_LIMIT, **params),
        cost_estimate=pl.CostEstimate(
            flops=2 * rows * D * D * 5 + 16 * rows * SLOT * D,
            bytes_accessed=60 * rows * D,
            transcendentals=rows * SLOT * 12,
        ),
        name="front",
    )(ints, x, angles, *(shards if comm else gathered))
    if comm:
        return out
    return (*out, gathered[1], gathered[0])


def attend_back_kernel(side, leads, *refs):
    n = len(leads)
    ints, q_ref, k_ref, v_ref, do_ref, lse_ref, extra_ref, cosk_ref, sink_ref = refs[:9]
    used = 9
    second = side == 0
    if second:
        cosq_ref, sinq_ref, dq_in = refs[9:12]
        used = 12
    grads = refs[used : used + n]
    used += n
    dq_ref, dk_ref, dv_ref = refs[used : used + 3]
    used += 3
    if not second:
        delta_ref = refs[used]
        used += 1
    outs = refs[used : used + n]
    used += n
    if second:
        dq_cols = refs[used]
        used += 1
    else:
        dq_cols = dq_ref
    pair = pl.program_id(0)
    schedule, last = {}, []
    if n and side:
        begin, cores, firsts, seconds, lasts, end = scatter_parts(
            leads, grads, outs, refs[used : used + 7 * n], *refs[used + 7 * n :], (0, 1)
        )
        schedule = {
            0: [greet] + begin, 3: cores[:2], 10: firsts[:2] + cores[2:], 14: seconds[:2], 20: firsts[2:],
            23: seconds[2:] + lasts[:1],
        }
        last = lasts[1:] + end
    elif n:
        begin, after_c, after_x, after_z, send_y, end = scatter_xzy_parts(
            grads, outs, refs[used : used + 7 * n], *refs[used + 7 * n :]
        )
        schedule = {0: [greet, begin], 2: [functools.partial(after_c, 2)], 3: [functools.partial(after_c, dz) for dz in ORDER[1:]]}
        for slot, dz in zip((8, 13, 18, 22), ORDER):
            schedule[slot] = [functools.partial(after_x, dz)]
        schedule[23] = [functools.partial(after_z, dz) for dz in ORDER[:2]]
        last = [functools.partial(after_z, ORDER[2]), send_y, end]
    rows, keys = q_ref.shape[1], k_ref.shape[2]
    part = 256
    k, v = k_ref[0, 0], v_ref[0, 0]
    y = lax.axis_index("tensor")
    place = (y if second else 1 - y) * rows + lax.broadcasted_iota(jnp.int32, (keys, 1), 0)
    bias = jnp.where(place < ints[0], 0.0, NEG_LARGE)
    k_cols = jnp.transpose(k.astype(F32)).astype(BF)
    if not second:
        both = jnp.transpose(do_ref[...].astype(F32) * extra_ref[...].astype(F32))
        delta_ref[0, 0:1, :] = jnp.sum(both[:HD], axis=0, keepdims=True)
        delta_ref[0, 1:2, :] = jnp.sum(both[HD:], axis=0, keepdims=True)
    delta = extra_ref if second else delta_ref
    dk = jnp.zeros((keys, PAIR), F32)
    dv = jnp.zeros((keys, PAIR), F32)
    for at, first in enumerate(range(0, rows, part)):
        for slot, todo in schedule.items():
            if slot % 4 == at:

                @pl.when(pair == slot // 4)
                def _(todo=todo):
                    for one in todo:
                        one()

        here = slice(first, first + part)
        q, do = q_ref[0, here, :], do_ref[here, :]
        q_heads = [pick(in_head(part, head), q) for head in range(2)]
        do_heads = [pick(in_head(part, head), do) for head in range(2)]
        probs, slopes = [], []
        for head in range(2):
            one = slice(head, head + 1)
            s = dot(k, q_heads[head], NT)
            p = jnp.exp2(s - lse_ref[0, one, here] + bias)
            dp = dot(v, do_heads[head], NT)
            ds = (p * (dp - delta[0, one, here])).astype(BF)
            probs.append(p.astype(BF))
            slopes.append(ds)
            span = slice(head * HD, (head + 1) * HD)
            dq = dot(k_cols[span], ds, NN)
            dq_cols[span, here] = dq + dq_in[span, here] if second else dq
        dv += dot(jnp.concatenate(probs, axis=1), jnp.concatenate(do_heads, axis=0), NN)
        dk += dot(jnp.concatenate(slopes, axis=1), jnp.concatenate(q_heads, axis=0), NN)
    dk_ref[...] = turn_back(dk * LN2, cosk_ref[...], sink_ref[...]).astype(BF)
    dv_ref[...] = dv.astype(BF)
    if second:
        dq = jnp.transpose(dq_cols[...]) * 0.125
        dq_ref[...] = turn_back(dq, cosq_ref[...], sinq_ref[...]).astype(BF)

    if n:

        @pl.when(pair == 5)
        def _():
            for one in last:
                one()


def attend_back(side, ints, q, k, v, do, lse, extra, tables, dq_part=None, grads=(), ident=None):
    pairs, rows = q.shape[:2]
    n = len(grads)
    leads = [0] * n
    second = side == 0
    row_spec = pl.BlockSpec((rows, PAIR), lambda p: (0, p))
    k_spec = pl.BlockSpec((1, 1, rows, PAIR), lambda p: (side, p, 0, 0))
    stat_spec = pl.BlockSpec((1, 8, rows), lambda p: (p, 0, 0))
    q_table = pl.BlockSpec((rows, PAIR), lambda p: (0, 0))
    k_table = pl.BlockSpec((rows, PAIR), lambda p: (side, 0))
    col_spec = pl.BlockSpec((PAIR, rows), lambda p: (p, 0))
    narrow = jax.ShapeDtypeStruct((rows, D), BF)
    stats = jax.ShapeDtypeStruct((pairs, 8, rows), F32)
    cols = jax.ShapeDtypeStruct((D, rows), F32)
    views, sums, scratch = [], [], []
    if n:
        views, sums, scratch = scatter_xzy_shapes(grads) if second else scatter_shapes(grads, leads)
    params = dict(collective_id=ident, has_side_effects=True) if n else {}
    return pl.pallas_call(
        functools.partial(attend_back_kernel, side, leads),
        grid=(pairs,),
        in_specs=[
            SMEM, pl.BlockSpec((1, rows, PAIR), lambda p: (p, 0, 0)), k_spec, k_spec, row_spec, stat_spec,
            stat_spec if second else row_spec, k_table, k_table,
        ]
        + ([q_table, q_table, col_spec] if second else [])
        + [VMEM] * n,
        out_specs=[row_spec if second else col_spec, row_spec, row_spec]
        + ([] if second else [stat_spec])
        + [VMEM] * n,
        out_shape=[narrow if second else cols, narrow, narrow] + ([] if second else [stats]) + sums,
        scratch_shapes=([pltpu.VMEM((PAIR, rows), F32)] if second else []) + scratch,
        compiler_params=pltpu.CompilerParams(vmem_limit_bytes=VMEM_LIMIT, **params),
        cost_estimate=pl.CostEstimate(
            flops=40 * rows * rows * D, bytes_accessed=16 * rows * D, transcendentals=rows * rows * 12
        ),
        name="attend_back",
    )(ints, q, k, v, do, lse, extra, *tables, *((*tables, dq_part) if second else ()), *views)


def norm(values):
    centre = values - jnp.mean(values, axis=-1, keepdims=True)
    inverse = lax.rsqrt(jnp.mean(centre * centre, axis=-1, keepdims=True) + EPSILON)
    return centre * inverse, inverse


def norm_back(grad_result, normed, inverse, gain):
    scaled = grad_result * gain
    return inverse * (
        scaled
        - jnp.mean(scaled, axis=-1, keepdims=True)
        - normed * jnp.mean(scaled * normed, axis=-1, keepdims=True)
    )


def middle_kernel(
    ints, scale_ref, ctx_ref, x_ref, teacher_ref, vec_ref, wo_ref, wi_ref, wd_ref,
    out_ref, act_ref, hin_ref, gb_ref, gp_ref, ga_ref, gc_ref, gr_ref, part_ref, slope_ref,
):
    block = ctx_ref.shape[0]
    chunk = 1024
    hidden_units = wi_ref.shape[0]
    gain_one, bias_one, gain_two, bias_two = (vec_ref[i : i + 1, :] for i in range(4))
    attended = dot(ctx_ref[...], wo_ref[...], NN)
    normed_one, inverse_one = norm(x_ref[...].astype(F32) + attended)
    hidden = normed_one * gain_one + bias_one
    hidden_in = hidden.astype(BF)
    hin_ref[...] = hidden_in
    total = hidden
    for first in range(0, hidden_units, chunk):
        here = slice(first, first + chunk)
        pre = dot(hidden_in, wi_ref[here, :], NT)
        below = 0.5 + 0.5 * lax.erf(pre * INV_ROOT2)
        act = (pre * below).astype(BF)
        act_ref[:, here] = act
        slope_ref[:, here] = below + pre * jnp.exp(-0.5 * pre * pre) * INV_ROOT_TWO_PI
        total = total + dot(act, wd_ref[here, :], NN)
    normed_two, inverse_two = norm(total)
    final = normed_two * gain_two + bias_two
    out_ref[...] = final.astype(BF)
    place = ints[1] + pl.program_id(0) * block + lax.broadcasted_iota(jnp.int32, (block, D), 0)
    misfit = jnp.where(place < ints[0], final - teacher_ref[...].astype(F32), 0.0)
    grad_final = misfit * scale_ref[0]
    grad_mid = norm_back(grad_final, normed_two, inverse_two, gain_two)
    g_branch = grad_mid.astype(BF)
    gb_ref[...] = g_branch
    grad_hidden = grad_mid
    for first in range(0, hidden_units, chunk):
        here = slice(first, first + chunk)
        grad_act = dot(g_branch, wd_ref[here, :], NT)
        g_pre = (grad_act * slope_ref[:, here]).astype(BF)
        gp_ref[:, here] = g_pre
        grad_hidden = grad_hidden + dot(g_pre, wi_ref[here, :], NN)
    grad_res = norm_back(grad_hidden, normed_one, inverse_one, gain_one)
    gr_ref[...] = grad_res
    g_att = grad_res.astype(BF)
    ga_ref[...] = g_att
    gc_ref[...] = dot(g_att, wo_ref[...], NT).astype(BF)

    @pl.when(pl.program_id(0) == 0)
    def _():
        part_ref[...] = jnp.zeros_like(part_ref)

    for row, term in enumerate(
        (grad_hidden * normed_one, grad_hidden, grad_final * normed_two, grad_final, misfit * misfit)
    ):
        part_ref[row : row + 1, :] += jnp.sum(term, axis=0, keepdims=True)


def middle(ints, scale, context, x, teacher, vectors, out_full, in_full, down_full):
    rows = x.shape[0]
    block = 256
    hidden_units = in_full.shape[0]
    row = pl.BlockSpec((block, D), lambda i: (i, 0))
    wide = pl.BlockSpec((block, hidden_units), lambda i: (i, 0))

    def fixed(shape):
        return pl.BlockSpec(shape, lambda i: (0, 0), pipeline_mode=pl.Buffered(1))

    narrow_out = jax.ShapeDtypeStruct((rows, D), BF)
    wide_out = jax.ShapeDtypeStruct((rows, hidden_units), BF)
    return pl.pallas_call(
        middle_kernel,
        grid=(rows // block,),
        in_specs=[
            SMEM, SMEM, row, row, row, fixed((8, D)), fixed((D, D)), fixed((hidden_units, D)), fixed((hidden_units, D)),
        ],
        out_specs=[row, wide, row, row, wide, row, row, row, pl.BlockSpec((8, D), lambda i: (0, 0))],
        out_shape=[
            narrow_out, wide_out, narrow_out, narrow_out, wide_out, narrow_out, narrow_out,
            jax.ShapeDtypeStruct((rows, D), F32), jax.ShapeDtypeStruct((8, D), F32),
        ],
        scratch_shapes=[pltpu.VMEM((block, hidden_units), F32)],
        compiler_params=pltpu.CompilerParams(vmem_limit_bytes=VMEM_LIMIT),
        cost_estimate=pl.CostEstimate(
            flops=2 * rows * D * (2 * D + 4 * hidden_units),
            bytes_accessed=30 * rows * D + 4 * hidden_units * (rows + D),
            transcendentals=2 * rows * hidden_units,
        ),
        name="middle",
    )(ints, scale, context, x, teacher, vectors, out_full, in_full, down_full)


def on_device(
    layer_input, teacher, lengths, qkv_weight, out_weight, ln1_gain, ln1_bias,
    in_weight, down_weight, ln2_gain, ln2_bias,
):
    own_rows = layer_input.shape[0]
    data_size = lax.axis_size("dp")
    tensor_index = lax.axis_index("tensor")
    group_rows = own_rows * lax.axis_size("tensor")
    assert group_rows == SLOT and lax.axis_size("tensor") == 2 and lengths.shape[0] == 1
    own_comm = data_size == 16

    def gather(values, axis):
        return lax.all_gather(values, EVERYONE, axis=axis, tiled=True)

    def scatter(values, axis):
        return lax.psum_scatter(values, EVERYONE, scatter_dimension=axis, tiled=True)

    def swap(values):
        return lax.ppermute(values, "tensor", [(0, 1), (1, 0)])

    share = D // data_size
    norms = (ln1_gain, ln1_bias, ln2_gain, ln2_bias)
    angles = angle_tables()
    ints = jnp.stack([lengths[0], (tensor_index * own_rows).astype(jnp.int32)])
    if own_comm:
        small = jnp.pad(jnp.stack(norms).astype(F32), ((0, 4), (0, 128 - share)))
        small = jnp.where(lax.broadcasted_iota(jnp.int32, small.shape, 0) == 4, lengths[0].astype(F32), small)
        q, k, v, context, lse, cosine, sine, other_x, qkv_full, small_full, out_full, in_full, down_full = front(
            ints, layer_input, angles, [qkv_weight, small, out_weight, in_weight, down_weight]
        )
        small_full = small_full.reshape(2, data_size, 8, 128)[0]
        vectors = small_full[:, :, :share].transpose(1, 0, 2).reshape(8, D)
        valid_count = jnp.sum(small_full[:, 4, 0])
    else:
        vectors = jnp.stack([lax.all_gather(v, "dp", axis=0, tiled=True).astype(F32) for v in norms])
        vectors = jnp.concatenate([vectors, jnp.zeros((4, D), F32)])
        valid_count = lax.psum(jnp.sum(lengths).astype(F32), "dp")
        out_full, in_full, down_full = gather(out_weight, 0), gather(in_weight, 0), gather(down_weight, 0)
        q, k, v, context, lse, cosine, sine, other_x, qkv_full = front(
            ints, layer_input, angles, gathered=(gather(qkv_weight, 1), swap(layer_input))
        )

    grad_scale = group_rows * data_size * D // 4
    scale = (2.0 * grad_scale / (valid_count * D)).reshape(1)
    final, activated, hidden_in, g_branch, g_pre, g_att, g_context, grad_res, parts = middle(
        ints, scale, context, layer_input, teacher, vectors, out_full, in_full, down_full
    )

    def over_rows(left, right):
        return lax.dot_general(left, right, (((0,), (0,)), ((), ())), preferred_element_type=F32)

    grad_down_w = over_rows(activated, g_branch)
    grad_in_w = over_rows(g_pre, hidden_in)
    grad_out_w = over_rows(context, g_att)
    tables = (cosine, sine)
    if own_comm:
        sum_first, sum_second = [grad_down_w.astype(BF), grad_out_w.astype(BF)], [grad_in_w.astype(BF)]
    else:
        grad_down, grad_in, grad_out = scatter(grad_down_w, 0), scatter(grad_in_w, 0), scatter(grad_out_w, 0)
        sum_first, sum_second = [], []
    dq_part, dk_other, dv_other, delta, *sums = attend_back(
        1, ints, q, k, v, g_context, lse, context, tables, None, sum_first, 1
    )
    if own_comm:
        grad_down, grad_out = sums
    pass_on = dot(dk_other, qkv_full[1], NN) + dot(dv_other, qkv_full[2], NN)
    from_other = swap(pass_on.astype(BF))
    dq, dk_own, dv_own, *sums = attend_back(
        0, ints, q, k, v, g_context, lse, delta, tables, dq_part, sum_second, 2
    )
    if own_comm:
        grad_in = sums[0]
    if own_comm:
        grad_qkv, sums, input_grad = tail(
            dq, dk_own, dv_own, dk_other, dv_other, layer_input, other_x, qkv_full, grad_res, parts, 3
        )
        input_grad = input_grad + from_other.astype(F32)
    else:
        grad_qkv_w = [
            over_rows(dq, layer_input),
            over_rows(dk_own, layer_input) + over_rows(dk_other, other_x),
            over_rows(dv_own, layer_input) + over_rows(dv_other, other_x),
        ]
        grad_qkv = scatter(jnp.stack(grad_qkv_w), 1)
        sums = lax.psum(parts, ("dp", "tensor"))
        input_grad = (
            grad_res
            + dot(dq, qkv_full[0], NN)
            + dot(dk_own, qkv_full[1], NN)
            + dot(dv_own, qkv_full[2], NN)
            + from_other.astype(F32)
        )
    loss_value = jnp.sum(sums[4]) / (valid_count * D)
    own_norms = lax.dynamic_slice_in_dim(sums, lax.axis_index("dp") * share, share, 1)
    return (
        final, loss_value, input_grad, grad_qkv, grad_out,
        own_norms[0], own_norms[1], grad_in, grad_down, own_norms[2], own_norms[3],
    )


def solution(mesh):
    rows = P(("dp", "tensor"), None)
    shard = P(EVERYONE, None)
    in_specs = (
        rows, rows, P("dp"), P(None, EVERYONE, None), shard, P("dp"), P("dp"), shard, shard, P("dp"), P("dp"),
    )
    out_specs = (
        rows, P(), rows, P(None, EVERYONE, None), shard, P("dp"), P("dp"), shard, shard, P("dp"), P("dp"),
    )
    return jax.shard_map(on_device, mesh=mesh, in_specs=in_specs, out_specs=out_specs, check_vma=False)
```

```python
import functools

import jax
import jax.numpy as jnp
from jax import lax
from jax.experimental import pallas as pl
from jax.experimental.pallas import tpu as pltpu
from jax.sharding import PartitionSpec as P

D = 768
HD = 64
SLOT = 2048
PAIR = 2 * HD
EPSILON = 1e-05
NEG_LARGE = -1e30
ROPE_BASE = 10000.0
INV_ROOT2 = 0.7071067811865476
INV_ROOT_TWO_PI = 0.3989422804014327
LOG2E = 1.4426950408889634
LN2 = 0.6931471805599453
EVERYONE = ("tensor", "dp")

BF = jnp.bfloat16
F32 = jnp.float32
NT = (((1,), (1,)), ((), ()))
NN = (((1,), (0,)), ((), ()))
VMEM_LIMIT = 56 << 20
MESH = pl.DeviceIdType.MESH
HBM = pl.BlockSpec(memory_space=pl.ANY)
VMEM = pl.BlockSpec(memory_space=pltpu.VMEM)
SMEM = pl.BlockSpec(memory_space=pltpu.SMEM)


def dot(a, b, dims):
    return lax.dot_general(a, b, dims, preferred_element_type=F32)


GRID = (2, 4, 2, 2)
ORDER = (2, 1, 3, 0)


def coords():
    dp = lax.axis_index("dp")
    return lax.axis_index("tensor"), dp // 4, (dp // 2) % 2, dp % 2


def device(y, z, x, c):
    return (z * 4 + x * 2 + c, y)


def greet():
    y, z, x, c = coords()
    barrier = pltpu.get_barrier_semaphore()
    peers = [device(y, (z + dz) % 4, x, c) for dz in (1, 2, 3)]
    peers += [device(1 - y, z, x, c), device(y, z, 1 - x, c), device(y, z, x, 1 - c)]
    for peer in peers:
        pl.semaphore_signal(barrier, inc=1, device_id=peer, device_id_type=MESH)
    pl.semaphore_wait(barrier, len(peers))


def full_shapes(shards, leads):
    return [jax.ShapeDtypeStruct(s.shape[:l] + (32 * s.shape[l],) + s.shape[l + 1 :], s.dtype) for s, l in zip(shards, leads)]


DELTAS = (0, -1, 1, -2, 2, -3, 3)


def gather_sems(count):
    return [pltpu.SemaphoreType.DMA((count, 81)), pltpu.SemaphoreType.DMA((count, 32))]


def gather_parts(order, leads, shards, fulls, send_sem, recv_sem):
    y, z, x, c = coords()
    to_y, to_x, to_c = device(1 - y, z, x, c), device(y, z, 1 - x, c), device(y, z, x, 1 - c)
    own = (0, 0, 0)

    def arrives_over(block):
        apart = dict(zip("yzx", block))
        return [axis for axis in order if apart[axis]][-1]

    def plan(i):
        at = (slice(None),) * leads[i]
        shard, full = shards[i], fulls[i]
        count = shard.shape[leads[i]]

        def spot(block):
            dy, delta, dx = block
            place = (y if dy == 0 else 1 - y) * 16 + (z + delta) * 4 + (x if dx == 0 else 1 - x) * 2 + c
            return full.at[at + (pl.ds(pl.multiple_of(place * count, 8), count),)]

        def copy(block, send_slot, dy, dx, to, recv_base=0):
            place = z + block[1]
            return pltpu.make_async_remote_copy(
                src_ref=shard if block == own else spot(block),
                dst_ref=spot(block),
                send_sem=send_sem.at[i, send_slot + 8 * block[2] + 4 * block[0] + place],
                recv_sem=recv_sem.at[i, recv_base + 8 * dx + 4 * dy + place],
                device_id=to,
                device_id_type=MESH,
            )

        return dict(
            right=lambda b: copy(b, 0, b[0], b[2], device(y, z + 1, x, c)),
            left=lambda b: copy(b, 16, b[0], b[2], device(y, z - 1, x, c)),
            y=lambda b: copy(b, 32, 1, b[2], to_y),
            x=lambda b: copy(b, 48, b[0], 1, to_x),
            core=lambda b: copy(b, 64, b[0], b[2], to_c, 16),
            landed=lambda b: copy(b, 64, b[0], b[2], to_c),
            local=lambda: pltpu.make_async_copy(shard, spot(own), send_sem.at[i, 80]),
        )

    plans = [plan(i) for i in range(len(shards))]

    def when_there(block, action):
        if block[1] == 0:
            action()
        else:
            pl.when((z + block[1] >= 0) & (z + block[1] <= 3))(action)

    def onward(p, block, run, axes=None):
        axis = None if block == own else arrives_over(block)
        if axes is None:
            axes = order if axis is None else order[order.index(axis) + (axis != "z") :]
        for later in axes:
            if later != "z":
                run(p[later](block))
                continue
            if block[1] <= 0:
                pl.when(z < 3)(lambda: run(p["right"](block)))
            if block[1] >= 0:
                pl.when(z > 0)(lambda: run(p["left"](block)))

    def begin(axes, last):
        for p in plans:
            onward(p, own, lambda copy: copy.start(), axes)
            if last:
                p["core"](own).start()
                p["local"]().start()

    def after(block):
        def action():
            for p in plans:
                p["landed"](block).wait_recv()
                onward(p, block, lambda copy: copy.start())
                p["core"](block).start()

        when_there(block, action)

    def finish():
        def action_of(block):
            def action():
                for p in plans:
                    onward(p, block, lambda copy: copy.wait_send())
                    p["core"](block).wait()

            return action

        for dy in range(2):
            for dx in range(2):
                for delta in DELTAS:
                    when_there((dy, delta, dx), action_of((dy, delta, dx)))
        for p in plans:
            p["local"]().wait()

    return begin, after, finish


def both_ways(dy, distance, dx):
    return [(dy, delta, dx) for delta in ((0,) if distance == 0 else (-distance, distance))]


def scatter_shapes(grads, leads):
    views, outs, scratch = [], [], []
    for g, l in zip(grads, leads):
        head, rows, tail = g.shape[:l], g.shape[l] // 32, g.shape[l + 1 :]
        if not isinstance(g, jax.ShapeDtypeStruct):
            views.append(g.reshape(head + GRID + (rows,) + tail))
        shard = head + (rows,) + tail
        outs.append(jax.ShapeDtypeStruct(shard, F32))
        wide = pltpu.VMEM((4,) + head + (2, 2, rows) + tail, BF)
        pair = pltpu.VMEM((4,) + head + (2, rows) + tail, BF)
        one = pltpu.VMEM((4,) + shard, BF)
        scratch += [wide, pair, pair, one, one, one, one]
    count = len(grads)
    return views, outs, scratch + [pltpu.SemaphoreType.DMA((count, 16))] * 2


def scatter_parts(leads, grads, outs, bufs, send_sem, recv_sem, x_first):
    y, z, x, c = coords()
    n = len(leads)
    to_y, to_x, to_c = device(1 - y, z, x, c), device(y, z, 1 - x, c), device(y, z, x, 1 - c)

    def zz(dz):
        return (z + dz) % 4

    def lead(i):
        return (slice(None),) * leads[i]

    def copy(i, slot, source, target, to):
        return pltpu.make_async_remote_copy(
            src_ref=source, dst_ref=target, send_sem=send_sem.at[i, slot], recv_sem=recv_sem.at[i, slot],
            device_id=to, device_id_type=MESH,
        )

    def over_c(i, dz):
        return copy(i, dz, grads[i].at[lead(i) + (slice(None), zz(dz), slice(None), 1 - c)], bufs[7 * i].at[dz], to_c)

    def over_first(i, dz):
        to = to_x if dz in x_first else to_y
        return copy(i, 4 + dz, bufs[7 * i + 1].at[dz], bufs[7 * i + 2].at[dz], to)

    def over_second(i, dz):
        to = to_y if dz in x_first else to_x
        return copy(i, 8 + dz, bufs[7 * i + 3].at[dz], bufs[7 * i + 4].at[dz], to)

    def over_z(i, dz):
        return copy(i, 12 + dz, bufs[7 * i + 5].at[dz], bufs[7 * i + 6].at[dz], device(y, zz(dz), x, c))

    def chip_sum(i, dz, yy, xx):
        own = grads[i][lead(i) + (yy, zz(dz), xx, c)].astype(F32)
        return own + bufs[7 * i][(dz,) + lead(i) + (yy, xx)].astype(F32)

    def begin():
        for dz in ORDER:
            for i in range(n):
                over_c(i, dz).start()

    def after_c(dz):
        for i in range(n):
            over_c(i, dz).wait_recv()
            for far in range(2):
                yy, xx = ((1 - y if far else y), 1 - x) if dz in x_first else (1 - y, (1 - x if far else x))
                bufs[7 * i + 1][(dz,) + lead(i) + (far,)] = chip_sum(i, dz, yy, xx).astype(BF)
            over_first(i, dz).start()

    def after_first(dz):
        for i in range(n):
            over_first(i, dz).wait_recv()
            yy, xx = (1 - y, x) if dz in x_first else (y, 1 - x)
            total = chip_sum(i, dz, yy, xx) + bufs[7 * i + 2][(dz,) + lead(i) + (1,)].astype(F32)
            bufs[7 * i + 3][dz] = total.astype(BF)
            over_second(i, dz).start()

    def after_second(dz):
        for i in range(n):
            over_second(i, dz).wait_recv()
            total = chip_sum(i, dz, y, x) + bufs[7 * i + 2][(dz,) + lead(i) + (0,)].astype(F32)
            total = total + bufs[7 * i + 4][dz].astype(F32)
            if dz == 0:
                outs[i][...] = total
            else:
                bufs[7 * i + 5][dz] = total.astype(BF)
                over_z(i, dz).start()

    def after_z(dz):
        for i in range(n):
            over_z(i, dz).wait_recv()
            outs[i][...] += bufs[7 * i + 6][dz].astype(F32)

    def finish():
        for i in range(n):
            for dz in range(4):
                over_c(i, dz).wait_send()
                over_first(i, dz).wait_send()
                over_second(i, dz).wait_send()
                if dz:
                    over_z(i, dz).wait_send()

    stages = [[functools.partial(f, dz) for dz in ORDER] for f in (after_c, after_first, after_second)]
    last = [functools.partial(after_z, dz) for dz in ORDER[:3]]
    return [begin], stages[0], stages[1], stages[2], last, [finish]


def scatter_xzy_shapes(grads):
    views, outs, scratch = [], [], []
    for g in grads:
        rows = g.shape[0] // 32
        shard = (rows,) + g.shape[1:]
        views.append(g.reshape(GRID + shard))
        outs.append(jax.ShapeDtypeStruct(shard, F32))
        pair = pltpu.VMEM((4, 2) + shard, BF)
        scratch += [pltpu.VMEM((4, 2, 2) + shard, BF), pair, pair, pair, pair]
        scratch += [pltpu.VMEM((2,) + shard, F32), pltpu.VMEM((2,) + shard, BF)]
    count = len(grads)
    return views, outs, scratch + [pltpu.SemaphoreType.DMA((count, 16))] * 2


def scatter_xzy_parts(grads, outs, bufs, send_sem, recv_sem):
    y, z, x, c = coords()
    n = len(grads)

    def zz(dz):
        return (z + dz) % 4

    def copy(i, slot, source, target, to):
        return pltpu.make_async_remote_copy(
            src_ref=source, dst_ref=target, send_sem=send_sem.at[i, slot], recv_sem=recv_sem.at[i, slot],
            device_id=to, device_id_type=MESH,
        )

    def over_c(i, dz):
        source = grads[i].at[:, zz(dz), :, 1 - c]
        return copy(i, dz, source, bufs[7 * i].at[dz], device(y, z, x, 1 - c))

    def over_x(i, dz):
        return copy(i, 4 + dz, bufs[7 * i + 1].at[dz], bufs[7 * i + 2].at[dz], device(y, z, 1 - x, c))

    def over_z(i, dz):
        return copy(i, 8 + dz, bufs[7 * i + 3].at[dz], bufs[7 * i + 4].at[dz], device(y, zz(dz), x, c))

    def over_y(i):
        return copy(i, 12, bufs[7 * i + 6].at[0], bufs[7 * i + 6].at[1], device(1 - y, z, x, c))

    def chip_sum(i, dz, yy, xx):
        return grads[i][yy, zz(dz), xx, c].astype(F32) + bufs[7 * i][dz, yy, xx].astype(F32)

    def begin():
        for dz in ORDER:
            for i in range(n):
                over_c(i, dz).start()

    def after_c(dz):
        for i in range(n):
            over_c(i, dz).wait_recv()
            for yy in range(2):
                bufs[7 * i + 1][dz, yy] = chip_sum(i, dz, yy, 1 - x).astype(BF)
            over_x(i, dz).start()

    def after_x(dz):
        for i in range(n):
            over_x(i, dz).wait_recv()
            for yy in range(2):
                total = chip_sum(i, dz, yy, x) + bufs[7 * i + 2][dz, yy].astype(F32)
                if dz:
                    bufs[7 * i + 3][dz, yy] = total.astype(BF)
                else:
                    bufs[7 * i + 5][yy] = total
            if dz:
                over_z(i, dz).start()

    def after_z(dz):
        for i in range(n):
            over_z(i, dz).wait_recv()
            for yy in range(2):
                bufs[7 * i + 5][yy] += bufs[7 * i + 4][dz, yy].astype(F32)

    def send_y():
        for i in range(n):
            bufs[7 * i + 6][0] = bufs[7 * i + 5][1 - y].astype(BF)
            over_y(i).start()

    def finish():
        for i in range(n):
            over_y(i).wait()
            outs[i][...] = bufs[7 * i + 5][y] + bufs[7 * i + 6][1].astype(F32)
            for dz in range(4):
                over_c(i, dz).wait_send()
                over_x(i, dz).wait_send()
                if dz:
                    over_z(i, dz).wait_send()

    return begin, after_c, after_x, after_z, send_y, finish


def tail_kernel(
    dq_hbm, dk_hbm, dv_hbm, dk_far_hbm, dv_far_hbm, x_hbm, far_hbm, w_hbm, res_hbm, small_in,
    out_q, out_k, out_v, small_out, input_hbm,
    dq, dk, dv, dk_far, dv_far, x, far, w, res, load_sem, store_sem, grad_q, grad_k, grad_v, *refs,
):
    sums = (out_q, out_k, out_v)
    grads = (grad_q, grad_k, grad_v)
    per = 9
    hops, small_send, small_recv = refs[3 * per :]
    y, z, at_x, c = coords()
    rows = x.shape[0]
    pairs = (
        (dq_hbm, dq), (x_hbm, x), (dk_hbm, dk), (dk_far_hbm, dk_far), (far_hbm, far), (dv_hbm, dv),
        (dv_far_hbm, dv_far), (w_hbm, w), (res_hbm, res),
    )
    loads = [pltpu.make_async_copy(src, dst, load_sem.at[i]) for i, (src, dst) in enumerate(pairs)]
    for load in loads:
        load.start()
    greet()
    stages = [
        scatter_parts([0], grads[j : j + 1], sums[j : j + 1], refs[per * j : per * j + 7], *refs[per * j + 7 : per * j + 9], (0, 1))
        for j in range(3)
    ]

    def run(j, stage):
        for part in stages[j][stage]:
            part()

    def hop(source, target, to):
        return pltpu.make_async_remote_copy(
            src_ref=hops.at[source], dst_ref=hops.at[target], send_sem=small_send.at[target],
            recv_sem=small_recv.at[target], device_id=to, device_id_type=MESH,
        )

    hops[0] = small_in[...]
    over_c = hop(0, 1, device(y, z, at_x, 1 - c))
    over_c.start()

    def weight_grad(j, terms):
        half = D // 2
        for yy in range(2):
            cols = slice(yy * half, (yy + 1) * half)
            total = None
            for left, right in terms:
                part = dot(left[:, cols], right[...], (((0,), (0,)), ((), ())))
                total = part if total is None else total + part
            grads[j][yy] = total.astype(BF).reshape(grads[j].shape[1:])
        run(j, 0)

    def input_block(block):
        here = slice(block * ROWS_STEP, (block + 1) * ROWS_STEP)
        total = res[here, :]
        for j, left in enumerate((dq, dk, dv)):
            total = total + dot(left[here, :], w[j], NN)
        res[here, :] = total
        pltpu.make_async_copy(res.at[here], input_hbm.at[here], store_sem.at[block]).start()

    loads[0].wait()
    loads[1].wait()
    weight_grad(0, [(dq, x)])
    for i in (2, 3, 4):
        loads[i].wait()
    weight_grad(1, [(dk, x), (dk_far, far)])
    run(0, 1)
    loads[5].wait()
    loads[6].wait()
    weight_grad(2, [(dv, x), (dv_far, far)])
    run(1, 1)
    over_c.wait()
    hops[2] = hops[0] + hops[1]
    over_x = hop(2, 3, device(y, z, 1 - at_x, c))
    over_x.start()
    run(0, 2)
    run(2, 1)
    for i in (7, 8):
        loads[i].wait()
    input_block(0)
    over_x.wait()
    hops[4] = hops[2] + hops[3]
    over_y = hop(4, 5, device(1 - y, z, at_x, c))
    over_y.start()
    run(0, 3)
    run(1, 2)
    input_block(1)
    run(1, 3)
    run(2, 2)
    over_y.wait()
    hops[6] = hops[4] + hops[5]
    over_z = [hop(6, 6 + dz, device(y, (z + dz) % 4, at_x, c)) for dz in (1, 2, 3)]
    for one in over_z:
        one.start()
    input_block(2)
    run(2, 3)
    run(0, 4)
    input_block(3)
    run(1, 4)
    run(2, 4)
    for one in over_z:
        one.wait()
    small_out[...] = (hops[6] + hops[8]) + (hops[7] + hops[9])
    for j in range(3):
        run(j, 5)
    for block in range(rows // ROWS_STEP):
        here = slice(block * ROWS_STEP, (block + 1) * ROWS_STEP)
        pltpu.make_async_copy(res.at[here], input_hbm.at[here], store_sem.at[block]).wait()


def tail(dq, dk, dv, dk_far, dv_far, x, far, w, res, small, ident):
    rows = x.shape[0]
    share = D // 32
    grad = jax.ShapeDtypeStruct((D, D), BF)
    outs, scratch = [], []
    for _ in range(3):
        _, out, bufs = scatter_shapes([grad], [0])
        outs += out
        scratch += bufs
    narrow = pltpu.VMEM((rows, D), BF)
    out = pl.pallas_call(
        tail_kernel,
        in_specs=[HBM] * 9 + [VMEM],
        out_specs=[VMEM] * 4 + [HBM],
        out_shape=outs + [jax.ShapeDtypeStruct(small.shape, F32), jax.ShapeDtypeStruct((rows, D), F32)],
        scratch_shapes=[narrow] * 7
        + [pltpu.VMEM((3, D, D), BF), pltpu.VMEM((rows, D), F32)]
        + [pltpu.SemaphoreType.DMA((9,)), pltpu.SemaphoreType.DMA((rows // ROWS_STEP,))]
        + [pltpu.VMEM(GRID + (share, D), BF)] * 3
        + scratch
        + [pltpu.VMEM((10,) + small.shape, F32)]
        + [pltpu.SemaphoreType.DMA((10,))] * 2,
        compiler_params=pltpu.CompilerParams(collective_id=ident, has_side_effects=True, vmem_limit_bytes=VMEM_LIMIT),
        name="tail",
    )(dq, dk, dv, dk_far, dv_far, x, far, w, res, small)
    return jnp.stack(out[:3]), out[3], out[4]


def in_head(rows, head):
    lane = lax.broadcasted_iota(jnp.int32, (rows, PAIR), 1)
    return lane < HD if head == 0 else lane >= HD


def pick(mask, values):
    return jnp.where(mask, values, jnp.zeros_like(values))


def swap_pairs(values):
    even = lax.broadcasted_iota(jnp.int32, values.shape, 1) % 2 == 0
    return jnp.where(even, pltpu.roll(values, PAIR - 1, 1), pltpu.roll(values, 1, 1))


def turn(values, cosine, signed_sine):
    return values * cosine + swap_pairs(values) * signed_sine


def turn_back(values, cosine, signed_sine):
    return values * cosine - swap_pairs(values) * signed_sine


def angle_tables():
    lane = jnp.arange(PAIR)
    inverse_freq = ROPE_BASE ** (-2.0 * ((lane % HD) // 2).astype(F32) / HD)
    places = jnp.concatenate([jnp.arange(SLOT // 64) * 64, jnp.arange(64)]).astype(F32)
    angles = places[:, None] * inverse_freq[None, :]
    return jnp.stack([jnp.cos(angles), jnp.sin(angles)])


ROWS_STEP = 256
B1 = (2, 8, 12, 17, 21)
B2 = (2, 8, 13, 18, 22)
QUERY_STEP = 1024


def front_plan(rows):
    project_steps = rows // ROWS_STEP
    attend_steps = (D // PAIR) * (rows // QUERY_STEP)
    return project_steps, attend_steps


def project_step(side, block, x_ref, w_ref, cos_ref, sin_ref, q_ref, k_ref, v_ref):
    rows = x_ref.shape[0]
    here = pl.ds(pl.multiple_of(block * ROWS_STEP, ROWS_STEP), ROWS_STEP)
    x = x_ref[here, :]
    table = pl.ds(pl.multiple_of(side * rows + block * ROWS_STEP, ROWS_STEP), ROWS_STEP)
    cosine, sine = cos_ref[table, :], sin_ref[table, :]
    for j in range(0 if side == 0 else 1, 3):
        full = dot(x, w_ref[j], NT)
        for pair in range(D // PAIR):
            part = full[:, pair * PAIR : (pair + 1) * PAIR]
            if j < 2:
                part = turn(part, cosine, sine)
            if j == 0:
                q_ref[pair, here, :] = (part * (0.125 * LOG2E)).astype(BF)
            elif j == 1:
                k_ref[side, pair, here, :] = part.astype(BF)
            else:
                v_ref[side, pair, here, :] = part.astype(BF)


def attend_step(side, place, bias, q_ref, k_ref, v_ref, mix_ref, stat_ref, ctx_ref, lse_ref):
    rows = q_ref.shape[1]
    blocks = rows // QUERY_STEP
    pair, block = place // blocks, lax.rem(place, blocks)
    here = pl.ds(pl.multiple_of(block * QUERY_STEP, QUERY_STEP), QUERY_STEP)
    q, k = q_ref[pair, here, :], k_ref[side, pair]
    keys = k.shape[0]
    v_cols = jnp.transpose(v_ref[side, pair].astype(F32)).astype(BF)
    scores = [dot(k, pick(in_head(QUERY_STEP, head), q), NT) + bias for head in range(2)]
    outs = []
    for head, s in enumerate(scores):
        span = slice(head * HD, (head + 1) * HD)
        one, two = slice(head, head + 1), slice(2 + head, 3 + head)
        peak = jnp.max(s, axis=0, keepdims=True)
        if side:
            before = stat_ref[pair, one, here]
            peak = jnp.maximum(peak, before)
        p = jnp.exp2(s - peak).astype(BF)
        v_aug = jnp.concatenate([v_cols[span], jnp.ones((16, keys), BF)], axis=0)
        mixed = dot(v_aug, p, NN)
        total = mixed[HD : HD + 1]
        mixed = mixed[:HD]
        if side:
            shrink = jnp.exp2(before - peak)
            total = total + shrink * stat_ref[pair, two, here]
            mixed = mixed + shrink * mix_ref[pair, span, here]
            outs.append(mixed / total)
            lse_ref[pair, one, here] = peak + jnp.log2(total)
        else:
            mix_ref[pair, span, here] = mixed
            stat_ref[pair, one, here] = peak
            stat_ref[pair, two, here] = total
    if side:
        columns = pl.ds(pl.multiple_of(pair * PAIR, PAIR), PAIR)
        ctx_ref[here, columns] = jnp.transpose(jnp.concatenate(outs, axis=0)).astype(BF)


def fill_tables(coarse_fine, first, cos_ref, sin_ref):
    rows = cos_ref.shape[0] // 2
    lane = lax.broadcasted_iota(jnp.int32, (64, PAIR), 1)
    sign = jnp.where(lane % 2 == 0, -1.0, 1.0)
    fine = pl.ds(SLOT // 64, 64)
    fine_cos, fine_sin = coarse_fine[0, fine, :], coarse_fine[1, fine, :]
    for side in range(2):
        start = first if side == 0 else rows - first
        for at in range(rows // 64):
            place = pl.ds(start // 64 + at, 1)
            cos_a, sin_a = coarse_fine[0, place, :], coarse_fine[1, place, :]
            target = slice(side * rows + at * 64, side * rows + (at + 1) * 64)
            cos_ref[target, :] = cos_a * fine_cos - sin_a * fine_sin
            sin_ref[target, :] = (sin_a * fine_cos + cos_a * fine_sin) * sign


def front_kernel(comm, *refs):
    step = pl.program_id(0)
    y, z, x, c = coords()
    if comm:
        ints, x_ref, angle_ref, qkv_shard, small_shard, out_shard, in_shard, down_shard = refs[:8]
        q_ref, k_ref, v_ref, ctx_ref, lse_ref, cos_ref, sin_ref, other_hbm = refs[8:16]
        qkv_full, small_full, out_full, in_full, down_full = refs[16:21]
        mix_ref, stat_ref, w_ref, other_ref, first_send, first_recv, send_sem, recv_sem, swap_sem, load_sem = refs[21:]
        first_begin, first_after, first_finish = gather_parts(
            "zyx", [1, 0], [qkv_shard, small_shard], [qkv_full, small_full], first_send, first_recv
        )
        rest_begin, rest_after, rest_finish = gather_parts(
            "yzx", [0, 0, 0], [out_shard, in_shard, down_shard], [out_full, in_full, down_full], send_sem, recv_sem
        )
        swap = pltpu.make_async_remote_copy(
            src_ref=x_ref, dst_ref=other_ref, send_sem=swap_sem.at[0], recv_sem=swap_sem.at[1],
            device_id=device(1 - y, z, x, c), device_id_type=MESH,
        )
        load = pltpu.make_async_copy(qkv_full, w_ref, load_sem.at[0])
        keep = pltpu.make_async_copy(other_ref, other_hbm, load_sem.at[1])
    else:
        ints, x_ref, angle_ref, w_ref, other_ref = refs[:5]
        q_ref, k_ref, v_ref, ctx_ref, lse_ref, cos_ref, sin_ref = refs[5:12]
        mix_ref, stat_ref = refs[12:]
    rows = x_ref.shape[0]
    projects, attends = front_plan(rows)

    @pl.when(step == 0)
    def _():
        if comm:
            greet()
            first_begin("zyx", True)
        fill_tables(angle_ref, y * rows, cos_ref, sin_ref)
        if comm:
            for places in (
                ((0, 1, 0), (1, 0, 0), (0, 0, 1), (0, 2, 0), (1, 1, 0), (0, 3, 0)),
                ((0, 1, 1), (1, 0, 1), (1, 2, 0), (1, 3, 0), (0, 2, 1), (1, 1, 1), (0, 3, 1), (1, 2, 1), (1, 3, 1)),
            ):
                for where in places:
                    for block in both_ways(*where):
                        first_after(block)
                if places[0] == (0, 1, 0):
                    rest_begin("y", False)
                    swap.start()
            rest_begin("zx", True)
            first_finish()
            load.start()
            load.wait()

    if comm:

        schedule = {
            1: [(1, 0, 0)], 4: [(1, 1, 0)], 7: [(0, 1, 0)], 9: [(1, 2, 0)], 10: [(1, 0, 1), (0, 0, 1)], 11: [(0, 2, 0)],
            12: [(1, 1, 1)], 13: [(1, 3, 0)], 16: [(0, 3, 0)], 17: [(0, 1, 1)], 19: [(1, 2, 1), (1, 3, 1)],
        }
        for at, places in schedule.items():

            @pl.when(step == at)
            def _(places=places):
                for where in places:
                    for block in both_ways(*where):
                        rest_after(block)

    begin = 1
    for side in range(2):
        source = x_ref if side == 0 else other_ref
        start = y * rows if side == 0 else (1 - y) * rows
        if side and comm:

            @pl.when(step == begin)
            def _():
                swap.wait()
                keep.start()


        @pl.when((step >= begin) & (step < begin + projects))
        def _(side=side, begin=begin, source=source):
            project_step(side, step - begin, source, w_ref, cos_ref, sin_ref, q_ref, k_ref, v_ref)

        begin += projects

        @pl.when((step >= begin) & (step < begin + attends))
        def _(side=side, begin=begin, start=start):
            place = start + lax.broadcasted_iota(jnp.int32, (rows, 1), 0)
            bias = jnp.where(place < ints[0], 0.0, NEG_LARGE)
            attend_step(side, step - begin, bias, q_ref, k_ref, v_ref, mix_ref, stat_ref, ctx_ref, lse_ref)

        begin += attends

    if comm:

        @pl.when(step == begin - 1)
        def _():
            for block in both_ways(0, 2, 1) + both_ways(0, 3, 1):
                rest_after(block)
            rest_finish()
            keep.wait()


def front(ints, x, angles, shards=None, gathered=None):
    rows = x.shape[0]
    pairs = D // PAIR
    projects, attends = front_plan(rows)
    heads = jax.ShapeDtypeStruct((2, pairs, rows, PAIR), BF)
    table = jax.ShapeDtypeStruct((2 * rows, PAIR), F32)
    narrow = jax.ShapeDtypeStruct((rows, D), BF)
    outs = [
        jax.ShapeDtypeStruct((pairs, rows, PAIR), BF), heads, heads, narrow,
        jax.ShapeDtypeStruct((pairs, 8, rows), F32), table, table,
    ]
    scratch = [pltpu.VMEM((pairs, PAIR, rows), F32), pltpu.VMEM((pairs, 8, rows), F32)]
    params = {}
    comm = shards is not None
    if comm:
        leads = [1, 0, 0, 0, 0]
        outs += [narrow] + full_shapes(shards, leads)
        scratch += [pltpu.VMEM((3, D, D), BF), pltpu.VMEM((rows, D), BF)] + gather_sems(2) + gather_sems(3)
        scratch += [pltpu.SemaphoreType.DMA((2,)), pltpu.SemaphoreType.DMA((2,))]
        params = dict(collective_id=0, has_side_effects=True)
    out = pl.pallas_call(
        functools.partial(front_kernel, comm),
        grid=(1 + 2 * (projects + attends),),
        in_specs=[SMEM, VMEM, VMEM] + ([HBM] * 5 if comm else [VMEM] * 2),
        out_specs=[VMEM] * 7 + ([HBM] * 6 if comm else []),
        out_shape=outs,
        scratch_shapes=scratch,
        compiler_params=pltpu.CompilerParams(vmem_limit_bytes=VMEM_LIMIT, **params),
        cost_estimate=pl.CostEstimate(
            flops=2 * rows * D * D * 5 + 16 * rows * SLOT * D,
            bytes_accessed=60 * rows * D,
            transcendentals=rows * SLOT * 12,
        ),
        name="front",
    )(ints, x, angles, *(shards if comm else gathered))
    if comm:
        return out
    return (*out, gathered[1], gathered[0])


def attend_back_kernel(side, leads, *refs):
    n = len(leads)
    ints, q_ref, k_ref, v_ref, do_ref, lse_ref, extra_ref, cosk_ref, sink_ref = refs[:9]
    used = 9
    second = side == 0
    if second:
        cosq_ref, sinq_ref, dq_in = refs[9:12]
        used = 12
    grads = refs[used : used + n]
    used += n
    dq_ref, dk_ref, dv_ref = refs[used : used + 3]
    used += 3
    if not second:
        delta_ref = refs[used]
        used += 1
    outs = refs[used : used + n]
    used += n
    if second:
        dq_cols = refs[used]
        used += 1
    else:
        dq_cols = dq_ref
    pair = pl.program_id(0)
    schedule, last = {}, []
    if n and side:
        begin, cores, firsts, seconds, lasts, end = scatter_parts(
            leads, grads, outs, refs[used : used + 7 * n], *refs[used + 7 * n :], (0, 1)
        )
        schedule = {
            0: [greet] + begin, B1[0]: cores[:2], B1[1]: firsts[:2] + cores[2:], B1[2]: seconds[:2], B1[3]: firsts[2:],
            B1[4]: seconds[2:] + lasts[:1],
        }
        last = lasts[1:] + end
    elif n:
        begin, after_c, after_x, after_z, send_y, end = scatter_xzy_parts(
            grads, outs, refs[used : used + 7 * n], *refs[used + 7 * n :]
        )
        schedule = {0: [greet, begin], B2[0]: [functools.partial(after_c, dz) for dz in ORDER]}
        for slot, dz in zip(B2[1:], ORDER):
            schedule[slot] = [functools.partial(after_x, dz)]
        schedule[23] = [functools.partial(after_z, dz) for dz in ORDER[:2]]
        last = [functools.partial(after_z, ORDER[2]), send_y, end]
    rows, keys = q_ref.shape[1], k_ref.shape[2]
    part = 256
    k, v = k_ref[0, 0], v_ref[0, 0]
    y = lax.axis_index("tensor")
    place = (y if second else 1 - y) * rows + lax.broadcasted_iota(jnp.int32, (keys, 1), 0)
    bias = jnp.where(place < ints[0], 0.0, NEG_LARGE)
    k_cols = jnp.transpose(k.astype(F32)).astype(BF)
    if not second:
        both = jnp.transpose(do_ref[...].astype(F32) * extra_ref[...].astype(F32))
        delta_ref[0, 0:1, :] = jnp.sum(both[:HD], axis=0, keepdims=True)
        delta_ref[0, 1:2, :] = jnp.sum(both[HD:], axis=0, keepdims=True)
    delta = extra_ref if second else delta_ref
    dk = jnp.zeros((keys, PAIR), F32)
    dv = jnp.zeros((keys, PAIR), F32)
    for at, first in enumerate(range(0, rows, part)):
        for slot, todo in schedule.items():
            if slot % 4 == at:

                @pl.when(pair == slot // 4)
                def _(todo=todo):
                    for one in todo:
                        one()

        here = slice(first, first + part)
        q, do = q_ref[0, here, :], do_ref[here, :]
        q_heads = [pick(in_head(part, head), q) for head in range(2)]
        do_heads = [pick(in_head(part, head), do) for head in range(2)]
        probs, slopes = [], []
        for head in range(2):
            one = slice(head, head + 1)
            s = dot(k, q_heads[head], NT)
            p = jnp.exp2(s - lse_ref[0, one, here] + bias)
            dp = dot(v, do_heads[head], NT)
            ds = (p * (dp - delta[0, one, here])).astype(BF)
            probs.append(p.astype(BF))
            slopes.append(ds)
            span = slice(head * HD, (head + 1) * HD)
            dq = dot(k_cols[span], ds, NN)
            dq_cols[span, here] = dq + dq_in[span, here] if second else dq
        dv += dot(jnp.concatenate(probs, axis=1), jnp.concatenate(do_heads, axis=0), NN)
        dk += dot(jnp.concatenate(slopes, axis=1), jnp.concatenate(q_heads, axis=0), NN)
    dk_ref[...] = turn_back(dk * LN2, cosk_ref[...], sink_ref[...]).astype(BF)
    dv_ref[...] = dv.astype(BF)
    if second:
        dq = jnp.transpose(dq_cols[...]) * 0.125
        dq_ref[...] = turn_back(dq, cosq_ref[...], sinq_ref[...]).astype(BF)

    if n:

        @pl.when(pair == 5)
        def _():
            for one in last:
                one()


def attend_back(side, ints, q, k, v, do, lse, extra, tables, dq_part=None, grads=(), ident=None):
    pairs, rows = q.shape[:2]
    n = len(grads)
    leads = [0] * n
    second = side == 0
    row_spec = pl.BlockSpec((rows, PAIR), lambda p: (0, p))
    k_spec = pl.BlockSpec((1, 1, rows, PAIR), lambda p: (side, p, 0, 0))
    stat_spec = pl.BlockSpec((1, 8, rows), lambda p: (p, 0, 0))
    q_table = pl.BlockSpec((rows, PAIR), lambda p: (0, 0))
    k_table = pl.BlockSpec((rows, PAIR), lambda p: (side, 0))
    col_spec = pl.BlockSpec((PAIR, rows), lambda p: (p, 0))
    narrow = jax.ShapeDtypeStruct((rows, D), BF)
    stats = jax.ShapeDtypeStruct((pairs, 8, rows), F32)
    cols = jax.ShapeDtypeStruct((D, rows), F32)
    views, sums, scratch = [], [], []
    if n:
        views, sums, scratch = scatter_xzy_shapes(grads) if second else scatter_shapes(grads, leads)
    params = dict(collective_id=ident, has_side_effects=True) if n else {}
    return pl.pallas_call(
        functools.partial(attend_back_kernel, side, leads),
        grid=(pairs,),
        in_specs=[
            SMEM, pl.BlockSpec((1, rows, PAIR), lambda p: (p, 0, 0)), k_spec, k_spec, row_spec, stat_spec,
            stat_spec if second else row_spec, k_table, k_table,
        ]
        + ([q_table, q_table, col_spec] if second else [])
        + [VMEM] * n,
        out_specs=[row_spec if second else col_spec, row_spec, row_spec]
        + ([] if second else [stat_spec])
        + [VMEM] * n,
        out_shape=[narrow if second else cols, narrow, narrow] + ([] if second else [stats]) + sums,
        scratch_shapes=([pltpu.VMEM((PAIR, rows), F32)] if second else []) + scratch,
        compiler_params=pltpu.CompilerParams(vmem_limit_bytes=VMEM_LIMIT, **params),
        cost_estimate=pl.CostEstimate(
            flops=40 * rows * rows * D, bytes_accessed=16 * rows * D, transcendentals=rows * rows * 12
        ),
        name="attend_back",
    )(ints, q, k, v, do, lse, extra, *tables, *((*tables, dq_part) if second else ()), *views)


def norm(values):
    centre = values - jnp.mean(values, axis=-1, keepdims=True)
    inverse = lax.rsqrt(jnp.mean(centre * centre, axis=-1, keepdims=True) + EPSILON)
    return centre * inverse, inverse


def norm_back(grad_result, normed, inverse, gain):
    scaled = grad_result * gain
    return inverse * (
        scaled
        - jnp.mean(scaled, axis=-1, keepdims=True)
        - normed * jnp.mean(scaled * normed, axis=-1, keepdims=True)
    )


def middle_kernel(
    ints, scale_ref, ctx_ref, x_ref, teacher_ref, vec_ref, wo_ref, wi_ref, wd_ref,
    out_ref, act_ref, hin_ref, gb_ref, gp_ref, ga_ref, gc_ref, gr_ref, part_ref, slope_ref,
):
    block = ctx_ref.shape[0]
    chunk = 1024
    hidden_units = wi_ref.shape[0]
    gain_one, bias_one, gain_two, bias_two = (vec_ref[i : i + 1, :] for i in range(4))
    attended = dot(ctx_ref[...], wo_ref[...], NN)
    normed_one, inverse_one = norm(x_ref[...].astype(F32) + attended)
    hidden = normed_one * gain_one + bias_one
    hidden_in = hidden.astype(BF)
    hin_ref[...] = hidden_in
    total = hidden
    for first in range(0, hidden_units, chunk):
        here = slice(first, first + chunk)
        pre = dot(hidden_in, wi_ref[here, :], NT)
        below = 0.5 + 0.5 * lax.erf(pre * INV_ROOT2)
        act = (pre * below).astype(BF)
        act_ref[:, here] = act
        slope_ref[:, here] = below + pre * jnp.exp(-0.5 * pre * pre) * INV_ROOT_TWO_PI
        total = total + dot(act, wd_ref[here, :], NN)
    normed_two, inverse_two = norm(total)
    final = normed_two * gain_two + bias_two
    out_ref[...] = final.astype(BF)
    place = ints[1] + pl.program_id(0) * block + lax.broadcasted_iota(jnp.int32, (block, D), 0)
    misfit = jnp.where(place < ints[0], final - teacher_ref[...].astype(F32), 0.0)
    grad_final = misfit * scale_ref[0]
    grad_mid = norm_back(grad_final, normed_two, inverse_two, gain_two)
    g_branch = grad_mid.astype(BF)
    gb_ref[...] = g_branch
    grad_hidden = grad_mid
    for first in range(0, hidden_units, chunk):
        here = slice(first, first + chunk)
        grad_act = dot(g_branch, wd_ref[here, :], NT)
        g_pre = (grad_act * slope_ref[:, here]).astype(BF)
        gp_ref[:, here] = g_pre
        grad_hidden = grad_hidden + dot(g_pre, wi_ref[here, :], NN)
    grad_res = norm_back(grad_hidden, normed_one, inverse_one, gain_one)
    gr_ref[...] = grad_res
    g_att = grad_res.astype(BF)
    ga_ref[...] = g_att
    gc_ref[...] = dot(g_att, wo_ref[...], NT).astype(BF)

    @pl.when(pl.program_id(0) == 0)
    def _():
        part_ref[...] = jnp.zeros_like(part_ref)

    for row, term in enumerate(
        (grad_hidden * normed_one, grad_hidden, grad_final * normed_two, grad_final, misfit * misfit)
    ):
        part_ref[row : row + 1, :] += jnp.sum(term, axis=0, keepdims=True)


def middle(ints, scale, context, x, teacher, vectors, out_full, in_full, down_full):
    rows = x.shape[0]
    block = 256
    hidden_units = in_full.shape[0]
    row = pl.BlockSpec((block, D), lambda i: (i, 0))
    wide = pl.BlockSpec((block, hidden_units), lambda i: (i, 0))

    def fixed(shape):
        return pl.BlockSpec(shape, lambda i: (0, 0), pipeline_mode=pl.Buffered(1))

    narrow_out = jax.ShapeDtypeStruct((rows, D), BF)
    wide_out = jax.ShapeDtypeStruct((rows, hidden_units), BF)
    return pl.pallas_call(
        middle_kernel,
        grid=(rows // block,),
        in_specs=[
            SMEM, SMEM, row, row, row, fixed((8, D)), fixed((D, D)), fixed((hidden_units, D)), fixed((hidden_units, D)),
        ],
        out_specs=[row, wide, row, row, wide, row, row, row, pl.BlockSpec((8, D), lambda i: (0, 0))],
        out_shape=[
            narrow_out, wide_out, narrow_out, narrow_out, wide_out, narrow_out, narrow_out,
            jax.ShapeDtypeStruct((rows, D), F32), jax.ShapeDtypeStruct((8, D), F32),
        ],
        scratch_shapes=[pltpu.VMEM((block, hidden_units), F32)],
        compiler_params=pltpu.CompilerParams(vmem_limit_bytes=VMEM_LIMIT),
        cost_estimate=pl.CostEstimate(
            flops=2 * rows * D * (2 * D + 4 * hidden_units),
            bytes_accessed=30 * rows * D + 4 * hidden_units * (rows + D),
            transcendentals=2 * rows * hidden_units,
        ),
        name="middle",
    )(ints, scale, context, x, teacher, vectors, out_full, in_full, down_full)


def on_device(
    layer_input, teacher, lengths, qkv_weight, out_weight, ln1_gain, ln1_bias,
    in_weight, down_weight, ln2_gain, ln2_bias,
):
    own_rows = layer_input.shape[0]
    data_size = lax.axis_size("dp")
    tensor_index = lax.axis_index("tensor")
    group_rows = own_rows * lax.axis_size("tensor")
    assert group_rows == SLOT and lax.axis_size("tensor") == 2 and lengths.shape[0] == 1
    own_comm = data_size == 16

    def gather(values, axis):
        return lax.all_gather(values, EVERYONE, axis=axis, tiled=True)

    def scatter(values, axis):
        return lax.psum_scatter(values, EVERYONE, scatter_dimension=axis, tiled=True)

    def swap(values):
        return lax.ppermute(values, "tensor", [(0, 1), (1, 0)])

    share = D // data_size
    norms = (ln1_gain, ln1_bias, ln2_gain, ln2_bias)
    angles = angle_tables()
    ints = jnp.stack([lengths[0], (tensor_index * own_rows).astype(jnp.int32)])
    if own_comm:
        small = jnp.pad(jnp.stack(norms).astype(F32), ((0, 4), (0, 128 - share)))
        small = jnp.where(lax.broadcasted_iota(jnp.int32, small.shape, 0) == 4, lengths[0].astype(F32), small)
        q, k, v, context, lse, cosine, sine, other_x, qkv_full, small_full, out_full, in_full, down_full = front(
            ints, layer_input, angles, [qkv_weight, small, out_weight, in_weight, down_weight]
        )
        small_full = small_full.reshape(2, data_size, 8, 128)[0]
        vectors = small_full[:, :, :share].transpose(1, 0, 2).reshape(8, D)
        valid_count = jnp.sum(small_full[:, 4, 0])
    else:
        vectors = jnp.stack([lax.all_gather(v, "dp", axis=0, tiled=True).astype(F32) for v in norms])
        vectors = jnp.concatenate([vectors, jnp.zeros((4, D), F32)])
        valid_count = lax.psum(jnp.sum(lengths).astype(F32), "dp")
        out_full, in_full, down_full = gather(out_weight, 0), gather(in_weight, 0), gather(down_weight, 0)
        q, k, v, context, lse, cosine, sine, other_x, qkv_full = front(
            ints, layer_input, angles, gathered=(gather(qkv_weight, 1), swap(layer_input))
        )

    grad_scale = group_rows * data_size * D // 4
    scale = (2.0 * grad_scale / (valid_count * D)).reshape(1)
    final, activated, hidden_in, g_branch, g_pre, g_att, g_context, grad_res, parts = middle(
        ints, scale, context, layer_input, teacher, vectors, out_full, in_full, down_full
    )

    def over_rows(left, right):
        return lax.dot_general(left, right, (((0,), (0,)), ((), ())), preferred_element_type=F32)

    grad_down_w = over_rows(activated, g_branch)
    grad_in_w = over_rows(g_pre, hidden_in)
    grad_out_w = over_rows(context, g_att)
    tables = (cosine, sine)
    if own_comm:
        sum_first, sum_second = [grad_down_w.astype(BF), grad_out_w.astype(BF)], [grad_in_w.astype(BF)]
    else:
        grad_down, grad_in, grad_out = scatter(grad_down_w, 0), scatter(grad_in_w, 0), scatter(grad_out_w, 0)
        sum_first, sum_second = [], []
    dq_part, dk_other, dv_other, delta, *sums = attend_back(
        1, ints, q, k, v, g_context, lse, context, tables, None, sum_first, 1
    )
    if own_comm:
        grad_down, grad_out = sums
    pass_on = dot(dk_other, qkv_full[1], NN) + dot(dv_other, qkv_full[2], NN)
    from_other = swap(pass_on.astype(BF))
    dq, dk_own, dv_own, *sums = attend_back(
        0, ints, q, k, v, g_context, lse, delta, tables, dq_part, sum_second, 2
    )
    if own_comm:
        grad_in = sums[0]
    if own_comm:
        grad_qkv, sums, input_grad = tail(
            dq, dk_own, dv_own, dk_other, dv_other, layer_input, other_x, qkv_full, grad_res, parts, 3
        )
        input_grad = input_grad + from_other.astype(F32)
    else:
        grad_qkv_w = [
            over_rows(dq, layer_input),
            over_rows(dk_own, layer_input) + over_rows(dk_other, other_x),
            over_rows(dv_own, layer_input) + over_rows(dv_other, other_x),
        ]
        grad_qkv = scatter(jnp.stack(grad_qkv_w), 1)
        sums = lax.psum(parts, ("dp", "tensor"))
        input_grad = (
            grad_res
            + dot(dq, qkv_full[0], NN)
            + dot(dk_own, qkv_full[1], NN)
            + dot(dv_own, qkv_full[2], NN)
            + from_other.astype(F32)
        )
    loss_value = jnp.sum(sums[4]) / (valid_count * D)
    own_norms = lax.dynamic_slice_in_dim(sums, lax.axis_index("dp") * share, share, 1)
    return (
        final, loss_value, input_grad, grad_qkv, grad_out,
        own_norms[0], own_norms[1], grad_in, grad_down, own_norms[2], own_norms[3],
    )


def solution(mesh):
    rows = P(("dp", "tensor"), None)
    shard = P(EVERYONE, None)
    in_specs = (
        rows, rows, P("dp"), P(None, EVERYONE, None), shard, P("dp"), P("dp"), shard, shard, P("dp"), P("dp"),
    )
    out_specs = (
        rows, P(), rows, P(None, EVERYONE, None), shard, P("dp"), P("dp"), shard, shard, P("dp"), P("dp"),
    )
    return jax.shard_map(on_device, mesh=mesh, in_specs=in_specs, out_specs=out_specs, check_vma=False)
```
